32 devices in a mesh: groups: 2 (over y), region: 8 (over z, x), sub: 2 (over core).
Axes of the slice: x: 2, y: 2, z: 4, core: 2. Of those that a mesh axis runs over, the one named last changes fastest.
Arguments:
- basis: float32 [128, 32, 2048], P('groups', None, ('region', 'sub')), parts along dimension 0, may hold values from -6 to 6
- weights: float32 [4, 32, 2048], P(None, None, ('region', 'sub')), may hold values from 0.02 to 0.2
- kappa: float32 [32, 2048], P(None, ('region', 'sub')), may hold values from 0.1 to 10
- thickness: float32 [32, 2048], P(None, ('region', 'sub')), may hold values from 0.5 to 2
- depth: int32 [2048], P(('region', 'sub')), may hold values from 1 to 32
- neighbours: int32 [4, 2048], P(None, ('region', 'sub')), may hold values from 0 to 155, as said below
- rim_lists: int32 [2, 256], P(None, ('region', 'sub')), may hold values from 0 to 127, as said below
- counts: int32 [16], P(('region', 'sub')), may hold values from 32 to 128, as said below
Outputs:
- next_basis: float32 [128, 32, 2048], P('groups', None, ('region', 'sub')), parts along dimension 0
- coupling: float32 [128, 64], P('groups'), parts along dimension 0
The draws below stay inside these ranges and needn't reach their ends.
There are 2 independent parts, one for each index of `groups`. The reference program is written for one: setup_inputs(seed, part) draws one part's arguments, and reference() takes and returns one part's arrays. A program takes and returns all parts, laid end to end along the dimension named above; an argument that names none is the same for every part. Nothing has to cross between parts.
Inputs may be any that keep to these rules, and one draw needn't show every extreme that they name: `neighbours`: each link names a column of the same block within 12 of its own, or a halo slot below 12 on the side it leaves from. `rim_lists`: within one block, each row lists distinct columns; row 0 lists the block's last 16 columns, row 1 its first 16. Column slots at local index counts[b] up to 95 are empty.
All inputs are finite; a program needn't handle non-finite values.
Results may differ from the reference program's by a relative error of at most 0.0001.
Values sent between devices are 32-bit elements; how exact they have to be, the bound alone decides.
No kernel may reach another device: no remote copies, remote signals or barrier semaphores. Data moves between devices by JAX's collectives and lax.ppermute only.
A program may use at most 64 MiB of HBM per device.

```python
import math
import jax
import jax.numpy as jnp
from jax import lax

K = 64
LEV = 32
NB = 4
ITERS = 2
COL_DEV = 128
HALO = 16
BLOCKS = 16
NCOL = 2048


def draw_neighbours(key, part):
    local = jnp.arange(NCOL, dtype=jnp.int32) % COL_DEV
    offsets = jnp.array([-1, 1, -(HALO // 2), HALO // 2], dtype=jnp.int32)
    spread_w = HALO // 4
    jitter = jax.random.randint(key, (NB, NCOL), -spread_w, spread_w + 1, dtype=jnp.int32)
    row_ids = jnp.arange(NB, dtype=jnp.int32)[:, None]
    jitter = jnp.where((row_ids == 3) & (local[None, :] == COL_DEV - 1), spread_w, jitter)
    jitter = jnp.where((row_ids == 0) & (local[None, :] == 1), 0, jitter)
    target = local[None, :] + offsets[:, None] + jitter
    left_slot = COL_DEV + (-1 - target)
    right_slot = COL_DEV + HALO + (target - COL_DEV)
    return jnp.where(target < 0, left_slot, jnp.where(target >= COL_DEV, right_slot, target)).astype(jnp.int32)


def draw_rim_lists(key, part):
    keys = jax.random.split(key, 2 * BLOCKS)
    orders = jax.vmap(lambda sub_key: jax.random.permutation(sub_key, HALO))(keys).astype(jnp.int32)
    orders = orders.reshape(2, BLOCKS * HALO)
    first_row = COL_DEV - HALO + orders[0]
    return jnp.stack([first_row, orders[1]], axis=0).astype(jnp.int32)


def draw_counts(key, part):
    index = jnp.arange(BLOCKS, dtype=jnp.int32)
    base = COL_DEV // 4 + 3 * COL_DEV // 4 * index // max(BLOCKS - 1, 1)
    jitter = jax.random.randint(key, (BLOCKS,), -(COL_DEV // 8), COL_DEV // 8 + 1, dtype=jnp.int32)
    value = jnp.clip(base + jitter, COL_DEV // 4, COL_DEV)
    value = jnp.where(index == BLOCKS - 1, COL_DEV, value)
    value = jnp.where(index == 0, COL_DEV // 4, value)
    return value.astype(jnp.int32)


def set_ends(values, rng, smallest, largest):
    longest = values.shape.index(max(values.shape))
    spots = []
    for shift in (0, 1):
        where = [jax.random.randint(jax.random.fold_in(rng, axis), (), 0, length) for axis, length in enumerate(values.shape)]
        where[longest] = (where[longest] + shift) % values.shape[longest]
        spots.append(tuple(where))
    return values.at[spots[0]].set(smallest).at[spots[1]].set(largest)


def steps_of(rng, extent, shards, low, top_value):
    factor_of, own = 1.0, jax.random.fold_in(rng, 6)
    for axis_at, parts in shards:
        draws = jnp.exp(jax.random.uniform(jax.random.fold_in(own, axis_at), (parts,), jnp.float32, low / len(shards), top_value / len(shards)))
        factor_of = factor_of * jnp.repeat(draws, extent[axis_at] // parts).reshape([-1 if axis == axis_at else 1 for axis in range(len(extent))])
    return factor_of


def centred(rng, dims, scale, bound, shards=(), kind=jnp.bfloat16):
    level = steps_of(rng, dims, shards, -0.22, 0.18) if shards else 1.0
    values = jax.random.normal(rng, dims, jnp.float32) * scale * level
    return jnp.minimum(jnp.maximum(values, -bound), bound).astype(kind)


def setup_inputs(seed: int = 0, part: int = 0) -> dict:
    splits = jax.random.split(jax.random.key(seed), 9)
    part_splits = jax.random.split(jax.random.fold_in(splits[8], part), 9)
    basis = centred(part_splits[0], (K, LEV, NCOL), 1.0, 6.0, ((2, 16),), jnp.float32)
    weights = jnp.clip(0.02 + 0.18 * jax.random.uniform(splits[1], (NB, LEV, NCOL), jnp.float32) ** steps_of(splits[1], (NB, LEV, NCOL), ((2, 16),), -0.2, 0.2), 0.02, 0.2)
    kappa = jnp.clip(jnp.exp(math.log(10.0) - 4.6051702 * jax.random.uniform(splits[2], (LEV, NCOL), jnp.float32) ** steps_of(splits[2], (LEV, NCOL), ((1, 16),), -0.2, 0.2)), 0.1, 10.0)
    thickness = jnp.clip(0.5 + 1.5 * jax.random.uniform(splits[3], (LEV, NCOL), jnp.float32) ** steps_of(splits[3], (LEV, NCOL), ((1, 16),), -0.2, 0.2), 0.5, 2.0)
    depth = set_ends(jax.random.randint(splits[4], (NCOL,), 1, LEV + 1), jax.random.fold_in(splits[4], 1), 1, LEV).astype(jnp.int32)
    neighbours = draw_neighbours(jax.random.fold_in(splits[8], 71), part)
    rim_lists = draw_rim_lists(jax.random.fold_in(splits[8], 71), part)
    counts = draw_counts(jax.random.fold_in(splits[8], 71), part)
    return {"basis": basis, "weights": weights, "kappa": kappa, "thickness": thickness, "depth": depth, "neighbours": neighbours, "rim_lists": rim_lists, "counts": counts}


def global_targets(neighbours, rim_lists):
    column = jnp.arange(NCOL, dtype=jnp.int32)
    owner = jnp.broadcast_to(column // COL_DEV, neighbours.shape).astype(jnp.int32)
    before = (owner - 1) % BLOCKS
    after = (owner + 1) % BLOCKS
    left_slot = jnp.clip(neighbours - COL_DEV, 0, HALO - 1)
    right_slot = jnp.clip(neighbours - COL_DEV - HALO, 0, HALO - 1)
    left_col = rim_lists[0][before * HALO + left_slot]
    right_col = rim_lists[1][after * HALO + right_slot]
    target = jnp.where(neighbours < COL_DEV, owner * COL_DEV + neighbours, jnp.where(neighbours < COL_DEV + HALO, before * COL_DEV + left_col, after * COL_DEV + right_col))
    return target.astype(jnp.int32)

def column_factors(kappa, thickness, keep):
    levels = kappa.shape[0]
    below = jnp.concatenate([keep[1:], jnp.zeros_like(keep[:1])], axis=0)
    interface = kappa * keep * below
    lower, inv_pivot, ratio = ([], [], [])
    for level in range(levels):
        upper_term = interface[level]
        diag_term = 1.0 + upper_term / thickness[level]
        if level > 0:
            diag_term = diag_term + interface[level - 1] / thickness[level]
            low = -interface[level - 1] / thickness[level - 1]
        else:
            low = jnp.zeros_like(upper_term)
        if level < levels - 1:
            upp = -upper_term / thickness[level + 1]
        else:
            upp = jnp.zeros_like(upper_term)
        pivot = diag_term - low * ratio[level - 1] if level > 0 else diag_term
        inverse = 1.0 / pivot
        lower.append(low)
        inv_pivot.append(inverse)
        ratio.append(upp * inverse)
    return (lower, inv_pivot, ratio)

def column_solve(rhs, lower, inv_pivot, ratio):
    levels = rhs.shape[1]
    forward = []
    for level in range(levels):
        if level == 0:
            forward.append(rhs[:, 0] * inv_pivot[0])
        else:
            forward.append((rhs[:, level] - lower[level] * forward[level - 1]) * inv_pivot[level])
    result = [None] * levels
    result[levels - 1] = forward[levels - 1]
    for level in range(levels - 2, -1, -1):
        result[level] = forward[level] - ratio[level] * result[level + 1]
    return jnp.stack(result, axis=1)

def reference(basis, weights, kappa, thickness, depth, neighbours, rim_lists, counts):
    column = jnp.arange(NCOL, dtype=jnp.int32)
    local_index = column % COL_DEV
    live = (local_index < counts[column // COL_DEV]) | (local_index >= COL_DEV - 2 * HALO)
    wet = jnp.arange(LEV, dtype=jnp.int32)[:, None] < depth[None, :]
    keep = (live[None, :] & wet).astype(jnp.float32)
    target = global_targets(neighbours, rim_lists).reshape(-1)
    self_weight = 1.0 - lax.optimization_barrier(jnp.sum(weights, axis=0))
    lower, inv_pivot, ratio = column_factors(kappa, thickness, keep)

    def advance(block):
        field = block
        for step in range(ITERS):
            masked = keep * field
            spread = jnp.moveaxis(weights[None] * masked[:, None], 1, 2).reshape(block.shape[0], LEV, NB * NCOL)
            moved = (self_weight * masked).at[:, :, target].add(spread)
            field = column_solve(keep * (keep * moved), lower, inv_pivot, ratio)
        return field
    blocks = basis.reshape(K // 8, 8, LEV, NCOL)
    images = lax.map(advance, blocks).reshape(K, LEV, NCOL)
    cells = float(LEV * NCOL)
    high = lax.Precision.HIGHEST
    coupling = jnp.einsum('ilc,jlc->ij', basis, images, precision=high) / cells
    residual = images - jnp.einsum('ilc,ij->jlc', basis, coupling, precision=high)
    norms = jnp.einsum('jlc,jlc->j', residual, residual, precision=high) / cells
    next_basis = residual / jnp.sqrt(norms + 1e-06)[:, None, None]
    return (next_basis, coupling)
```

```python
import functools

import jax
import jax.numpy as jnp
from jax import lax
from jax.experimental import pallas as pl
from jax.experimental.pallas import tpu as pltpu
from jax.sharding import PartitionSpec as P

AXES = ("region", "sub")
LANES = 128
F32 = jnp.float32
BF16 = jnp.bfloat16
NT = (((1,), (1,)), ((), ()))


def split(x):
    top = x.astype(BF16)
    return top, (x - top.astype(F32)).astype(BF16)


def dot3(a, b, dims):
    a_top, a_low = split(a)
    b_top, b_low = split(b)
    dot = functools.partial(lax.dot_general, dimension_numbers=dims, preferred_element_type=F32)
    return dot(a_top, b_top) + (dot(a_top, b_low) + dot(a_low, b_top))


def link_targets(neighbours_ref, targets_ref, halo):
    links, columns = neighbours_ref.shape
    padded = jnp.concatenate([neighbours_ref[...].astype(F32), jnp.zeros((8 - links, columns), F32)], axis=0)
    by_column = padded.T
    lane = lax.broadcasted_iota(jnp.int32, (columns, LANES), 1)
    own = lane.astype(F32)
    slot = (columns + lane % (2 * halo)).astype(F32)
    for link in range(links):
        target = jnp.broadcast_to(by_column[:, link : link + 1], (columns, LANES))
        rows = slice(link * columns, (link + 1) * columns)
        targets_ref[rows, 0:columns] = jnp.where(target == own, 1.0, 0.0).astype(BF16)
        targets_ref[rows, columns : columns + LANES] = jnp.where(target == slot, 1.0, 0.0).astype(BF16)


def spread_level(value, level, weights_ref, spread_ref, group):
    links, _, columns = weights_ref.shape
    vectors = value.shape[0]
    first = level // group * 2 * group * vectors + level % group * vectors
    second = first + group * vectors
    for link in range(links):
        top, low = split(value * weights_ref[link, level : level + 1, :])
        cols = slice(link * columns, (link + 1) * columns)
        spread_ref[first : first + vectors, cols] = top
        spread_ref[second : second + vectors, cols] = low


def move_group(index, spread_ref, targets_ref, rows, columns):
    both = jnp.dot(spread_ref[2 * rows * index : 2 * rows * (index + 1), :], targets_ref[...], preferred_element_type=F32)
    both = both[:rows] + both[rows:]
    return both[:, :columns], both[:, columns:]


def pack(parts, halo):
    lane = lax.broadcasted_iota(jnp.int32, parts[0].shape, 1)
    left = jnp.zeros_like(parts[0])
    right = jnp.zeros_like(parts[0])
    for index, part in enumerate(parts):
        turned = pltpu.roll(part, halo, 1)
        mine = lane // halo == index
        left = jnp.where(mine, turned if index % 2 else part, left)
        right = jnp.where(mine, part if index % 2 else turned, right)
    return left, right


def factor_columns(kappa_ref, thickness_ref, keep, carry_ref, pivot_ref, ratio_ref):
    levels = keep.shape[0]
    interface = [kappa_ref[i : i + 1, :] * keep[i : i + 1] * keep[i + 1 : i + 2] for i in range(levels - 1)]
    ratio = None
    for level in range(levels):
        thick = thickness_ref[level : level + 1, :]
        pivot = jnp.ones_like(thick)
        if level < levels - 1:
            pivot = pivot + interface[level] / thick
        if level > 0:
            pivot = pivot + interface[level - 1] / thick
            low = -interface[level - 1] / thickness_ref[level - 1 : level, :]
            pivot = pivot - low * ratio
        inverse = 1.0 / pivot
        carry_ref[level : level + 1, :] = low * inverse if level > 0 else jnp.zeros_like(thick)
        pivot_ref[level : level + 1, :] = keep[level : level + 1] * inverse
        if level < levels - 1:
            ratio = -interface[level] / thickness_ref[level + 1 : level + 2, :] * inverse
            ratio_ref[level : level + 1, :] = ratio
        else:
            ratio_ref[level : level + 1, :] = jnp.zeros_like(thick)


def first_kernel(halo, group, counts_ref, basis_ref, weights_ref, kappa_ref, thickness_ref, depth_ref, neighbours_ref,
                 own_ref, left_ref, right_ref, field_ref, live_ref, self_ref, carry_ref, pivot_ref, ratio_ref, targets_ref,
                 spread_ref):
    vectors, levels, columns = basis_ref.shape
    links = weights_ref.shape[0]
    lane = lax.broadcasted_iota(jnp.int32, (levels, columns), 1)
    level_of = lax.broadcasted_iota(jnp.int32, (levels, columns), 0)
    live = (lane < counts_ref[0]) | (lane >= columns - 2 * halo)
    keep = jnp.where(live & (level_of < depth_ref[...]), 1.0, 0.0)
    total = weights_ref[0]
    for link in range(1, links):
        total = total + weights_ref[link]
    self_ref[...] = keep * (1.0 - total)
    for link in range(links):
        live_ref[link] = keep * weights_ref[link]
    link_targets(neighbours_ref, targets_ref, halo)
    rows = group * vectors
    parts = []
    for index in range(levels // group):
        for level in range(index * group, (index + 1) * group):
            value = basis_ref[:, level, :]
            field_ref[level] = value
            spread_level(value, level, live_ref, spread_ref, group)
        own, slots = move_group(index, spread_ref, targets_ref, rows, columns)
        parts.append(slots)
        for level in range(index * group, (index + 1) * group):
            at = (level - index * group) * vectors
            own_ref[level] = own[at : at + vectors] + field_ref[level] * self_ref[level : level + 1, :]
    left_ref[...], right_ref[...] = pack(parts, halo)
    factor_columns(kappa_ref, thickness_ref, keep, carry_ref, pivot_ref, ratio_ref)


def rim_slots(rim_ref, row, halo, shape):
    lane = lax.broadcasted_iota(jnp.int32, shape, 1)
    slot = jnp.full(shape, -1, jnp.int32)
    for index in range(halo):
        slot = jnp.where(lane == rim_ref[row, index], index, slot)
    return slot


def eliminate(halo, group, rim_ref, own_ref, from_left_ref, from_right_ref, carry_ref, pivot_ref, forward_ref):
    levels, vectors, columns = own_ref.shape
    rows = group * vectors
    lead = rim_slots(rim_ref, 1, halo, (rows, columns))
    trail = rim_slots(rim_ref, 0, halo, (rows, columns))
    above = None
    for index in range(levels // group):
        from_left = jnp.take_along_axis(from_left_ref[...], jnp.maximum(lead, 0) + halo * index, axis=1, mode="promise_in_bounds")
        from_right = jnp.take_along_axis(from_right_ref[...], jnp.maximum(trail, 0) + halo * index, axis=1, mode="promise_in_bounds")
        rim = jnp.where(lead >= 0, from_left, 0.0) + jnp.where(trail >= 0, from_right, 0.0)
        for level in range(index * group, (index + 1) * group):
            at = (level - index * group) * vectors
            value = (own_ref[level] + rim[at : at + vectors]) * pivot_ref[level : level + 1, :]
            if level > 0:
                value = value - carry_ref[level : level + 1, :] * above
            forward_ref[level] = value
            above = value


def second_kernel(halo, group, rim_ref, own_ref, from_left_ref, from_right_ref, live_ref, self_ref, carry_ref, pivot_ref,
                  ratio_ref, targets_ref, moved_ref, left_ref, right_ref, forward_ref, spread_ref):
    levels, vectors, columns = own_ref.shape
    rows = group * vectors
    eliminate(halo, group, rim_ref, own_ref, from_left_ref, from_right_ref, carry_ref, pivot_ref, forward_ref)
    parts = [None] * (levels // group)
    below = None
    for index in range(levels // group - 1, -1, -1):
        for level in range((index + 1) * group - 1, index * group - 1, -1):
            value = forward_ref[level]
            if below is not None:
                value = value - ratio_ref[level : level + 1, :] * below
            below = value
            forward_ref[level] = value
            spread_level(value, level, live_ref, spread_ref, group)
        own, parts[index] = move_group(index, spread_ref, targets_ref, rows, columns)
        for level in range(index * group, (index + 1) * group):
            at = (level - index * group) * vectors
            moved_ref[level] = own[at : at + vectors] + forward_ref[level] * self_ref[level : level + 1, :]
    left_ref[...], right_ref[...] = pack(parts, halo)


def third_kernel(halo, group, rim_ref, own_ref, from_left_ref, from_right_ref, carry_ref, pivot_ref, ratio_ref, field_ref,
                 image_ref, sums_ref, forward_ref):
    levels, vectors, columns = own_ref.shape
    eliminate(halo, group, rim_ref, own_ref, from_left_ref, from_right_ref, carry_ref, pivot_ref, forward_ref)
    cross = jnp.zeros((vectors, vectors), F32)
    gram = jnp.zeros((vectors, vectors), F32)
    square = jnp.zeros((vectors, columns), F32)
    below = None
    for level in range(levels - 1, -1, -1):
        value = forward_ref[level]
        if below is not None:
            value = value - ratio_ref[level : level + 1, :] * below
        below = value
        image_ref[level] = value
        square = square + value * value
        basis = field_ref[level]
        cross = cross + dot3(value, basis, NT)
        gram = gram + dot3(basis, basis, NT)
    sums_ref[0:vectors, 0:vectors] = cross
    sums_ref[0:vectors, vectors : 2 * vectors] = gram
    norm = jnp.sum(square, axis=1, keepdims=True)
    eye = lax.broadcasted_iota(jnp.int32, (vectors, 2 * vectors), 0) == lax.broadcasted_iota(jnp.int32, (vectors, 2 * vectors), 1)
    norm = jnp.sum(jnp.where(eye, norm, 0.0), axis=0, keepdims=True)
    sums_ref[vectors : vectors + 8, :] = jnp.broadcast_to(norm, (8, 2 * vectors))


def last_kernel(cells, sums_ref, image_ref, field_ref, next_ref, coupling_ref):
    levels, vectors, columns = image_ref.shape
    cross = sums_ref[0:vectors, 0:vectors] / cells
    gram = sums_ref[0:vectors, vectors : 2 * vectors] / cells
    coupling_ref[...] = cross.T
    eye = lax.broadcasted_iota(jnp.int32, (vectors, vectors), 0) == lax.broadcasted_iota(jnp.int32, (vectors, vectors), 1)
    square = sums_ref[vectors : vectors + 1, 0:vectors] / cells
    square = jnp.sum(jnp.where(eye, square, 0.0), axis=1, keepdims=True)
    mixed = dot3(cross, gram, (((1,), (0,)), ((), ())))
    norm = square + jnp.sum(cross * (mixed - 2.0 * cross), axis=1, keepdims=True)
    scale = 1.0 / jnp.sqrt(jnp.maximum(norm, 0.0) + 1e-6)
    cross_top, cross_low = split(cross)
    weights = jnp.concatenate([cross_top, cross_top, cross_low], axis=1)
    for level in range(levels):
        top, low = split(field_ref[level])
        spanned = jnp.dot(weights, jnp.concatenate([top, low, top], axis=0), preferred_element_type=F32)
        next_ref[:, level, :] = (image_ref[level] - spanned) * scale


def call(kernel, outs, scratch, scalars, *operands):
    vmem = pl.BlockSpec(memory_space=pltpu.VMEM)
    smem = pl.BlockSpec(memory_space=pltpu.SMEM)
    return pl.pallas_call(
        kernel,
        out_shape=outs,
        in_specs=[smem] * scalars + [vmem] * (len(operands) - scalars),
        out_specs=[vmem] * len(outs),
        scratch_shapes=scratch,
        compiler_params=pltpu.CompilerParams(vmem_limit_bytes=40 << 20),
    )(*operands)


def exchange(left, right):
    blocks = lax.axis_size(AXES)
    even = lax.axis_index(AXES) % 2 == 0
    outer = jnp.where(even, left, right)
    inner = jnp.where(even, right, left)
    outer = lax.ppermute(outer, AXES, [(i, (i - 1) % blocks if i % 2 == 0 else (i + 1) % blocks) for i in range(blocks)])
    inner = lax.ppermute(inner, AXES, [(i, i ^ 1) for i in range(blocks)])
    return jnp.where(even, outer, inner), jnp.where(even, inner, outer)


def total_over_blocks(value):
    blocks = lax.axis_size(AXES)
    if blocks & (blocks - 1):
        return lax.psum(value, AXES)
    distance = 1
    while distance < blocks:
        value = value + lax.ppermute(value, AXES, [(i, i ^ distance) for i in range(blocks)])
        distance *= 2
    return value


def shards(basis, weights, kappa, thickness, depth, neighbours, rim_lists, counts):
    vectors, levels, columns = basis.shape
    links = weights.shape[0]
    halo = rim_lists.shape[1]
    group = levels * halo // LANES
    rows = group * vectors

    def out(*shape, dtype=F32):
        return jax.ShapeDtypeStruct(shape, dtype)

    slots = out(rows, LANES)
    whole = out(levels, vectors, columns)
    plane = out(levels, columns)
    spread = pltpu.VMEM((2 * levels * vectors, links * columns), BF16)
    forward = pltpu.VMEM((levels, vectors, columns), F32)
    targets = out(links * columns, columns + LANES, dtype=BF16)
    own, left, right, field, live, self_weight, carry, pivot, ratio, targets = call(
        functools.partial(first_kernel, halo, group),
        (whole, slots, slots, whole, out(links, levels, columns), plane, plane, plane, plane, targets), [spread], 1,
        counts, basis, weights, kappa, thickness, depth.reshape(1, columns), neighbours)
    from_left, from_right = exchange(left, right)
    own, left, right = call(
        functools.partial(second_kernel, halo, group), (whole, slots, slots), [forward, spread], 1,
        rim_lists, own, from_left, from_right, live, self_weight, carry, pivot, ratio, targets)
    from_left, from_right = exchange(left, right)
    image, sums = call(
        functools.partial(third_kernel, halo, group), (whole, out(vectors + 8, 2 * vectors)), [forward], 1,
        rim_lists, own, from_left, from_right, carry, pivot, ratio, field)
    sums = total_over_blocks(sums)
    cells = float(levels * columns * lax.axis_size(AXES))
    return tuple(call(functools.partial(last_kernel, cells), (out(vectors, levels, columns), out(vectors, vectors)), [], 0,
                      sums, image, field))


def solution(mesh):
    placed = (
        P("groups", None, AXES),
        P(None, None, AXES),
        P(None, AXES),
        P(None, AXES),
        P(AXES),
        P(None, AXES),
        P(None, AXES),
        P(AXES),
    )
    return jax.shard_map(
        shards,
        mesh=mesh,
        in_specs=placed,
        out_specs=(P("groups", None, AXES), P("groups", None)),
        check_vma=False,
    )
```

```python
import functools

import jax
import jax.numpy as jnp
from jax import lax
from jax.experimental import pallas as pl
from jax.experimental.pallas import tpu as pltpu
from jax.sharding import PartitionSpec as P

AXES = ("region", "sub")
LANES = 128
F32 = jnp.float32
BF16 = jnp.bfloat16
NT = (((1,), (1,)), ((), ()))


def split(x):
    top = x.astype(BF16)
    return top, (x - top.astype(F32)).astype(BF16)


def dot3(a, b, dims):
    a_top, a_low = split(a)
    b_top, b_low = split(b)
    dot = functools.partial(lax.dot_general, dimension_numbers=dims, preferred_element_type=F32)
    return dot(a_top, b_top) + (dot(a_top, b_low) + dot(a_low, b_top))


def link_targets(neighbours_ref, targets_ref, halo):
    links, columns = neighbours_ref.shape
    padded = jnp.concatenate([neighbours_ref[...].astype(F32), jnp.zeros((8 - links, columns), F32)], axis=0)
    by_column = padded.T
    lane = lax.broadcasted_iota(jnp.int32, (columns, LANES), 1)
    own = lane.astype(F32)
    slot = (columns + lane % (2 * halo)).astype(F32)
    for link in range(links):
        target = jnp.broadcast_to(by_column[:, link : link + 1], (columns, LANES))
        rows = slice(link * columns, (link + 1) * columns)
        targets_ref[rows, 0:columns] = jnp.where(target == own, 1.0, 0.0).astype(BF16)
        targets_ref[rows, columns : columns + LANES] = jnp.where(target == slot, 1.0, 0.0).astype(BF16)


def spread_level(value, level, weights_ref, spread_ref, group):
    links, _, columns = weights_ref.shape
    vectors = value.shape[0]
    first = level // group * 2 * group * vectors + level % group * vectors
    second = first + group * vectors
    for link in range(links):
        top, low = split(value * weights_ref[link, level : level + 1, :])
        cols = slice(link * columns, (link + 1) * columns)
        spread_ref[first : first + vectors, cols] = top
        spread_ref[second : second + vectors, cols] = low


def move_group(index, spread_ref, targets_ref, rows, columns):
    both = jnp.dot(spread_ref[2 * rows * index : 2 * rows * (index + 1), :], targets_ref[...], preferred_element_type=F32)
    both = both[:rows] + both[rows:]
    return both[:, :columns], both[:, columns:]


def pack(parts, halo):
    lane = lax.broadcasted_iota(jnp.int32, parts[0].shape, 1)
    left = jnp.zeros_like(parts[0])
    right = jnp.zeros_like(parts[0])
    for index, part in enumerate(parts):
        turned = pltpu.roll(part, halo, 1)
        mine = lane // halo == index
        left = jnp.where(mine, turned if index % 2 else part, left)
        right = jnp.where(mine, part if index % 2 else turned, right)
    return left, right


def factor_columns(kappa_ref, thickness_ref, keep, carry_ref, pivot_ref, ratio_ref):
    levels = keep.shape[0]
    interface = [kappa_ref[i : i + 1, :] * keep[i : i + 1] * keep[i + 1 : i + 2] for i in range(levels - 1)]
    ratio = None
    for level in range(levels):
        thick = thickness_ref[level : level + 1, :]
        pivot = jnp.ones_like(thick)
        if level < levels - 1:
            pivot = pivot + interface[level] / thick
        if level > 0:
            pivot = pivot + interface[level - 1] / thick
            low = -interface[level - 1] / thickness_ref[level - 1 : level, :]
            pivot = pivot - low * ratio
        inverse = 1.0 / pivot
        carry_ref[level : level + 1, :] = low * inverse if level > 0 else jnp.zeros_like(thick)
        pivot_ref[level : level + 1, :] = keep[level : level + 1] * inverse
        if level < levels - 1:
            ratio = -interface[level] / thickness_ref[level + 1 : level + 2, :] * inverse
            ratio_ref[level : level + 1, :] = ratio
        else:
            ratio_ref[level : level + 1, :] = jnp.zeros_like(thick)


def lane_group(shape, width):
    return lax.broadcasted_iota(jnp.int32, shape, 1) // width


def pick(plane, lanes):
    return jnp.take_along_axis(plane, lanes, axis=1, mode="promise_in_bounds")


def rim_lanes(rim_ref, row, halo, shape):
    slot = lax.broadcasted_iota(jnp.int32, shape, 1) % halo
    columns = jnp.zeros(shape, jnp.int32)
    for index in range(halo):
        columns = jnp.where(slot == index, rim_ref[row, index], columns)
    return columns


def rim_coefficients(planes, neighbours, columns, first, halo):
    group = lane_group(columns.shape, halo)
    packed = jnp.zeros(columns.shape, F32)
    for index, plane in enumerate(planes):
        packed = jnp.where(group == index, pick(plane, columns), packed)
    slot = pick(neighbours, columns) - first
    slot = jnp.where((slot >= 0) & (slot < halo), slot, -1)
    return jnp.where(group == len(planes), slot.astype(F32), packed)


def padded_links(neighbours_ref, rows):
    links, columns = neighbours_ref.shape
    padded = jnp.concatenate([neighbours_ref[...], jnp.zeros((8 - links, columns), jnp.int32)], axis=0)
    if rows > 8:
        padded = jnp.concatenate([padded, jnp.zeros((rows - 8, columns), jnp.int32)], axis=0)
    return padded


def first_kernel(halo, group, counts_ref, even_ref, rim_ref, basis_ref, weights_ref, kappa_ref, thickness_ref, depth_ref,
                 neighbours_ref, outer_ref, inner_ref, left_ref, right_ref, field_ref, moved_ref, live_ref, self_ref,
                 carry_ref, pivot_ref, ratio_ref, targets_ref, spread_ref, forward_ref, chunk_ref, sems):
    vectors, levels, columns = basis_ref.shape
    links = weights_ref.shape[0]
    chunks = chunk_ref.shape[0]
    step = levels // chunks
    copies = [pltpu.make_async_copy(basis_ref.at[:, step * i : step * (i + 1), :], chunk_ref.at[i], sems.at[i]) for i in range(chunks)]
    for copy in copies:
        copy.start()
    lane = lax.broadcasted_iota(jnp.int32, (levels, columns), 1)
    level_of = lax.broadcasted_iota(jnp.int32, (levels, columns), 0)
    live = (lane < counts_ref[0]) | (lane >= columns - 2 * halo)
    keep = jnp.where(live & (level_of < depth_ref[...]), 1.0, 0.0)
    total = weights_ref[0]
    for link in range(1, links):
        total = total + weights_ref[link]
    self_ref[...] = keep * (1.0 - total)
    for link in range(links):
        live_ref[link] = keep * weights_ref[link]
    link_targets(neighbours_ref, targets_ref, halo)
    factor_columns(kappa_ref, thickness_ref, keep, carry_ref, pivot_ref, ratio_ref)
    rows = group * vectors
    parts = []
    above = None
    for index in range(levels // group):
        for level in range(index * group, (index + 1) * group):
            if level % step == 0:
                copies[level // step].wait()
            value = chunk_ref[level // step, :, level % step, :]
            field_ref[level] = value
            spread_level(value, level, live_ref, spread_ref, group)
        own, slots = move_group(index, spread_ref, targets_ref, rows, columns)
        parts.append(slots)
        for level in range(index * group, (index + 1) * group):
            at = (level - index * group) * vectors
            value = own[at : at + vectors] + field_ref[level] * self_ref[level : level + 1, :]
            value = value * pivot_ref[level : level + 1, :]
            if level > 0:
                value = value - carry_ref[level : level + 1, :] * above
            forward_ref[level] = value
            above = value
    left, right = pack(parts, halo)
    left_ref[...] = left
    right_ref[...] = right
    even = even_ref[0] > 0
    outer_ref[0:rows, :] = jnp.where(even, left, right)
    inner_ref[0:rows, :] = jnp.where(even, right, left)
    below = None
    for index in range(levels // group - 1, -1, -1):
        for level in range((index + 1) * group - 1, index * group - 1, -1):
            value = forward_ref[level]
            if below is not None:
                value = value - ratio_ref[level : level + 1, :] * below
            below = value
            forward_ref[level] = value
            spread_level(value, level, live_ref, spread_ref, group)
        own, parts[index] = move_group(index, spread_ref, targets_ref, rows, columns)
        for level in range(index * group, (index + 1) * group):
            at = (level - index * group) * vectors
            moved_ref[level] = own[at : at + vectors] + forward_ref[level] * self_ref[level : level + 1, :]
    left, right = pack(parts, halo)
    outer_ref[rows : 2 * rows, :] = jnp.where(even, left, right)
    inner_ref[rows : 2 * rows, :] = jnp.where(even, right, left)
    planes = [carry_ref[...], pivot_ref[...], ratio_ref[...]] + [live_ref[link] for link in range(links)]
    neighbours = padded_links(neighbours_ref, levels)
    left = rim_coefficients(planes, neighbours, rim_lanes(rim_ref, 1, halo, (levels, columns)), columns, halo)
    right = rim_coefficients(planes, neighbours, rim_lanes(rim_ref, 0, halo, (levels, columns)), columns + halo, halo)
    outer_ref[2 * rows :, :] = jnp.where(even, left, right)
    inner_ref[2 * rows :, :] = jnp.where(even, right, left)


def gram_kernel(field_ref, gram_ref):
    levels, vectors, _ = field_ref.shape
    gram = jnp.zeros((vectors, vectors), F32)
    for level in range(levels):
        gram = gram + dot3(field_ref[level], field_ref[level], NT)
    gram_ref[...] = gram


def turn_groups(blocks, halo):
    blocks = list(blocks)
    lanes = blocks[0].shape[1]
    group = lane_group(blocks[0].shape, halo)
    bit = 1
    while bit < len(blocks):
        upper = group // bit % 2 == 1
        for low in range(len(blocks)):
            if low & bit:
                continue
            high = low | bit
            a, b = blocks[low], blocks[high]
            blocks[low] = jnp.where(upper, pltpu.roll(b, halo * bit, 1), a)
            blocks[high] = jnp.where(upper, b, pltpu.roll(a, lanes - halo * bit, 1))
        bit *= 2
    return blocks


def second_kernel(halo, group, even_ref, rim_ref, outer_ref, inner_ref, left_ref, right_ref, field_ref, moved_ref, live_ref,
                  self_ref, carry_ref, pivot_ref, ratio_ref, neighbours_ref, gram_ref, image_ref, sums_ref,
                  plane_ref, target_ref, rim_field_ref, late_ref, spread_ref, forward_ref):
    levels, vectors, columns = field_ref.shape
    links = live_ref.shape[0]
    rows = group * vectors
    half = vectors // 2
    even = even_ref[0] > 0
    outer = outer_ref[...]
    inner = inner_ref[...]
    from_left = jnp.where(even, outer, inner)
    from_right = jnp.where(even, inner, outer)

    def parts_of(shape):
        return lane_group(shape, halo) % 4

    shape = (levels, columns)
    part = parts_of(shape)
    slot = lax.broadcasted_iota(jnp.int32, shape, 1) % halo
    lead = rim_lanes(rim_ref, 1, halo, shape)
    trail = rim_lanes(rim_ref, 0, halo, shape)
    own_column = jnp.where(part % 2 == 0, lead, trail)
    planes = [carry_ref[...], pivot_ref[...], ratio_ref[...]] + [live_ref[link] for link in range(links)]
    for index, plane in enumerate(planes):
        theirs = jnp.where(part == 2, pick(from_left[2 * rows :], slot + halo * index), pick(from_right[2 * rows :], slot + halo * index))
        plane_ref[index] = jnp.where(part < 2, pick(plane, own_column), theirs)
    plane_ref[len(planes)] = pick(self_ref[...], own_column)

    shape = (8, columns)
    part, slot, lead, trail, own_column = part[0:8], slot[0:8], lead[0:8], trail[0:8], own_column[0:8]
    named = pick(padded_links(neighbours_ref, 8), own_column)
    from_links = slot + halo * len(planes)
    theirs = jnp.where(part == 2, pick(from_left[2 * rows : 2 * rows + 8], from_links), pick(from_right[2 * rows : 2 * rows + 8], from_links)).astype(jnp.int32)
    facing = jnp.where(part == 2, pick(lead, jnp.maximum(theirs, 0)), pick(trail, jnp.maximum(theirs, 0)))
    target = jnp.where(part < 2, jnp.where(named < columns, named, -1), jnp.where(theirs >= 0, facing, -1))
    link_row = lax.broadcasted_iota(jnp.int32, shape, 0)
    target = jnp.where(link_row == links, own_column, target)
    far = ((part == 0) & (named >= columns + halo)) | ((part == 1) & (named >= columns) & (named < columns + halo))
    far = jnp.sum(jnp.where(far & (link_row < links), 1.0, 0.0), axis=1, keepdims=True)
    far = jnp.sum(far, axis=0, keepdims=True)
    by_lane = target.astype(F32).T
    column = lax.broadcasted_iota(jnp.int32, (columns, columns), 1).astype(F32)
    first_half = lax.broadcasted_iota(jnp.int32, (columns, columns), 0) < 4 * halo
    for link in range(links + 1):
        hit = jnp.broadcast_to(by_lane[:, link : link + 1], (columns, columns)) == column
        target_ref[link * columns : (link + 1) * columns, 0:columns] = jnp.where(hit & first_half, 1.0, 0.0).astype(BF16)
        target_ref[link * columns : (link + 1) * columns, columns:] = jnp.where(hit & ~first_half, 1.0, 0.0).astype(BF16)

    sources = [from_left[0:rows], from_right[0:rows], left_ref[...], right_ref[...]]
    second = [from_left[rows : 2 * rows], from_right[rows : 2 * rows]]
    for index in range(group):
        cut = [slice(index * vectors + kk * half, index * vectors + (kk + 1) * half) for kk in (0, 1)]
        for position, block in enumerate(turn_groups([s[c] for c in cut for s in sources], halo)):
            rim_field_ref[position * group + index] = block
        for position, block in enumerate(turn_groups([s[c] for c in cut for s in second + second], halo)):
            late_ref[position * group + index] = block

    above = None
    for level in range(levels):
        value = rim_field_ref[level] * plane_ref[1, level : level + 1, :]
        if level > 0:
            value = value - plane_ref[0, level : level + 1, :] * above
        rim_field_ref[level] = value
        above = value
    own_lanes = parts_of((half, columns)) < 2
    wide = 2 * group
    below = None
    for level in range(levels - 1, -1, -1):
        value = rim_field_ref[level]
        if below is not None:
            value = value - plane_ref[2, level : level + 1, :] * below
        below = value
        at = level // wide * 2 * wide * half + level % wide * half
        for link in range(links + 1):
            term = value * plane_ref[3 + link, level : level + 1, :]
            if link == links:
                term = jnp.where(own_lanes, term, late_ref[level])
            top, low = split(term)
            cols = slice(link * columns, (link + 1) * columns)
            spread_ref[at : at + half, cols] = top
            spread_ref[at + wide * half : at + (wide + 1) * half, cols] = low

    above = None
    span = wide * half
    for index in range(levels // wide):
        both = jnp.dot(spread_ref[2 * span * index : 2 * span * (index + 1), :], target_ref[...], preferred_element_type=F32)
        both = both[:span] + both[span:]
        for level in range(index * wide, (index + 1) * wide):
            at = (level - index * wide) * half
            came = jnp.concatenate([both[at : at + half, :columns], both[at : at + half, columns:]], axis=0)
            value = (moved_ref[level] + came) * pivot_ref[level : level + 1, :]
            if level > 0:
                value = value - carry_ref[level : level + 1, :] * above
            forward_ref[level] = value
            above = value

    cross = jnp.zeros((vectors, vectors), F32)
    square = jnp.zeros((vectors, columns), F32)
    below = None
    for level in range(levels - 1, -1, -1):
        value = forward_ref[level]
        if below is not None:
            value = value - ratio_ref[level : level + 1, :] * below
        below = value
        image_ref[level] = value
        square = square + value * value
        cross = cross + dot3(value, field_ref[level], NT)
    sums_ref[0:vectors, 0:vectors] = cross
    sums_ref[0:vectors, vectors : 2 * vectors] = gram_ref[...]
    norm = jnp.sum(square, axis=1, keepdims=True)
    shape = (vectors, 2 * vectors)
    eye = lax.broadcasted_iota(jnp.int32, shape, 0) == lax.broadcasted_iota(jnp.int32, shape, 1)
    norm = jnp.sum(jnp.where(eye, norm, 0.0), axis=0, keepdims=True)
    shape = (8, 2 * vectors)
    sums_ref[vectors : vectors + 8, :] = jnp.where(lax.broadcasted_iota(jnp.int32, shape, 0) == 0, norm, far)


def weigh_kernel(cells, sums_ref, more_ref, spans_ref, scale_ref, coupling_ref, direct_ref):
    vectors = coupling_ref.shape[0]
    sums = sums_ref[...] + more_ref[...]
    cross = sums[0:vectors, 0:vectors] / cells
    gram = sums[0:vectors, vectors : 2 * vectors] / cells
    coupling_ref[...] = cross.T
    shape = (vectors, vectors)
    eye = lax.broadcasted_iota(jnp.int32, shape, 0) == lax.broadcasted_iota(jnp.int32, shape, 1)
    square = sums[vectors : vectors + 1, 0:vectors] / cells
    square = jnp.sum(jnp.where(eye, square, 0.0), axis=1, keepdims=True)
    mixed = dot3(cross, gram, (((1,), (0,)), ((), ())))
    spanned = jnp.sum(cross * mixed, axis=1, keepdims=True)
    shared = 2.0 * jnp.sum(cross * cross, axis=1, keepdims=True)
    norm = square - shared + spanned
    small = norm + 1e-6 < 1e-2 * (square + shared + jnp.abs(spanned))
    scale_ref[...] = jnp.broadcast_to(1.0 / jnp.sqrt(jnp.maximum(norm, 0.0) + 1e-6), scale_ref.shape)
    far = jnp.sum(sums[vectors + 1 : vectors + 2, 0:1])
    direct_ref[0] = jnp.where(far + jnp.sum(jnp.where(small, 1.0, 0.0)) > 0.0, 1, 0)
    top, low = split(cross)
    spans_ref[...] = jnp.concatenate([top, top, low], axis=1)


def last_kernel(spans_ref, scale_ref, image_ref, field_ref, next_ref, chunk_ref, sems):
    levels, vectors, columns = image_ref.shape
    chunks = chunk_ref.shape[0]
    step = levels // chunks
    copies = [pltpu.make_async_copy(chunk_ref.at[i], next_ref.at[:, step * i : step * (i + 1), :], sems.at[i]) for i in range(chunks)]
    for level in range(levels):
        top, low = split(field_ref[level])
        spanned = jnp.dot(spans_ref[...], jnp.concatenate([top, low, top], axis=0), preferred_element_type=F32)
        chunk_ref[level // step, :, level % step, :] = (image_ref[level] - spanned) * scale_ref[...]
        if level % step == step - 1:
            copies[level // step].start()
    for copy in copies:
        copy.wait()


VMEM = pl.BlockSpec(memory_space=pltpu.VMEM)
SMEM = pl.BlockSpec(memory_space=pltpu.SMEM)
ANY = pl.BlockSpec(memory_space=pl.ANY)


def call(kernel, outs, out_specs, scratch, specs, *operands):
    return pl.pallas_call(
        kernel,
        out_shape=outs,
        in_specs=specs,
        out_specs=out_specs,
        scratch_shapes=scratch,
        compiler_params=pltpu.CompilerParams(vmem_limit_bytes=40 << 20),
    )(*operands)


def exchange(outer, inner):
    blocks = lax.axis_size(AXES)
    outer = lax.ppermute(outer, AXES, [(i, (i - 1) % blocks if i % 2 == 0 else (i + 1) % blocks) for i in range(blocks)])
    inner = lax.ppermute(inner, AXES, [(i, i ^ 1) for i in range(blocks)])
    return outer, inner


def almost_total(value):
    blocks = lax.axis_size(AXES)
    if blocks & (blocks - 1):
        return lax.psum(value, AXES), jnp.zeros_like(value)
    more = lax.ppermute(value, AXES, [(i, i ^ 1) for i in range(blocks)])
    distance = 2
    while distance < blocks:
        value = value + more
        more = lax.ppermute(value, AXES, [(i, i ^ distance) for i in range(blocks)])
        distance *= 2
    return value, more


def shards(basis, weights, kappa, thickness, depth, neighbours, rim_lists, counts):
    vectors, levels, columns = basis.shape
    links = weights.shape[0]
    halo = rim_lists.shape[1]
    group = levels * halo // LANES
    rows = group * vectors
    chunks = 4

    def out(*shape, dtype=F32):
        return jax.ShapeDtypeStruct(shape, dtype)

    slots = out(rows, LANES)
    message = out(2 * rows + levels, LANES)
    whole = out(levels, vectors, columns)
    plane = out(levels, columns)
    forward = pltpu.VMEM((levels, vectors, columns), F32)
    chunk = pltpu.VMEM((chunks, vectors, levels // chunks, columns), F32)
    sems = pltpu.SemaphoreType.DMA((chunks,))
    even = (1 - lax.axis_index(AXES) % 2).astype(jnp.int32).reshape(1)
    outer, inner, left, right, field, moved, live, self_weight, carry, pivot, ratio = call(
        functools.partial(first_kernel, halo, group),
        (message, message, slots, slots, whole, whole, out(links, levels, columns), plane, plane, plane, plane), [VMEM] * 11,
        [pltpu.VMEM((links * columns, columns + LANES), BF16), pltpu.VMEM((2 * levels * vectors, links * columns), BF16),
         forward, chunk, sems],
        [SMEM] * 3 + [ANY] + [VMEM] * 5,
        counts, even, rim_lists, basis, weights, kappa, thickness, depth.reshape(1, columns), neighbours)
    outer, inner = exchange(outer, inner)
    (gram,) = call(gram_kernel, (out(vectors, vectors),), [VMEM], [], [VMEM], field)
    image, sums = call(
        functools.partial(second_kernel, halo, group), (whole, out(vectors + 8, 2 * vectors)), [VMEM] * 2,
        [pltpu.VMEM((links + 4, levels, columns), F32), pltpu.VMEM(((links + 1) * columns, 2 * columns), BF16),
         pltpu.VMEM((levels, vectors // 2, columns), F32), pltpu.VMEM((levels, vectors // 2, columns), F32),
         pltpu.VMEM((levels * vectors, (links + 1) * columns), BF16), forward],
        [SMEM] * 2 + [VMEM] * 13,
        even, rim_lists, outer, inner, left, right, field, moved, live, self_weight, carry, pivot, ratio, neighbours, gram)
    sums, more = almost_total(sums)
    cells = float(levels * columns * lax.axis_size(AXES))
    spans, scale, coupling, direct = call(
        functools.partial(weigh_kernel, cells),
        (out(vectors, 3 * vectors, dtype=BF16), out(vectors, columns), out(vectors, vectors), out(1, dtype=jnp.int32)),
        [VMEM] * 3 + [SMEM], [], [VMEM] * 2, sums, more)

    def from_sums():
        (result,) = call(last_kernel, (out(vectors, levels, columns),), [ANY], [chunk, sems], [VMEM] * 4, spans, scale, image, field)
        return result, coupling

    def from_scratch():
        return direct_form(basis, weights, kappa, thickness, depth, neighbours, rim_lists, counts)

    return lax.cond(direct[0] > 0, from_scratch, from_sums)


ITERS = 2


def from_behind(block, axis, distance):
    devices = range(lax.axis_size(axis))
    route = [((i - distance) % len(devices), i) for i in devices]
    return lax.ppermute(block, axis, route)


def column_factors(kappa, thickness, keep):
    levels = kappa.shape[0]
    below = jnp.concatenate([keep[1:], jnp.zeros_like(keep[:1])], axis=0)
    interface = kappa * keep * below
    lower, inv_pivot, ratio = ([], [], [])
    for level in range(levels):
        upper_term = interface[level]
        diag_term = 1.0 + upper_term / thickness[level]
        if level > 0:
            diag_term = diag_term + interface[level - 1] / thickness[level]
            low = -interface[level - 1] / thickness[level - 1]
        else:
            low = jnp.zeros_like(upper_term)
        if level < levels - 1:
            upp = -upper_term / thickness[level + 1]
        else:
            upp = jnp.zeros_like(upper_term)
        pivot = diag_term - low * ratio[level - 1] if level > 0 else diag_term
        inverse = 1.0 / pivot
        lower.append(low)
        inv_pivot.append(inverse)
        ratio.append(upp * inverse)
    return (lower, inv_pivot, ratio)


def column_solve(rhs, lower, inv_pivot, ratio):
    levels = rhs.shape[1]
    forward = []
    for level in range(levels):
        if level == 0:
            forward.append(rhs[:, 0] * inv_pivot[0])
        else:
            forward.append((rhs[:, level] - lower[level] * forward[level - 1]) * inv_pivot[level])
    result = [None] * levels
    result[levels - 1] = forward[levels - 1]
    for level in range(levels - 2, -1, -1):
        result[level] = forward[level] - ratio[level] * result[level + 1]
    return jnp.stack(result, axis=1)


def transport_back(field, weights, keep, self_weight, neighbours, rim_lists):
    columns = field.shape[2]
    halo_width = rim_lists.shape[1]
    masked = keep * field
    extended = jnp.zeros((field.shape[0], field.shape[1], columns + 2 * halo_width), jnp.float32)
    for link in range(weights.shape[0]):
        extended = extended.at[:, :, neighbours[link]].add(weights[link] * masked)
    from_right = from_behind(extended[:, :, columns : columns + halo_width], ("region", "sub"), -1)
    from_left = from_behind(extended[:, :, columns + halo_width :], ("region", "sub"), 1)
    result = self_weight * masked + extended[:, :, :columns]
    result = result.at[:, :, rim_lists[0]].add(from_right).at[:, :, rim_lists[1]].add(from_left)
    return keep * result


def direct_form(basis, weights, kappa, thickness, depth, neighbours, rim_lists, counts):
    vectors, levels, columns = basis.shape
    halo_width = rim_lists.shape[1]
    own_index = jnp.arange(columns, dtype=jnp.int32)
    live = (own_index < counts[0]) | (own_index >= columns - 2 * halo_width)
    wet = jnp.arange(levels, dtype=jnp.int32)[:, None] < depth[None, :]
    keep = (live[None, :] & wet).astype(jnp.float32)
    self_weight = 1.0 - jnp.sum(weights, axis=0)
    lower, inv_pivot, ratio = column_factors(kappa, thickness, keep)
    field = basis
    for step in range(ITERS):
        moved = transport_back(field, weights, keep, self_weight, neighbours, rim_lists)
        field = column_solve(keep * moved, lower, inv_pivot, ratio)
    cells = float(levels * columns * lax.axis_size(("region", "sub")))
    high = lax.Precision.HIGHEST
    local_cross = jnp.einsum("ilc,jlc->ij", basis, field, precision=high)
    coupling = lax.psum(local_cross, ("region", "sub")) / cells
    residual = field - jnp.einsum("ilc,ij->jlc", basis, coupling, precision=high)
    local_norms = jnp.einsum("jlc,jlc->j", residual, residual, precision=high)
    norms = lax.psum(local_norms, ("region", "sub")) / cells
    next_basis = residual / jnp.sqrt(norms + 1e-06)[:, None, None]
    return (next_basis, coupling)


def solution(mesh):
    placed = (
        P("groups", None, AXES),
        P(None, None, AXES),
        P(None, AXES),
        P(None, AXES),
        P(AXES),
        P(None, AXES),
        P(None, AXES),
        P(AXES),
    )
    return jax.shard_map(
        shards,
        mesh=mesh,
        in_specs=placed,
        out_specs=(P("groups", None, AXES), P("groups", None)),
        check_vma=False,
    )
```

```python
import functools

import jax
import jax.numpy as jnp
from jax import lax
from jax.experimental import pallas as pl
from jax.experimental.pallas import tpu as pltpu
from jax.sharding import PartitionSpec as P

AXES = ("region", "sub")
LANES = 128
F32 = jnp.float32
BF16 = jnp.bfloat16
NT = (((1,), (1,)), ((), ()))


def split(x):
    top = x.astype(BF16)
    return top, (x - top.astype(F32)).astype(BF16)


def dot3(a, b, dims):
    a_top, a_low = split(a)
    b_top, b_low = split(b)
    dot = functools.partial(lax.dot_general, dimension_numbers=dims, preferred_element_type=F32)
    return dot(a_top, b_top) + (dot(a_top, b_low) + dot(a_low, b_top))


def link_targets(neighbours_ref, targets_ref, halo):
    links, columns = neighbours_ref.shape
    padded = jnp.concatenate([neighbours_ref[...].astype(F32), jnp.zeros((8 - links, columns), F32)], axis=0)
    by_column = padded.T
    lane = lax.broadcasted_iota(jnp.int32, (columns, LANES), 1)
    own = lane.astype(F32)
    slot = (columns + lane % (2 * halo)).astype(F32)
    for link in range(links):
        target = jnp.broadcast_to(by_column[:, link : link + 1], (columns, LANES))
        rows = slice(link * columns, (link + 1) * columns)
        targets_ref[rows, 0:columns] = jnp.where(target == own, 1.0, 0.0).astype(BF16)
        targets_ref[rows, columns : columns + LANES] = jnp.where(target == slot, 1.0, 0.0).astype(BF16)


def spread_level(value, level, weights_ref, spread_ref, group):
    links, _, columns = weights_ref.shape
    vectors = value.shape[0]
    first = level // group * 2 * group * vectors + level % group * vectors
    second = first + group * vectors
    for link in range(links):
        top, low = split(value * weights_ref[link, level : level + 1, :])
        cols = slice(link * columns, (link + 1) * columns)
        spread_ref[first : first + vectors, cols] = top
        spread_ref[second : second + vectors, cols] = low


def move_group(index, spread_ref, targets_ref, rows, columns):
    both = jnp.dot(spread_ref[2 * rows * index : 2 * rows * (index + 1), :], targets_ref[...], preferred_element_type=F32)
    both = both[:rows] + both[rows:]
    return both[:, :columns], both[:, columns:]


def pack(parts, halo):
    lane = lax.broadcasted_iota(jnp.int32, parts[0].shape, 1)
    left = jnp.zeros_like(parts[0])
    right = jnp.zeros_like(parts[0])
    for index, part in enumerate(parts):
        turned = pltpu.roll(part, halo, 1)
        mine = lane // halo == index
        left = jnp.where(mine, turned if index % 2 else part, left)
        right = jnp.where(mine, part if index % 2 else turned, right)
    return left, right


def factor_columns(kappa_ref, thickness_ref, keep, carry_ref, pivot_ref, ratio_ref):
    levels = keep.shape[0]
    interface = [kappa_ref[i : i + 1, :] * keep[i : i + 1] * keep[i + 1 : i + 2] for i in range(levels - 1)]
    ratio = None
    for level in range(levels):
        thick = thickness_ref[level : level + 1, :]
        pivot = jnp.ones_like(thick)
        if level < levels - 1:
            pivot = pivot + interface[level] / thick
        if level > 0:
            pivot = pivot + interface[level - 1] / thick
            low = -interface[level - 1] / thickness_ref[level - 1 : level, :]
            pivot = pivot - low * ratio
        inverse = 1.0 / pivot
        carry_ref[level : level + 1, :] = low * inverse if level > 0 else jnp.zeros_like(thick)
        pivot_ref[level : level + 1, :] = keep[level : level + 1] * inverse
        if level < levels - 1:
            ratio = -interface[level] / thickness_ref[level + 1 : level + 2, :] * inverse
            ratio_ref[level : level + 1, :] = ratio
        else:
            ratio_ref[level : level + 1, :] = jnp.zeros_like(thick)


def lane_group(shape, width):
    return lax.broadcasted_iota(jnp.int32, shape, 1) // width


def pick(plane, lanes):
    return jnp.take_along_axis(plane, lanes, axis=1, mode="promise_in_bounds")


def rim_lanes(rim_ref, row, halo, shape):
    slot = lax.broadcasted_iota(jnp.int32, shape, 1) % halo
    columns = jnp.zeros(shape, jnp.int32)
    for index in range(halo):
        columns = jnp.where(slot == index, rim_ref[row, index], columns)
    return columns


def rim_coefficients(planes, neighbours, columns, first, halo):
    group = lane_group(columns.shape, halo)
    packed = jnp.zeros(columns.shape, F32)
    for index, plane in enumerate(planes):
        packed = jnp.where(group == index, pick(plane, columns), packed)
    slot = pick(neighbours, columns) - first
    slot = jnp.where((slot >= 0) & (slot < halo), slot, -1)
    return jnp.where(group == len(planes), slot.astype(F32), packed)


def padded_links(neighbours_ref, rows):
    links, columns = neighbours_ref.shape
    padded = jnp.concatenate([neighbours_ref[...], jnp.zeros((8 - links, columns), jnp.int32)], axis=0)
    if rows > 8:
        padded = jnp.concatenate([padded, jnp.zeros((rows - 8, columns), jnp.int32)], axis=0)
    return padded


def first_kernel(halo, group, counts_ref, even_ref, rim_ref, basis_ref, weights_ref, kappa_ref, thickness_ref, depth_ref,
                 neighbours_ref, outer_ref, inner_ref, left_ref, right_ref, field_ref, moved_ref, live_ref, self_ref,
                 carry_ref, pivot_ref, ratio_ref, targets_ref, spread_ref, forward_ref, chunk_ref, sems):
    vectors, levels, columns = basis_ref.shape
    links = weights_ref.shape[0]
    chunks = chunk_ref.shape[0]
    step = levels // chunks
    copies = [pltpu.make_async_copy(basis_ref.at[:, step * i : step * (i + 1), :], chunk_ref.at[i], sems.at[i]) for i in range(chunks)]
    for copy in copies:
        copy.start()
    lane = lax.broadcasted_iota(jnp.int32, (levels, columns), 1)
    level_of = lax.broadcasted_iota(jnp.int32, (levels, columns), 0)
    live = (lane < counts_ref[0]) | (lane >= columns - 2 * halo)
    keep = jnp.where(live & (level_of < depth_ref[...]), 1.0, 0.0)
    total = weights_ref[0]
    for link in range(1, links):
        total = total + weights_ref[link]
    self_ref[...] = keep * (1.0 - total)
    for link in range(links):
        live_ref[link] = keep * weights_ref[link]
    link_targets(neighbours_ref, targets_ref, halo)
    factor_columns(kappa_ref, thickness_ref, keep, carry_ref, pivot_ref, ratio_ref)
    rows = group * vectors
    parts = []
    above = None
    for index in range(levels // group):
        for level in range(index * group, (index + 1) * group):
            if level % step == 0:
                copies[level // step].wait()
            value = chunk_ref[level // step, :, level % step, :]
            field_ref[level] = value
            spread_level(value, level, live_ref, spread_ref, group)
        own, slots = move_group(index, spread_ref, targets_ref, rows, columns)
        parts.append(slots)
        for level in range(index * group, (index + 1) * group):
            at = (level - index * group) * vectors
            value = own[at : at + vectors] + field_ref[level] * self_ref[level : level + 1, :]
            value = value * pivot_ref[level : level + 1, :]
            if level > 0:
                value = value - carry_ref[level : level + 1, :] * above
            forward_ref[level] = value
            above = value
    left, right = pack(parts, halo)
    left_ref[...] = left
    right_ref[...] = right
    even = even_ref[0] > 0
    outer_ref[0:rows, :] = jnp.where(even, left, right)
    inner_ref[0:rows, :] = jnp.where(even, right, left)
    below = None
    for index in range(levels // group - 1, -1, -1):
        for level in range((index + 1) * group - 1, index * group - 1, -1):
            value = forward_ref[level]
            if below is not None:
                value = value - ratio_ref[level : level + 1, :] * below
            below = value
            forward_ref[level] = value
            spread_level(value, level, live_ref, spread_ref, group)
        own, parts[index] = move_group(index, spread_ref, targets_ref, rows, columns)
        for level in range(index * group, (index + 1) * group):
            at = (level - index * group) * vectors
            moved_ref[level] = own[at : at + vectors] + forward_ref[level] * self_ref[level : level + 1, :]
    left, right = pack(parts, halo)
    outer_ref[rows : 2 * rows, :] = jnp.where(even, left, right)
    inner_ref[rows : 2 * rows, :] = jnp.where(even, right, left)
    planes = [carry_ref[...], pivot_ref[...], ratio_ref[...]] + [live_ref[link] for link in range(links)]
    neighbours = padded_links(neighbours_ref, levels)
    left = rim_coefficients(planes, neighbours, rim_lanes(rim_ref, 1, halo, (levels, columns)), columns, halo)
    right = rim_coefficients(planes, neighbours, rim_lanes(rim_ref, 0, halo, (levels, columns)), columns + halo, halo)
    outer_ref[2 * rows :, :] = jnp.where(even, left, right)
    inner_ref[2 * rows :, :] = jnp.where(even, right, left)


def stack_terms(value, level, stack_ref):
    vectors, columns = value.shape
    top, low = split(value)
    cols = slice(level * columns, (level + 1) * columns)
    stack_ref[0:vectors, cols] = top
    stack_ref[vectors:, cols] = low


def stacked_products(a_ref, b_ref, first, last):
    return lax.dot_general(a_ref[:, first:last], b_ref[:, first:last], NT, preferred_element_type=F32)


def join_products(products):
    half = products.shape[0] // 2
    return products[:half, :half] + (products[:half, half:] + products[half:, :half])


def gram_kernel(field_ref, stack_ref, gram_ref):
    levels, _, columns = field_ref.shape
    span = levels // 4
    gram = None
    for index in range(4):
        for level in range(span * index, span * (index + 1)):
            stack_terms(field_ref[level], level, stack_ref)
        part = stacked_products(stack_ref, stack_ref, span * index * columns, span * (index + 1) * columns)
        gram = part if gram is None else gram + part
    gram_ref[...] = join_products(gram)


def turn_groups(blocks, halo):
    blocks = list(blocks)
    lanes = blocks[0].shape[1]
    group = lane_group(blocks[0].shape, halo)
    bit = 1
    while bit < len(blocks):
        upper = group // bit % 2 == 1
        for low in range(len(blocks)):
            if low & bit:
                continue
            high = low | bit
            a, b = blocks[low], blocks[high]
            blocks[low] = jnp.where(upper, pltpu.roll(b, halo * bit, 1), a)
            blocks[high] = jnp.where(upper, b, pltpu.roll(a, lanes - halo * bit, 1))
        bit *= 2
    return blocks


def second_kernel(halo, group, even_ref, rim_ref, outer_ref, inner_ref, left_ref, right_ref, stack_ref, moved_ref, live_ref,
                  self_ref, carry_ref, pivot_ref, ratio_ref, neighbours_ref, gram_ref, image_ref, sums_ref,
                  plane_ref, target_ref, rim_field_ref, late_ref, spread_ref, came_ref, forward_ref, images_ref):
    levels, vectors, columns = moved_ref.shape
    links = live_ref.shape[0]
    rows = group * vectors
    half = vectors // 2
    even = even_ref[0] > 0
    outer = outer_ref[...]
    inner = inner_ref[...]
    from_left = jnp.where(even, outer, inner)
    from_right = jnp.where(even, inner, outer)

    def parts_of(shape):
        return lane_group(shape, halo) % 4

    shape = (levels, columns)
    part = parts_of(shape)
    slot = lax.broadcasted_iota(jnp.int32, shape, 1) % halo
    lead = rim_lanes(rim_ref, 1, halo, shape)
    trail = rim_lanes(rim_ref, 0, halo, shape)
    own_column = jnp.where(part % 2 == 0, lead, trail)
    planes = [carry_ref[...], pivot_ref[...], ratio_ref[...]] + [live_ref[link] for link in range(links)]
    for index, plane in enumerate(planes):
        theirs = jnp.where(part == 2, pick(from_left[2 * rows :], slot + halo * index), pick(from_right[2 * rows :], slot + halo * index))
        plane_ref[index] = jnp.where(part < 2, pick(plane, own_column), theirs)
    plane_ref[len(planes)] = pick(self_ref[...], own_column)

    shape = (8, columns)
    part, slot, lead, trail, own_column = part[0:8], slot[0:8], lead[0:8], trail[0:8], own_column[0:8]
    named = pick(padded_links(neighbours_ref, 8), own_column)
    from_links = slot + halo * len(planes)
    theirs = jnp.where(part == 2, pick(from_left[2 * rows : 2 * rows + 8], from_links), pick(from_right[2 * rows : 2 * rows + 8], from_links)).astype(jnp.int32)
    facing = jnp.where(part == 2, pick(lead, jnp.maximum(theirs, 0)), pick(trail, jnp.maximum(theirs, 0)))
    target = jnp.where(part < 2, jnp.where(named < columns, named, -1), jnp.where(theirs >= 0, facing, -1))
    link_row = lax.broadcasted_iota(jnp.int32, shape, 0)
    target = jnp.where(link_row == links, own_column, target)
    far = ((part == 0) & (named >= columns + halo)) | ((part == 1) & (named >= columns) & (named < columns + halo))
    far = jnp.sum(jnp.where(far & (link_row < links), 1.0, 0.0), axis=1, keepdims=True)
    far = jnp.sum(far, axis=0, keepdims=True)
    by_lane = target.astype(F32).T
    column = lax.broadcasted_iota(jnp.int32, (columns, columns), 1).astype(F32)
    first_half = lax.broadcasted_iota(jnp.int32, (columns, columns), 0) < 4 * halo
    for link in range(links + 1):
        hit = jnp.broadcast_to(by_lane[:, link : link + 1], (columns, columns)) == column
        target_ref[link * columns : (link + 1) * columns, 0:columns] = jnp.where(hit & first_half, 1.0, 0.0).astype(BF16)
        target_ref[link * columns : (link + 1) * columns, columns:] = jnp.where(hit & ~first_half, 1.0, 0.0).astype(BF16)

    sources = [from_left[0:rows], from_right[0:rows], left_ref[...], right_ref[...]]
    second = [from_left[rows : 2 * rows], from_right[rows : 2 * rows]]
    for index in range(group):
        cut = [slice(index * vectors + kk * half, index * vectors + (kk + 1) * half) for kk in (0, 1)]
        for position, block in enumerate(turn_groups([s[c] for c in cut for s in sources], halo)):
            rim_field_ref[position * group + index] = block
        for position, block in enumerate(turn_groups([s[c] for c in cut for s in second + second], halo)):
            late_ref[position * group + index] = block

    above = None
    for level in range(levels):
        value = rim_field_ref[level] * plane_ref[1, level : level + 1, :]
        if level > 0:
            value = value - plane_ref[0, level : level + 1, :] * above
        rim_field_ref[level] = value
        above = value
    own_lanes = parts_of((half, columns)) < 2
    wide = 2 * group
    span = wide * half
    below = None
    for index in range(levels // wide - 1, -1, -1):
        for level in range((index + 1) * wide - 1, index * wide - 1, -1):
            value = rim_field_ref[level]
            if below is not None:
                value = value - plane_ref[2, level : level + 1, :] * below
            below = value
            at = 2 * span * index + level % wide * half
            for link in range(links + 1):
                term = value * plane_ref[3 + link, level : level + 1, :]
                if link == links:
                    term = jnp.where(own_lanes, term, late_ref[level])
                top, low = split(term)
                cols = slice(link * columns, (link + 1) * columns)
                spread_ref[at : at + half, cols] = top
                spread_ref[at + span : at + span + half, cols] = low
        both = jnp.dot(spread_ref[2 * span * index : 2 * span * (index + 1), :], target_ref[...], preferred_element_type=F32)
        came_ref[span * index : span * (index + 1), :] = both[:span] + both[span:]

    above = None
    for level in range(levels):
        rows = slice(level * half, (level + 1) * half)
        came = jnp.concatenate([came_ref[rows, :columns], came_ref[rows, columns:]], axis=0)
        value = (moved_ref[level] + came) * pivot_ref[level : level + 1, :]
        if level > 0:
            value = value - carry_ref[level : level + 1, :] * above
        forward_ref[level] = value
        above = value

    products = None
    square = jnp.zeros((vectors, columns), F32)
    below = None
    for index in range(levels // wide - 1, -1, -1):
        for level in range((index + 1) * wide - 1, index * wide - 1, -1):
            value = forward_ref[level]
            if below is not None:
                value = value - ratio_ref[level : level + 1, :] * below
            below = value
            image_ref[level] = value
            square = square + value * value
            stack_terms(value, level, images_ref)
        part = stacked_products(images_ref, stack_ref, wide * index * columns, wide * (index + 1) * columns)
        products = part if products is None else products + part
    cross = join_products(products)
    sums_ref[0:vectors, 0:vectors] = cross
    sums_ref[0:vectors, vectors : 2 * vectors] = gram_ref[...]
    norm = jnp.sum(square, axis=1, keepdims=True)
    shape = (vectors, 2 * vectors)
    eye = lax.broadcasted_iota(jnp.int32, shape, 0) == lax.broadcasted_iota(jnp.int32, shape, 1)
    norm = jnp.sum(jnp.where(eye, norm, 0.0), axis=0, keepdims=True)
    shape = (8, 2 * vectors)
    sums_ref[vectors : vectors + 8, :] = jnp.where(lax.broadcasted_iota(jnp.int32, shape, 0) == 0, norm, far)


def weigh_kernel(cells, sums_ref, more_ref, spans_ref, scale_ref, coupling_ref, direct_ref):
    vectors = coupling_ref.shape[0]
    sums = sums_ref[...] + more_ref[...]
    cross = sums[0:vectors, 0:vectors] / cells
    gram = sums[0:vectors, vectors : 2 * vectors] / cells
    coupling_ref[...] = cross.T
    shape = (vectors, vectors)
    eye = lax.broadcasted_iota(jnp.int32, shape, 0) == lax.broadcasted_iota(jnp.int32, shape, 1)
    square = sums[vectors : vectors + 1, 0:vectors] / cells
    square = jnp.sum(jnp.where(eye, square, 0.0), axis=1, keepdims=True)
    mixed = dot3(cross, gram, (((1,), (0,)), ((), ())))
    spanned = jnp.sum(cross * mixed, axis=1, keepdims=True)
    shared = 2.0 * jnp.sum(cross * cross, axis=1, keepdims=True)
    norm = square - shared + spanned
    small = norm + 1e-6 < 1e-2 * (square + shared + jnp.abs(spanned))
    scale_ref[...] = jnp.broadcast_to(1.0 / jnp.sqrt(jnp.maximum(norm, 0.0) + 1e-6), scale_ref.shape)
    far = jnp.sum(sums[vectors + 1 : vectors + 2, 0:1])
    direct_ref[0] = jnp.where(far + jnp.sum(jnp.where(small, 1.0, 0.0)) > 0.0, 1, 0)
    top, low = split(cross)
    spans_ref[...] = jnp.concatenate([jnp.concatenate([top, top], axis=1), jnp.concatenate([low, low], axis=1)], axis=0)


def last_kernel(spans_ref, scale_ref, image_ref, stack_ref, sums_ref, next_ref, coupling_ref, chunk_ref, sems):
    levels, vectors, columns = image_ref.shape
    chunks = chunk_ref.shape[0]
    step = levels // chunks
    copies = [pltpu.make_async_copy(chunk_ref.at[i], next_ref.at[:, step * i : step * (i + 1), :], sems.at[i]) for i in range(chunks)]
    copies.append(pltpu.make_async_copy(sums_ref, coupling_ref, sems.at[chunks]))
    copies[chunks].start()
    for index in range(chunks):
        cols = slice(step * index * columns, step * (index + 1) * columns)
        both = jnp.dot(spans_ref[...], stack_ref[:, cols], preferred_element_type=F32)
        spanned = both[:vectors] + both[vectors:]
        for level in range(step):
            at = level * columns
            chunk_ref[index, :, level, :] = (image_ref[step * index + level] - spanned[:, at : at + columns]) * scale_ref[...]
        copies[index].start()
    for copy in copies:
        copy.wait()


VMEM = pl.BlockSpec(memory_space=pltpu.VMEM)
SMEM = pl.BlockSpec(memory_space=pltpu.SMEM)
ANY = pl.BlockSpec(memory_space=pl.ANY)


def call(kernel, outs, out_specs, scratch, specs, *operands):
    return pl.pallas_call(
        kernel,
        out_shape=outs,
        in_specs=specs,
        out_specs=out_specs,
        scratch_shapes=scratch,
        compiler_params=pltpu.CompilerParams(vmem_limit_bytes=40 << 20),
    )(*operands)


def exchange(outer, inner):
    blocks = lax.axis_size(AXES)
    outer = lax.ppermute(outer, AXES, [(i, (i - 1) % blocks if i % 2 == 0 else (i + 1) % blocks) for i in range(blocks)])
    inner = lax.ppermute(inner, AXES, [(i, i ^ 1) for i in range(blocks)])
    return outer, inner


def almost_total(value):
    blocks = lax.axis_size(AXES)
    if blocks & (blocks - 1):
        return lax.psum(value, AXES), jnp.zeros_like(value)
    more = lax.ppermute(value, AXES, [(i, i ^ 1) for i in range(blocks)])
    distance = 2
    while distance < blocks:
        value = value + more
        more = lax.ppermute(value, AXES, [(i, i ^ distance) for i in range(blocks)])
        distance *= 2
    return value, more


def shards(basis, weights, kappa, thickness, depth, neighbours, rim_lists, counts):
    vectors, levels, columns = basis.shape
    links = weights.shape[0]
    halo = rim_lists.shape[1]
    group = levels * halo // LANES
    rows = group * vectors
    chunks = 4

    def out(*shape, dtype=F32):
        return jax.ShapeDtypeStruct(shape, dtype)

    slots = out(rows, LANES)
    message = out(2 * rows + levels, LANES)
    whole = out(levels, vectors, columns)
    plane = out(levels, columns)
    forward = pltpu.VMEM((levels, vectors, columns), F32)
    chunk = pltpu.VMEM((chunks, vectors, levels // chunks, columns), F32)
    sems = pltpu.SemaphoreType.DMA((chunks,))
    even = (1 - lax.axis_index(AXES) % 2).astype(jnp.int32).reshape(1)
    outer, inner, left, right, field, moved, live, self_weight, carry, pivot, ratio = call(
        functools.partial(first_kernel, halo, group),
        (message, message, slots, slots, whole, whole, out(links, levels, columns), plane, plane, plane, plane), [VMEM] * 11,
        [pltpu.VMEM((links * columns, columns + LANES), BF16), pltpu.VMEM((2 * levels * vectors, links * columns), BF16),
         forward, chunk, sems],
        [SMEM] * 3 + [ANY] + [VMEM] * 5,
        counts, even, rim_lists, basis, weights, kappa, thickness, depth.reshape(1, columns), neighbours)
    outer, inner = exchange(outer, inner)
    stacked = out(2 * vectors, levels * columns, dtype=BF16)
    stack, gram = call(gram_kernel, (stacked, out(vectors, vectors)), [VMEM] * 2, [], [VMEM], field)
    image, sums = call(
        functools.partial(second_kernel, halo, group), (whole, out(vectors + 8, 2 * vectors)), [VMEM] * 2,
        [pltpu.VMEM((links + 4, levels, columns), F32), pltpu.VMEM(((links + 1) * columns, 2 * columns), BF16),
         pltpu.VMEM((levels, vectors // 2, columns), F32), pltpu.VMEM((levels, vectors // 2, columns), F32),
         pltpu.VMEM((levels * vectors, (links + 1) * columns), BF16), pltpu.VMEM((levels * vectors // 2, 2 * columns), F32),
         forward, pltpu.VMEM((2 * vectors, levels * columns), BF16)],
        [SMEM] * 2 + [VMEM] * 13,
        even, rim_lists, outer, inner, left, right, stack, moved, live, self_weight, carry, pivot, ratio, neighbours, gram)
    sums, more = almost_total(sums)
    cells = float(levels * columns * lax.axis_size(AXES))
    spans, scale, coupling, direct = call(
        functools.partial(weigh_kernel, cells),
        (out(2 * vectors, 2 * vectors, dtype=BF16), out(vectors, columns), out(vectors, vectors), out(1, dtype=jnp.int32)),
        [VMEM] * 3 + [SMEM], [], [VMEM] * 2, sums, more)

    def from_sums():
        return call(last_kernel, (out(vectors, levels, columns), out(vectors, vectors)), [ANY] * 2,
                    [chunk, pltpu.SemaphoreType.DMA((chunks + 1,))], [VMEM] * 5, spans, scale, image, stack, coupling)

    def from_scratch():
        return direct_form(basis, weights, kappa, thickness, depth, neighbours, rim_lists, counts)

    return tuple(lax.cond(direct[0] > 0, from_scratch, lambda: tuple(from_sums())))


ITERS = 2


def from_behind(block, axis, distance):
    devices = range(lax.axis_size(axis))
    route = [((i - distance) % len(devices), i) for i in devices]
    return lax.ppermute(block, axis, route)


def column_factors(kappa, thickness, keep):
    levels = kappa.shape[0]
    below = jnp.concatenate([keep[1:], jnp.zeros_like(keep[:1])], axis=0)
    interface = kappa * keep * below
    lower, inv_pivot, ratio = ([], [], [])
    for level in range(levels):
        upper_term = interface[level]
        diag_term = 1.0 + upper_term / thickness[level]
        if level > 0:
            diag_term = diag_term + interface[level - 1] / thickness[level]
            low = -interface[level - 1] / thickness[level - 1]
        else:
            low = jnp.zeros_like(upper_term)
        if level < levels - 1:
            upp = -upper_term / thickness[level + 1]
        else:
            upp = jnp.zeros_like(upper_term)
        pivot = diag_term - low * ratio[level - 1] if level > 0 else diag_term
        inverse = 1.0 / pivot
        lower.append(low)
        inv_pivot.append(inverse)
        ratio.append(upp * inverse)
    return (lower, inv_pivot, ratio)


def column_solve(rhs, lower, inv_pivot, ratio):
    levels = rhs.shape[1]
    forward = []
    for level in range(levels):
        if level == 0:
            forward.append(rhs[:, 0] * inv_pivot[0])
        else:
            forward.append((rhs[:, level] - lower[level] * forward[level - 1]) * inv_pivot[level])
    result = [None] * levels
    result[levels - 1] = forward[levels - 1]
    for level in range(levels - 2, -1, -1):
        result[level] = forward[level] - ratio[level] * result[level + 1]
    return jnp.stack(result, axis=1)


def transport_back(field, weights, keep, self_weight, neighbours, rim_lists):
    columns = field.shape[2]
    halo_width = rim_lists.shape[1]
    masked = keep * field
    extended = jnp.zeros((field.shape[0], field.shape[1], columns + 2 * halo_width), jnp.float32)
    for link in range(weights.shape[0]):
        extended = extended.at[:, :, neighbours[link]].add(weights[link] * masked)
    from_right = from_behind(extended[:, :, columns : columns + halo_width], ("region", "sub"), -1)
    from_left = from_behind(extended[:, :, columns + halo_width :], ("region", "sub"), 1)
    result = self_weight * masked + extended[:, :, :columns]
    result = result.at[:, :, rim_lists[0]].add(from_right).at[:, :, rim_lists[1]].add(from_left)
    return keep * result


def direct_form(basis, weights, kappa, thickness, depth, neighbours, rim_lists, counts):
    vectors, levels, columns = basis.shape
    halo_width = rim_lists.shape[1]
    own_index = jnp.arange(columns, dtype=jnp.int32)
    live = (own_index < counts[0]) | (own_index >= columns - 2 * halo_width)
    wet = jnp.arange(levels, dtype=jnp.int32)[:, None] < depth[None, :]
    keep = (live[None, :] & wet).astype(jnp.float32)
    self_weight = 1.0 - jnp.sum(weights, axis=0)
    lower, inv_pivot, ratio = column_factors(kappa, thickness, keep)
    field = basis
    for step in range(ITERS):
        moved = transport_back(field, weights, keep, self_weight, neighbours, rim_lists)
        field = column_solve(keep * moved, lower, inv_pivot, ratio)
    cells = float(levels * columns * lax.axis_size(("region", "sub")))
    high = lax.Precision.HIGHEST
    local_cross = jnp.einsum("ilc,jlc->ij", basis, field, precision=high)
    coupling = lax.psum(local_cross, ("region", "sub")) / cells
    residual = field - jnp.einsum("ilc,ij->jlc", basis, coupling, precision=high)
    local_norms = jnp.einsum("jlc,jlc->j", residual, residual, precision=high)
    norms = lax.psum(local_norms, ("region", "sub")) / cells
    next_basis = residual / jnp.sqrt(norms + 1e-06)[:, None, None]
    return (next_basis, coupling)


def solution(mesh):
    placed = (
        P("groups", None, AXES),
        P(None, None, AXES),
        P(None, AXES),
        P(None, AXES),
        P(AXES),
        P(None, AXES),
        P(None, AXES),
        P(AXES),
    )
    return jax.shard_map(
        shards,
        mesh=mesh,
        in_specs=placed,
        out_specs=(P("groups", None, AXES), P("groups", None)),
        check_vma=False,
    )
```

```python
import functools

import jax
import jax.numpy as jnp
from jax import lax
from jax.experimental import pallas as pl
from jax.experimental.pallas import tpu as pltpu
from jax.sharding import PartitionSpec as P

AXES = ("region", "sub")
LANES = 128
F32 = jnp.float32
BF16 = jnp.bfloat16
NT = (((1,), (1,)), ((), ()))


def split(x):
    top = x.astype(BF16)
    return top, (x - top.astype(F32)).astype(BF16)


def dot3(a, b, dims):
    a_top, a_low = split(a)
    b_top, b_low = split(b)
    dot = functools.partial(lax.dot_general, dimension_numbers=dims, preferred_element_type=F32)
    return dot(a_top, b_top) + (dot(a_top, b_low) + dot(a_low, b_top))


def one_hot(hits, size):
    by_lane = hits.astype(F32).T
    lanes = by_lane.shape[0]
    column = lax.broadcasted_iota(jnp.int32, (lanes, size), 1).astype(F32)
    return [jnp.where(jnp.broadcast_to(by_lane[:, i : i + 1], (lanes, size)) == column, 1.0, 0.0).astype(BF16) for i in range(hits.shape[0])]


def spread_level(value, level, weights_ref, spread_ref, group):
    links, _, columns = weights_ref.shape
    vectors = value.shape[0]
    first = level // group * 2 * group * vectors + level % group * vectors
    second = first + group * vectors
    for link in range(links):
        top, low = split(value * weights_ref[link, level : level + 1, :])
        cols = slice(link * columns, (link + 1) * columns)
        spread_ref[first : first + vectors, cols] = top
        spread_ref[second : second + vectors, cols] = low


def matmul_group(index, spread_ref, targets_ref, rows):
    both = jnp.dot(spread_ref[2 * rows * index : 2 * rows * (index + 1), :], targets_ref[...], preferred_element_type=F32)
    return both[:rows] + both[rows:]


def factor_columns(kappa_ref, thickness_ref, keep, carry_ref, pivot_ref, ratio_ref):
    levels = keep.shape[0]
    interface = [kappa_ref[i : i + 1, :] * keep[i : i + 1] * keep[i + 1 : i + 2] for i in range(levels - 1)]
    ratio = None
    for level in range(levels):
        thick = thickness_ref[level : level + 1, :]
        pivot = jnp.ones_like(thick)
        if level < levels - 1:
            pivot = pivot + interface[level] / thick
        if level > 0:
            pivot = pivot + interface[level - 1] / thick
            low = -interface[level - 1] / thickness_ref[level - 1 : level, :]
            pivot = pivot - low * ratio
        inverse = 1.0 / pivot
        carry_ref[level : level + 1, :] = low * inverse if level > 0 else jnp.zeros_like(thick)
        pivot_ref[level : level + 1, :] = keep[level : level + 1] * inverse
        if level < levels - 1:
            ratio = -interface[level] / thickness_ref[level + 1 : level + 2, :] * inverse
            ratio_ref[level : level + 1, :] = ratio
        else:
            ratio_ref[level : level + 1, :] = jnp.zeros_like(thick)


def lane_group(shape, width):
    return lax.broadcasted_iota(jnp.int32, shape, 1) // width


def pick(plane, lanes):
    return jnp.take_along_axis(plane, lanes, axis=1, mode="promise_in_bounds")


def rim_lanes(rim_ref, row, halo, shape):
    slot = lax.broadcasted_iota(jnp.int32, shape, 1) % halo
    columns = jnp.zeros(shape, jnp.int32)
    for index in range(halo):
        columns = jnp.where(slot == index, rim_ref[row, index], columns)
    return columns


def rim_coefficients(planes, neighbours, columns, first, halo):
    group = lane_group(columns.shape, halo)
    packed = jnp.zeros(columns.shape, F32)
    for index, plane in enumerate(planes):
        packed = jnp.where(group == index, pick(plane, columns), packed)
    slot = pick(neighbours, columns) - first
    slot = jnp.where((slot >= 0) & (slot < halo), slot, -1)
    return jnp.where(group == len(planes), slot.astype(F32), packed)


def padded_links(neighbours_ref, rows):
    links, columns = neighbours_ref.shape
    padded = jnp.concatenate([neighbours_ref[...], jnp.zeros((8 - links, columns), jnp.int32)], axis=0)
    if rows > 8:
        padded = jnp.concatenate([padded, jnp.zeros((rows - 8, columns), jnp.int32)], axis=0)
    return padded


def pack_slots(levels, slot_group, halo):
    group = lane_group(levels[0].shape, halo) % 4
    packed = []
    for first in range(0, len(levels), 4):
        block = levels[first]
        for offset in range(4):
            turn = (offset - slot_group) * halo % LANES
            value = levels[first + offset]
            value = pltpu.roll(value, turn, 1) if turn else value
            block = value if offset == 0 else jnp.where(group == offset, value, block)
        packed.append(block)
    return packed


def edge_kernel(halo, counts_ref, rim_ref, basis_ref, weights_in, kappa_in, thickness_in, depth_in, neighbours_in,
                outer_ref, inner_ref, mirror_ref, field_ref, live_ref, self_ref, carry_ref, pivot_ref, ratio_ref, table_ref,
                near_ref, leave_ref, spread_ref, spread_two_ref, forward_ref, plane_ref, chunk_ref, weights_ref, kappa_ref,
                thickness_ref, depth_ref, neighbours_ref, sems, small_sems):
    small = [(weights_in, weights_ref), (kappa_in, kappa_ref), (thickness_in, thickness_ref), (depth_in, depth_ref), (neighbours_in, neighbours_ref)]
    small = [pltpu.make_async_copy(a, b, small_sems.at[i]) for i, (a, b) in enumerate(small)]
    for copy in small:
        copy.start()
    vectors, levels, columns = basis_ref.shape
    links = weights_ref.shape[0]
    half = vectors // 2
    chunks = chunk_ref.shape[0]
    step = levels // chunks
    copies = [pltpu.make_async_copy(basis_ref.at[:, step * i : step * (i + 1), :], chunk_ref.at[i], sems.at[i]) for i in range(chunks)]
    for copy in copies:
        copy.start()
    for copy in small:
        copy.wait()
    shape = (levels, columns)
    lane = lax.broadcasted_iota(jnp.int32, shape, 1)
    live = (lane < counts_ref[0]) | (lane >= columns - 2 * halo)
    keep = jnp.where(live & (lax.broadcasted_iota(jnp.int32, shape, 0) < depth_ref[...]), 1.0, 0.0)
    total = weights_ref[0]
    for link in range(1, links):
        total = total + weights_ref[link]
    self_ref[...] = keep * (1.0 - total)
    for link in range(links):
        live_ref[link] = keep * weights_ref[link]
    factor_columns(kappa_ref, thickness_ref, keep, carry_ref, pivot_ref, ratio_ref)

    def near(value, other):
        lanes = lax.broadcasted_iota(jnp.int32, value.shape, 1)
        return jnp.where((lanes >= columns // 4) & (lanes < 3 * columns // 4), pltpu.roll(other, columns // 2, 1), value)

    named = padded_links(neighbours_ref, 8)
    lane8 = lane[0:8]
    near_links = near(named.astype(F32), named.astype(F32)).astype(jnp.int32)
    second = (lane8 >= columns // 4) & (lane8 < 3 * columns // 4)
    first_rim = near_links < halo
    last_rim = (near_links >= columns - halo) & (near_links < columns + 2 * halo)
    hit = jnp.where(first_rim, near_links, jnp.where(last_rim, near_links - columns + 2 * halo, -1))
    hit = jnp.where((hit >= 0) & second, hit + columns // 2, hit)
    for link, matrix in enumerate(one_hot(hit, columns)[:links]):
        near_ref[link * columns : (link + 1) * columns, :] = matrix
    part8 = lane_group((8, columns), halo) % 4
    slot8 = lane8 % halo
    rim_column = jnp.where(part8 % 2 == 0, slot8, columns - halo + slot8)
    leaving = pick(named, rim_column)
    leaving = jnp.where(leaving >= columns, leaving - columns + 2 * halo + lane8 // (4 * halo) * (4 * halo), -1)
    leaving = jnp.where((part8 < 2) == (lax.broadcasted_iota(jnp.int32, (8, columns), 0) < links // 2), leaving, -1)
    matrices = one_hot(leaving, columns)
    for link in range(links // 2):
        leave_ref[link * columns : (link + 1) * columns, :] = matrices[link] + matrices[link + links // 2]

    for link in range(links):
        plane_ref[link] = near(live_ref[link], live_ref[link])
    plane_ref[links] = near(self_ref[...], self_ref[...])
    part = lane_group(shape, halo) % 4
    slot = lane % halo
    rim_column = jnp.where(part % 2 == 0, slot, columns - halo + slot)
    for index, ref in enumerate((carry_ref, pivot_ref, ratio_ref)):
        plane_ref[links + 1 + index] = jnp.where(part < 2, pick(ref[...], rim_column), 0.0)
    for link in range(links // 2):
        other = pick(live_ref[link + links // 2], rim_column)
        plane_ref[links + 4 + link] = jnp.where(part < 2, pick(live_ref[link], rim_column), other)

    def spread(value, level, wide, planes, target_ref):
        at = level // wide * 2 * wide * half + level % wide * half
        for index, plane in enumerate(planes):
            top, low = split(value * plane_ref[plane, level : level + 1, :])
            cols = slice(index * columns, (index + 1) * columns)
            target_ref[at : at + half, cols] = top
            target_ref[at + wide * half : at + (wide + 1) * half, cols] = low

    wide = levels // 4
    rows = wide * half
    part_half = lane_group((half, columns), halo) % 4
    above = None
    for index in range(levels // wide):
        own = []
        for level in range(index * wide, (index + 1) * wide):
            if level % step == 0:
                copies[level // step].wait()
            value = chunk_ref[level // step, :, level % step, :]
            field_ref[level] = value
            value = near(value[:half], value[half:])
            spread(value, level, wide, range(links), spread_ref)
            value = value * plane_ref[links, level : level + 1, :]
            own.append(jnp.where(part_half == 0, value, pltpu.roll(value, 2 * halo, 1)))
        moved = matmul_group(index, spread_ref, near_ref, rows)
        for level in range(index * wide, (index + 1) * wide):
            at = (level - index * wide) * half
            value = moved[at : at + half]
            mirror_ref[level] = value
            value = (value + own[level - index * wide]) * plane_ref[links + 2, level : level + 1, :]
            if level > 0:
                value = value - plane_ref[links + 1, level : level + 1, :] * above
            forward_ref[level] = value
            above = value

    even = lax.axis_index(AXES) % 2 == 0
    table_ref[0:8, :] = named
    table_ref[8:16, :] = rim_lanes(rim_ref, 1, halo, (8, columns))
    table_ref[16:24, :] = rim_lanes(rim_ref, 0, halo, (8, columns))

    def send(first, levels_of):
        left = pack_slots(levels_of, 2, halo)
        right = pack_slots(levels_of, 3, halo)
        for index in range(len(left)):
            at = first + index * half
            outer_ref[at : at + half, :] = jnp.where(even, left[index], right[index])
            inner_ref[at : at + half, :] = jnp.where(even, right[index], left[index])

    total_rows = levels // 4 * half
    below = None
    for index in range(levels // wide - 1, -1, -1):
        for level in range((index + 1) * wide - 1, index * wide - 1, -1):
            value = forward_ref[level]
            if below is not None:
                value = value - plane_ref[links + 3, level : level + 1, :] * below
            below = value
            value = jnp.where(part_half < 2, value, pltpu.roll(value, 2 * halo, 1))
            spread(value, level, wide, range(links + 4, links + 4 + links // 2), spread_two_ref)
        moved = matmul_group(index, spread_two_ref, leave_ref, rows)
        span = range(index * wide, (index + 1) * wide)
        send(index * wide // 4 * half, [mirror_ref[level] for level in span])
        send(total_rows + index * wide // 4 * half, [moved[i * half : (i + 1) * half] for i in range(wide)])
    planes = [carry_ref[...], pivot_ref[...], ratio_ref[...]] + [live_ref[link] for link in range(links)]
    neighbours = padded_links(neighbours_ref, levels)
    left = rim_coefficients(planes, neighbours, rim_lanes(rim_ref, 1, halo, shape), columns, halo)
    right = rim_coefficients(planes, neighbours, rim_lanes(rim_ref, 0, halo, shape), columns + halo, halo)
    outer_ref[2 * total_rows :, :] = jnp.where(even, left, right)
    inner_ref[2 * total_rows :, :] = jnp.where(even, right, left)


def block_kernel(group, table_ref, field_ref, live_ref, self_ref, carry_ref, pivot_ref, ratio_ref, moved_ref, stack_ref,
                 gram_ref, targets_ref, spread_ref, forward_ref):
    levels, vectors, columns = field_ref.shape
    links = live_ref.shape[0]
    for link, matrix in enumerate(one_hot(table_ref[0:8, :], columns)[:links]):
        targets_ref[link * columns : (link + 1) * columns, :] = matrix
    rows = group * vectors
    above = None
    for index in range(levels // group):
        for level in range(index * group, (index + 1) * group):
            spread_level(field_ref[level], level, live_ref, spread_ref, group)
            stack_terms(field_ref[level], level, stack_ref)
        own = matmul_group(index, spread_ref, targets_ref, rows)
        for level in range(index * group, (index + 1) * group):
            at = (level - index * group) * vectors
            value = own[at : at + vectors] + field_ref[level] * self_ref[level : level + 1, :]
            value = value * pivot_ref[level : level + 1, :]
            if level > 0:
                value = value - carry_ref[level : level + 1, :] * above
            forward_ref[level] = value
            above = value
    below = None
    for index in range(levels // group - 1, -1, -1):
        for level in range((index + 1) * group - 1, index * group - 1, -1):
            value = forward_ref[level]
            if below is not None:
                value = value - ratio_ref[level : level + 1, :] * below
            below = value
            forward_ref[level] = value
            spread_level(value, level, live_ref, spread_ref, group)
        own = matmul_group(index, spread_ref, targets_ref, rows)
        for level in range(index * group, (index + 1) * group):
            at = (level - index * group) * vectors
            moved_ref[level] = own[at : at + vectors] + forward_ref[level] * self_ref[level : level + 1, :]
    gram = None
    span = levels * columns // 4
    for index in range(4):
        part = stacked_products(stack_ref, stack_ref, span * index, span * (index + 1))
        gram = part if gram is None else gram + part
    gram_ref[...] = join_products(gram)


def stack_terms(value, level, stack_ref):
    vectors, columns = value.shape
    top, low = split(value)
    cols = slice(level * columns, (level + 1) * columns)
    stack_ref[0:vectors, cols] = top
    stack_ref[vectors:, cols] = low


def stacked_products(a_ref, b_ref, first, last):
    return lax.dot_general(a_ref[:, first:last], b_ref[:, first:last], NT, preferred_element_type=F32)


def join_products(products):
    half = products.shape[0] // 2
    return products[:half, :half] + (products[:half, half:] + products[half:, :half])


def second_kernel(halo, outer_ref, inner_ref, mirror_ref, stack_ref, moved_ref, live_ref,
                  self_ref, carry_ref, pivot_ref, ratio_ref, table_ref, gram_ref, image_ref, sums_ref,
                  plane_ref, target_ref, rim_field_ref, spread_ref, came_ref, forward_ref, images_ref):
    levels, vectors, columns = moved_ref.shape
    links = live_ref.shape[0]
    half = vectors // 2
    rows = levels // 4 * half
    even = lax.axis_index(AXES) % 2 == 0
    outer = outer_ref[...]
    inner = inner_ref[...]
    from_left = jnp.where(even, outer, inner)
    from_right = jnp.where(even, inner, outer)

    def parts_of(shape):
        return lane_group(shape, halo) % 4

    shape = (levels, columns)
    part = parts_of(shape)
    slot = lax.broadcasted_iota(jnp.int32, shape, 1) % halo
    lead = table_ref[8:16, :]
    trail = table_ref[16:24, :]
    own_column = jnp.concatenate([jnp.where(part[0:8] % 2 == 0, lead, trail)] * (levels // 8), axis=0)
    planes = [carry_ref[...], pivot_ref[...], ratio_ref[...]] + [live_ref[link] for link in range(links)]
    for index, plane in enumerate(planes):
        theirs = jnp.where(part == 2, pick(from_left[2 * rows :], slot + halo * index), pick(from_right[2 * rows :], slot + halo * index))
        plane_ref[index] = jnp.where(part < 2, pick(plane, own_column), theirs)
    plane_ref[len(planes)] = pick(self_ref[...], own_column)

    shape = (8, columns)
    part, slot, own_column = part[0:8], slot[0:8], own_column[0:8]
    named = pick(table_ref[0:8, :], own_column)
    from_links = slot + halo * len(planes)
    theirs = jnp.where(part == 2, pick(from_left[2 * rows : 2 * rows + 8], from_links), pick(from_right[2 * rows : 2 * rows + 8], from_links)).astype(jnp.int32)
    facing = jnp.where(part == 2, pick(lead, jnp.maximum(theirs, 0)), pick(trail, jnp.maximum(theirs, 0)))
    target = jnp.where(part < 2, jnp.where(named < columns, named, -1), jnp.where(theirs >= 0, facing, -1))
    link_row = lax.broadcasted_iota(jnp.int32, shape, 0)
    target = jnp.where(link_row == links, own_column, target)
    lane = lax.broadcasted_iota(jnp.int32, shape, 1)
    links_of = jnp.where(link_row < links, table_ref[0:8, :], lane)
    far = (links_of >= columns) & (links_of < columns + halo) & (lane >= halo)
    far = far | ((links_of >= columns + halo) & (lane < columns - halo))
    far = far | ((links_of < halo) & (lane >= 2 * halo))
    far = far | ((links_of >= columns - halo) & (links_of < columns) & (lane < columns - 2 * halo))
    far = jnp.sum(jnp.where(far, 1.0, 0.0), axis=1, keepdims=True)
    far = jnp.sum(far, axis=0, keepdims=True)
    first_half = lax.broadcasted_iota(jnp.int32, (columns, columns), 0) < 4 * halo
    for link, matrix in enumerate(one_hot(target, columns)[: links + 1]):
        at = slice(link * columns, (link + 1) * columns)
        target_ref[at, 0:columns] = jnp.where(first_half, matrix, jnp.zeros_like(matrix))
        target_ref[at, columns:] = jnp.where(first_half, jnp.zeros_like(matrix), matrix)

    half_part = parts_of((half, columns))

    def came_in(message, level, to):
        block = message[level // 4 * half : (level // 4 + 1) * half]
        turn = (to - level % 4) * halo % LANES
        return pltpu.roll(block, turn, 1) if turn else block

    above = None
    for level in range(levels):
        value = jnp.where(half_part == 0, came_in(from_left, level, 0), mirror_ref[level])
        value = jnp.where(half_part == 1, came_in(from_right, level, 1), value)
        value = value * plane_ref[1, level : level + 1, :]
        if level > 0:
            value = value - plane_ref[0, level : level + 1, :] * above
        rim_field_ref[level] = value
        above = value
    late_left = from_left[rows : 2 * rows]
    late_right = from_right[rows : 2 * rows]
    wide = levels // 4
    span = wide * half
    below = None
    for index in range(levels // wide - 1, -1, -1):
        for level in range((index + 1) * wide - 1, index * wide - 1, -1):
            value = rim_field_ref[level]
            if below is not None:
                value = value - plane_ref[2, level : level + 1, :] * below
            below = value
            at = 2 * span * index + level % wide * half
            for link in range(links + 1):
                term = value * plane_ref[3 + link, level : level + 1, :]
                if link == links:
                    term = jnp.where(half_part == 2, came_in(late_left, level, 2), term)
                    term = jnp.where(half_part == 3, came_in(late_right, level, 3), term)
                top, low = split(term)
                cols = slice(link * columns, (link + 1) * columns)
                spread_ref[at : at + half, cols] = top
                spread_ref[at + span : at + span + half, cols] = low
        both = jnp.dot(spread_ref[2 * span * index : 2 * span * (index + 1), :], target_ref[...], preferred_element_type=F32)
        came_ref[span * index : span * (index + 1), :] = both[:span] + both[span:]

    above = None
    for level in range(levels):
        rows = slice(level * half, (level + 1) * half)
        came = jnp.concatenate([came_ref[rows, :columns], came_ref[rows, columns:]], axis=0)
        value = (moved_ref[level] + came) * pivot_ref[level : level + 1, :]
        if level > 0:
            value = value - carry_ref[level : level + 1, :] * above
        forward_ref[level] = value
        above = value

    products = None
    square = jnp.zeros((vectors, columns), F32)
    below = None
    for index in range(levels // wide - 1, -1, -1):
        for level in range((index + 1) * wide - 1, index * wide - 1, -1):
            value = forward_ref[level]
            if below is not None:
                value = value - ratio_ref[level : level + 1, :] * below
            below = value
            image_ref[level] = value
            square = square + value * value
            stack_terms(value, level, images_ref)
        part = stacked_products(images_ref, stack_ref, wide * index * columns, wide * (index + 1) * columns)
        products = part if products is None else products + part
    cross = join_products(products)
    sums_ref[0:vectors, 0:vectors] = cross
    sums_ref[0:vectors, vectors : 2 * vectors] = gram_ref[...]
    norm = jnp.sum(square, axis=1, keepdims=True)
    shape = (vectors, 2 * vectors)
    eye = lax.broadcasted_iota(jnp.int32, shape, 0) == lax.broadcasted_iota(jnp.int32, shape, 1)
    norm = jnp.sum(jnp.where(eye, norm, 0.0), axis=0, keepdims=True)
    shape = (8, 2 * vectors)
    sums_ref[vectors : vectors + 8, :] = jnp.where(lax.broadcasted_iota(jnp.int32, shape, 0) == 0, norm, far)


def weigh_kernel(cells, sums_ref, more_ref, spans_ref, scale_ref, coupling_ref, direct_ref):
    vectors = coupling_ref.shape[0]
    sums = sums_ref[...] + more_ref[...]
    cross = sums[0:vectors, 0:vectors] / cells
    gram = sums[0:vectors, vectors : 2 * vectors] / cells
    coupling_ref[...] = cross.T
    shape = (vectors, vectors)
    eye = lax.broadcasted_iota(jnp.int32, shape, 0) == lax.broadcasted_iota(jnp.int32, shape, 1)
    square = sums[vectors : vectors + 1, 0:vectors] / cells
    square = jnp.sum(jnp.where(eye, square, 0.0), axis=1, keepdims=True)
    mixed = dot3(cross, gram, (((1,), (0,)), ((), ())))
    spanned = jnp.sum(cross * mixed, axis=1, keepdims=True)
    shared = 2.0 * jnp.sum(cross * cross, axis=1, keepdims=True)
    norm = square - shared + spanned
    small = norm + 1e-6 < 1e-2 * (square + shared + jnp.abs(spanned))
    scale_ref[...] = jnp.broadcast_to(1.0 / jnp.sqrt(jnp.maximum(norm, 0.0) + 1e-6), scale_ref.shape)
    far = jnp.sum(sums[vectors + 1 : vectors + 2, 0:1])
    direct_ref[0] = jnp.where(far + jnp.sum(jnp.where(small, 1.0, 0.0)) > 0.0, 1, 0)
    top, low = split(cross)
    spans_ref[...] = jnp.concatenate([jnp.concatenate([top, top], axis=1), jnp.concatenate([low, low], axis=1)], axis=0)


def last_kernel(spans_ref, scale_ref, image_ref, stack_ref, sums_ref, next_ref, coupling_ref, chunk_ref, sems):
    levels, vectors, columns = image_ref.shape
    chunks = chunk_ref.shape[0]
    step = levels // chunks
    copies = [pltpu.make_async_copy(chunk_ref.at[i], next_ref.at[:, step * i : step * (i + 1), :], sems.at[i]) for i in range(chunks)]
    copies.append(pltpu.make_async_copy(sums_ref, coupling_ref, sems.at[chunks]))
    copies[chunks].start()
    for index in range(chunks):
        cols = slice(step * index * columns, step * (index + 1) * columns)
        both = jnp.dot(spans_ref[...], stack_ref[:, cols], preferred_element_type=F32)
        spanned = both[:vectors] + both[vectors:]
        for level in range(step):
            at = level * columns
            chunk_ref[index, :, level, :] = (image_ref[step * index + level] - spanned[:, at : at + columns]) * scale_ref[...]
        copies[index].start()
    for copy in copies:
        copy.wait()


VMEM = pl.BlockSpec(memory_space=pltpu.VMEM)
SMEM = pl.BlockSpec(memory_space=pltpu.SMEM)
ANY = pl.BlockSpec(memory_space=pl.ANY)


def call(kernel, outs, out_specs, scratch, specs, *operands):
    return pl.pallas_call(
        kernel,
        out_shape=outs,
        in_specs=specs,
        out_specs=out_specs,
        scratch_shapes=scratch,
        compiler_params=pltpu.CompilerParams(vmem_limit_bytes=40 << 20),
    )(*operands)


def exchange(outer, inner):
    blocks = lax.axis_size(AXES)
    outer = lax.ppermute(outer, AXES, [(i, (i - 1) % blocks if i % 2 == 0 else (i + 1) % blocks) for i in range(blocks)])
    inner = lax.ppermute(inner, AXES, [(i, i ^ 1) for i in range(blocks)])
    return outer, inner


def almost_total(value):
    blocks = lax.axis_size(AXES)
    if blocks & (blocks - 1):
        return lax.psum(value, AXES), jnp.zeros_like(value)
    more = lax.ppermute(value, AXES, [(i, i ^ 1) for i in range(blocks)])
    distance = 2
    while distance < blocks:
        value = value + more
        more = lax.ppermute(value, AXES, [(i, i ^ distance) for i in range(blocks)])
        distance *= 2
    return value, more


def shards(basis, weights, kappa, thickness, depth, neighbours, rim_lists, counts):
    vectors, levels, columns = basis.shape
    links = weights.shape[0]
    halo = rim_lists.shape[1]
    group = 4
    rows = levels // 4 * vectors // 2
    chunks = 4

    def out(*shape, dtype=F32):
        return jax.ShapeDtypeStruct(shape, dtype)

    message = out(2 * rows + levels, LANES)
    whole = out(levels, vectors, columns)
    halved = out(levels, vectors // 2, columns)
    plane = out(levels, columns)
    forward = pltpu.VMEM((levels, vectors, columns), F32)
    half_forward = pltpu.VMEM((levels, vectors // 2, columns), F32)
    chunk = pltpu.VMEM((chunks, vectors, levels // chunks, columns), F32)
    sems = pltpu.SemaphoreType.DMA((chunks,))
    cells = levels * vectors
    table = out(24, columns, dtype=jnp.int32)
    outer, inner, mirror, field, live, self_weight, carry, pivot, ratio, table = call(
        functools.partial(edge_kernel, halo),
        (message, message, halved, whole, out(links, levels, columns), plane, plane, plane, plane, table), [VMEM] * 10,
        [pltpu.VMEM((links * columns, columns), BF16), pltpu.VMEM((links // 2 * columns, columns), BF16),
         pltpu.VMEM((cells, links * columns), BF16), pltpu.VMEM((cells, links // 2 * columns), BF16),
         half_forward, pltpu.VMEM((links + 4 + links // 2, levels, columns), F32), chunk,
         pltpu.VMEM((links, levels, columns), F32), pltpu.VMEM((levels, columns), F32), pltpu.VMEM((levels, columns), F32),
         pltpu.VMEM((1, columns), jnp.int32), pltpu.VMEM((links, columns), jnp.int32), sems, pltpu.SemaphoreType.DMA((5,))],
        [SMEM] * 2 + [ANY] * 6,
        counts, rim_lists, basis, weights, kappa, thickness, depth.reshape(1, columns), neighbours)
    outer, inner = exchange(outer, inner)
    moved, stack, gram = call(
        functools.partial(block_kernel, group),
        (whole, out(2 * vectors, levels * columns, dtype=BF16), out(vectors, vectors)), [VMEM] * 3,
        [pltpu.VMEM((links * columns, columns), BF16), pltpu.VMEM((2 * cells, links * columns), BF16), forward],
        [VMEM] * 7, table, field, live, self_weight, carry, pivot, ratio)
    image, sums = call(
        functools.partial(second_kernel, halo), (whole, out(vectors + 8, 2 * vectors)), [VMEM] * 2,
        [pltpu.VMEM((links + 4, levels, columns), F32), pltpu.VMEM(((links + 1) * columns, 2 * columns), BF16), half_forward,
         pltpu.VMEM((cells, (links + 1) * columns), BF16), pltpu.VMEM((cells // 2, 2 * columns), F32),
         forward, pltpu.VMEM((2 * vectors, levels * columns), BF16)],
        [VMEM] * 12,
        outer, inner, mirror, stack, moved, live, self_weight, carry, pivot, ratio, table, gram)
    sums, more = almost_total(sums)
    cells = float(levels * columns * lax.axis_size(AXES))
    spans, scale, coupling, direct = call(
        functools.partial(weigh_kernel, cells),
        (out(2 * vectors, 2 * vectors, dtype=BF16), out(vectors, columns), out(vectors, vectors), out(1, dtype=jnp.int32)),
        [VMEM] * 3 + [SMEM], [], [VMEM] * 2, sums, more)

    def from_sums():
        return call(last_kernel, (out(vectors, levels, columns), out(vectors, vectors)), [ANY] * 2,
                    [chunk, pltpu.SemaphoreType.DMA((chunks + 1,))], [VMEM] * 5, spans, scale, image, stack, coupling)

    def from_scratch():
        return direct_form(basis, weights, kappa, thickness, depth, neighbours, rim_lists, counts)

    return tuple(lax.cond(direct[0] > 0, from_scratch, lambda: tuple(from_sums())))


ITERS = 2


def from_behind(block, axis, distance):
    devices = range(lax.axis_size(axis))
    route = [((i - distance) % len(devices), i) for i in devices]
    return lax.ppermute(block, axis, route)


def column_factors(kappa, thickness, keep):
    levels = kappa.shape[0]
    below = jnp.concatenate([keep[1:], jnp.zeros_like(keep[:1])], axis=0)
    interface = kappa * keep * below
    lower, inv_pivot, ratio = ([], [], [])
    for level in range(levels):
        upper_term = interface[level]
        diag_term = 1.0 + upper_term / thickness[level]
        if level > 0:
            diag_term = diag_term + interface[level - 1] / thickness[level]
            low = -interface[level - 1] / thickness[level - 1]
        else:
            low = jnp.zeros_like(upper_term)
        if level < levels - 1:
            upp = -upper_term / thickness[level + 1]
        else:
            upp = jnp.zeros_like(upper_term)
        pivot = diag_term - low * ratio[level - 1] if level > 0 else diag_term
        inverse = 1.0 / pivot
        lower.append(low)
        inv_pivot.append(inverse)
        ratio.append(upp * inverse)
    return (lower, inv_pivot, ratio)


def column_solve(rhs, lower, inv_pivot, ratio):
    levels = rhs.shape[1]
    forward = []
    for level in range(levels):
        if level == 0:
            forward.append(rhs[:, 0] * inv_pivot[0])
        else:
            forward.append((rhs[:, level] - lower[level] * forward[level - 1]) * inv_pivot[level])
    result = [None] * levels
    result[levels - 1] = forward[levels - 1]
    for level in range(levels - 2, -1, -1):
        result[level] = forward[level] - ratio[level] * result[level + 1]
    return jnp.stack(result, axis=1)


def transport_back(field, weights, keep, self_weight, neighbours, rim_lists):
    columns = field.shape[2]
    halo_width = rim_lists.shape[1]
    masked = keep * field
    extended = jnp.zeros((field.shape[0], field.shape[1], columns + 2 * halo_width), jnp.float32)
    for link in range(weights.shape[0]):
        extended = extended.at[:, :, neighbours[link]].add(weights[link] * masked)
    from_right = from_behind(extended[:, :, columns : columns + halo_width], ("region", "sub"), -1)
    from_left = from_behind(extended[:, :, columns + halo_width :], ("region", "sub"), 1)
    result = self_weight * masked + extended[:, :, :columns]
    result = result.at[:, :, rim_lists[0]].add(from_right).at[:, :, rim_lists[1]].add(from_left)
    return keep * result


def direct_form(basis, weights, kappa, thickness, depth, neighbours, rim_lists, counts):
    vectors, levels, columns = basis.shape
    halo_width = rim_lists.shape[1]
    own_index = jnp.arange(columns, dtype=jnp.int32)
    live = (own_index < counts[0]) | (own_index >= columns - 2 * halo_width)
    wet = jnp.arange(levels, dtype=jnp.int32)[:, None] < depth[None, :]
    keep = (live[None, :] & wet).astype(jnp.float32)
    self_weight = 1.0 - jnp.sum(weights, axis=0)
    lower, inv_pivot, ratio = column_factors(kappa, thickness, keep)
    field = basis
    for step in range(ITERS):
        moved = transport_back(field, weights, keep, self_weight, neighbours, rim_lists)
        field = column_solve(keep * moved, lower, inv_pivot, ratio)
    cells = float(levels * columns * lax.axis_size(("region", "sub")))
    high = lax.Precision.HIGHEST
    local_cross = jnp.einsum("ilc,jlc->ij", basis, field, precision=high)
    coupling = lax.psum(local_cross, ("region", "sub")) / cells
    residual = field - jnp.einsum("ilc,ij->jlc", basis, coupling, precision=high)
    local_norms = jnp.einsum("jlc,jlc->j", residual, residual, precision=high)
    norms = lax.psum(local_norms, ("region", "sub")) / cells
    next_basis = residual / jnp.sqrt(norms + 1e-06)[:, None, None]
    return (next_basis, coupling)


def solution(mesh):
    placed = (
        P("groups", None, AXES),
        P(None, None, AXES),
        P(None, AXES),
        P(None, AXES),
        P(AXES),
        P(None, AXES),
        P(None, AXES),
        P(AXES),
    )
    return jax.shard_map(
        shards,
        mesh=mesh,
        in_specs=placed,
        out_specs=(P("groups", None, AXES), P("groups", None)),
        check_vma=False,
    )
```

```python
import functools

import jax
import jax.numpy as jnp
from jax import lax
from jax.experimental import pallas as pl
from jax.experimental.pallas import tpu as pltpu
from jax.sharding import PartitionSpec as P

AXES = ("region", "sub")
LANES = 128
F32 = jnp.float32
BF16 = jnp.bfloat16
NT = (((1,), (1,)), ((), ()))


def split(x):
    top = x.astype(BF16)
    return top, (x - top.astype(F32)).astype(BF16)


def dot3(a, b, dims):
    a_top, a_low = split(a)
    b_top, b_low = split(b)
    dot = functools.partial(lax.dot_general, dimension_numbers=dims, preferred_element_type=F32)
    return dot(a_top, b_top) + (dot(a_top, b_low) + dot(a_low, b_top))


def one_hot(hits, size):
    by_lane = hits.astype(F32).T
    lanes = by_lane.shape[0]
    column = lax.broadcasted_iota(jnp.int32, (lanes, size), 1).astype(F32)
    return [jnp.where(jnp.broadcast_to(by_lane[:, i : i + 1], (lanes, size)) == column, 1.0, 0.0).astype(BF16) for i in range(hits.shape[0])]


def spread_level(value, level, weights_ref, spread_ref, group):
    links, _, columns = weights_ref.shape
    vectors = value.shape[0]
    first = level // group * 2 * group * vectors + level % group * vectors
    second = first + group * vectors
    for link in range(links):
        top, low = split(value * weights_ref[link, level : level + 1, :])
        cols = slice(link * columns, (link + 1) * columns)
        spread_ref[first : first + vectors, cols] = top
        spread_ref[second : second + vectors, cols] = low


def matmul_group(index, spread_ref, targets_ref, rows):
    both = jnp.dot(spread_ref[2 * rows * index : 2 * rows * (index + 1), :], targets_ref[...], preferred_element_type=F32)
    return both[:rows] + both[rows:]


def factor_columns(kappa_ref, thickness_ref, keep, carry_ref, pivot_ref, ratio_ref):
    levels = keep.shape[0]
    interface = [kappa_ref[i : i + 1, :] * keep[i : i + 1] * keep[i + 1 : i + 2] for i in range(levels - 1)]
    ratio = None
    for level in range(levels):
        thick = thickness_ref[level : level + 1, :]
        pivot = jnp.ones_like(thick)
        if level < levels - 1:
            pivot = pivot + interface[level] / thick
        if level > 0:
            pivot = pivot + interface[level - 1] / thick
            low = -interface[level - 1] / thickness_ref[level - 1 : level, :]
            pivot = pivot - low * ratio
        inverse = 1.0 / pivot
        carry_ref[level : level + 1, :] = low * inverse if level > 0 else jnp.zeros_like(thick)
        pivot_ref[level : level + 1, :] = keep[level : level + 1] * inverse
        if level < levels - 1:
            ratio = -interface[level] / thickness_ref[level + 1 : level + 2, :] * inverse
            ratio_ref[level : level + 1, :] = ratio
        else:
            ratio_ref[level : level + 1, :] = jnp.zeros_like(thick)


def lane_group(shape, width):
    return lax.broadcasted_iota(jnp.int32, shape, 1) // width


def pick(plane, lanes):
    return jnp.take_along_axis(plane, lanes, axis=1, mode="promise_in_bounds")


def rim_lanes(rim_ref, row, halo, shape):
    slot = lax.broadcasted_iota(jnp.int32, shape, 1) % halo
    columns = jnp.zeros(shape, jnp.int32)
    for index in range(halo):
        columns = jnp.where(slot == index, rim_ref[row, index], columns)
    return columns


def rim_coefficients(planes, neighbours, columns, first, halo):
    group = lane_group(columns.shape, halo)
    packed = jnp.zeros(columns.shape, F32)
    for index, plane in enumerate(planes):
        packed = jnp.where(group == index, pick(plane, columns), packed)
    slot = pick(neighbours, columns) - first
    slot = jnp.where((slot >= 0) & (slot < halo), slot, -1)
    return jnp.where(group == len(planes), slot.astype(F32), packed)


def padded_links(neighbours_ref, rows):
    links, columns = neighbours_ref.shape
    padded = jnp.concatenate([neighbours_ref[...], jnp.zeros((8 - links, columns), jnp.int32)], axis=0)
    if rows > 8:
        padded = jnp.concatenate([padded, jnp.zeros((rows - 8, columns), jnp.int32)], axis=0)
    return padded


def pack_slots(levels, slot_group, halo):
    group = lane_group(levels[0].shape, halo) % 4
    packed = []
    for first in range(0, len(levels), 4):
        block = levels[first]
        for offset in range(4):
            turn = (offset - slot_group) * halo % LANES
            value = levels[first + offset]
            value = pltpu.roll(value, turn, 1) if turn else value
            block = value if offset == 0 else jnp.where(group == offset, value, block)
        packed.append(block)
    return packed


def edge_kernel(halo, counts_ref, rim_ref, basis_ref, weights_in, kappa_in, thickness_in, depth_in, neighbours_in,
                outer_ref, inner_ref, mirror_ref, field_ref, live_ref, self_ref, carry_ref, pivot_ref, ratio_ref, table_ref,
                near_ref, leave_ref, spread_ref, spread_two_ref, forward_ref, plane_ref, chunk_ref, weights_ref, kappa_ref,
                thickness_ref, depth_ref, neighbours_ref, sems, small_sems):
    small = [(weights_in, weights_ref), (kappa_in, kappa_ref), (thickness_in, thickness_ref), (depth_in, depth_ref), (neighbours_in, neighbours_ref)]
    small = [pltpu.make_async_copy(a, b, small_sems.at[i]) for i, (a, b) in enumerate(small)]
    for copy in small:
        copy.start()
    vectors, levels, columns = basis_ref.shape
    links = weights_ref.shape[0]
    half = vectors // 2
    chunks = chunk_ref.shape[0]
    step = levels // chunks
    copies = [pltpu.make_async_copy(basis_ref.at[:, step * i : step * (i + 1), :], chunk_ref.at[i], sems.at[i]) for i in range(chunks)]
    for copy in copies:
        copy.start()
    for copy in small:
        copy.wait()
    shape = (levels, columns)
    lane = lax.broadcasted_iota(jnp.int32, shape, 1)
    live = (lane < counts_ref[0]) | (lane >= columns - 2 * halo)
    keep = jnp.where(live & (lax.broadcasted_iota(jnp.int32, shape, 0) < depth_ref[...]), 1.0, 0.0)
    total = weights_ref[0]
    for link in range(1, links):
        total = total + weights_ref[link]
    self_ref[...] = keep * (1.0 - total)
    for link in range(links):
        live_ref[link] = keep * weights_ref[link]
    factor_columns(kappa_ref, thickness_ref, keep, carry_ref, pivot_ref, ratio_ref)

    def near(value, other):
        lanes = lax.broadcasted_iota(jnp.int32, value.shape, 1)
        return jnp.where((lanes >= columns // 4) & (lanes < 3 * columns // 4), pltpu.roll(other, columns // 2, 1), value)

    named = padded_links(neighbours_ref, 8)
    lane8 = lane[0:8]
    near_links = near(named.astype(F32), named.astype(F32)).astype(jnp.int32)
    second = (lane8 >= columns // 4) & (lane8 < 3 * columns // 4)
    first_rim = near_links < halo
    last_rim = (near_links >= columns - halo) & (near_links < columns + 2 * halo)
    hit = jnp.where(first_rim, near_links, jnp.where(last_rim, near_links - columns + 2 * halo, -1))
    hit = jnp.where((hit >= 0) & second, hit + columns // 2, hit)
    for link, matrix in enumerate(one_hot(hit, columns)[:links]):
        near_ref[link * columns : (link + 1) * columns, :] = matrix
    part8 = lane_group((8, columns), halo) % 4
    slot8 = lane8 % halo
    rim_column = jnp.where(part8 % 2 == 0, slot8, columns - halo + slot8)
    leaving = pick(named, rim_column)
    leaving = jnp.where(leaving >= columns, leaving - columns + 2 * halo + lane8 // (4 * halo) * (4 * halo), -1)
    leaving = jnp.where((part8 < 2) == (lax.broadcasted_iota(jnp.int32, (8, columns), 0) < links // 2), leaving, -1)
    matrices = one_hot(leaving, columns)
    for link in range(links // 2):
        leave_ref[link * columns : (link + 1) * columns, :] = matrices[link] + matrices[link + links // 2]

    for link in range(links):
        plane_ref[link] = near(live_ref[link], live_ref[link])
    plane_ref[links] = near(self_ref[...], self_ref[...])
    part = lane_group(shape, halo) % 4
    slot = lane % halo
    rim_column = jnp.where(part % 2 == 0, slot, columns - halo + slot)
    for index, ref in enumerate((carry_ref, pivot_ref, ratio_ref)):
        plane_ref[links + 1 + index] = jnp.where(part < 2, pick(ref[...], rim_column), 0.0)
    for link in range(links // 2):
        other = pick(live_ref[link + links // 2], rim_column)
        plane_ref[links + 4 + link] = jnp.where(part < 2, pick(live_ref[link], rim_column), other)

    def spread(value, level, wide, planes, target_ref):
        at = level // wide * 2 * wide * half + level % wide * half
        for index, plane in enumerate(planes):
            top, low = split(value * plane_ref[plane, level : level + 1, :])
            cols = slice(index * columns, (index + 1) * columns)
            target_ref[at : at + half, cols] = top
            target_ref[at + wide * half : at + (wide + 1) * half, cols] = low

    wide = levels // 4
    rows = wide * half
    part_half = lane_group((half, columns), halo) % 4
    even = lax.axis_index(AXES) % 2 == 0
    table_ref[0:8, :] = named
    table_ref[8:16, :] = rim_lanes(rim_ref, 1, halo, (8, columns))
    table_ref[16:24, :] = rim_lanes(rim_ref, 0, halo, (8, columns))

    def send(first, levels_of):
        left = pack_slots(levels_of, 2, halo)
        right = pack_slots(levels_of, 3, halo)
        for index in range(len(left)):
            at = first + index * half
            outer_ref[at : at + half, :] = jnp.where(even, left[index], right[index])
            inner_ref[at : at + half, :] = jnp.where(even, right[index], left[index])

    total_rows = levels // 4 * half

    def enter(index):
        own = []
        for level in range(index * wide, (index + 1) * wide):
            value = chunk_ref[level // step, :, level % step, :]
            field_ref[level] = value
            value = near(value[:half], value[half:])
            spread(value, level, wide, range(links), spread_ref)
            value = value * plane_ref[links, level : level + 1, :]
            own.append(jnp.where(part_half == 0, value, pltpu.roll(value, 2 * halo, 1)))
        return matmul_group(index, spread_ref, near_ref, rows), own

    for copy in copies:
        copy.wait()
    above = None
    ready = enter(0)
    for index in range(levels // wide):
        moved, own = ready
        if index + 1 < levels // wide:
            ready = enter(index + 1)
        slots = [moved[i * half : (i + 1) * half] for i in range(wide)]
        for level in range(index * wide, (index + 1) * wide):
            value = slots[level - index * wide]
            mirror_ref[level] = value
            value = (value + own[level - index * wide]) * plane_ref[links + 2, level : level + 1, :]
            if level > 0:
                value = value - plane_ref[links + 1, level : level + 1, :] * above
            forward_ref[level] = value
            above = value
        send(index * wide // 4 * half, slots)

    below = None
    waiting = None
    for index in range(levels // wide - 1, -1, -1):
        for level in range((index + 1) * wide - 1, index * wide - 1, -1):
            value = forward_ref[level]
            if below is not None:
                value = value - plane_ref[links + 3, level : level + 1, :] * below
            below = value
            value = jnp.where(part_half < 2, value, pltpu.roll(value, 2 * halo, 1))
            spread(value, level, wide, range(links + 4, links + 4 + links // 2), spread_two_ref)
        moved = matmul_group(index, spread_two_ref, leave_ref, rows)
        if waiting is not None:
            send(total_rows + (index + 1) * wide // 4 * half, waiting)
        waiting = [moved[i * half : (i + 1) * half] for i in range(wide)]
    send(total_rows, waiting)
    planes = [carry_ref[...], pivot_ref[...], ratio_ref[...]] + [live_ref[link] for link in range(links)]
    neighbours = padded_links(neighbours_ref, levels)
    left = rim_coefficients(planes, neighbours, rim_lanes(rim_ref, 1, halo, shape), columns, halo)
    right = rim_coefficients(planes, neighbours, rim_lanes(rim_ref, 0, halo, shape), columns + halo, halo)
    outer_ref[2 * total_rows :, :] = jnp.where(even, left, right)
    inner_ref[2 * total_rows :, :] = jnp.where(even, right, left)


def block_kernel(group, table_ref, field_ref, live_ref, self_ref, carry_ref, pivot_ref, ratio_ref, moved_ref, stack_ref,
                 gram_ref, targets_ref, spread_ref, forward_ref):
    levels, vectors, columns = field_ref.shape
    links = live_ref.shape[0]
    for link, matrix in enumerate(one_hot(table_ref[0:8, :], columns)[:links]):
        targets_ref[link * columns : (link + 1) * columns, :] = matrix
    rows = group * vectors
    above = None
    for index in range(levels // group):
        for level in range(index * group, (index + 1) * group):
            spread_level(field_ref[level], level, live_ref, spread_ref, group)
            stack_terms(field_ref[level], level, stack_ref)
        own = matmul_group(index, spread_ref, targets_ref, rows)
        for level in range(index * group, (index + 1) * group):
            at = (level - index * group) * vectors
            value = own[at : at + vectors] + field_ref[level] * self_ref[level : level + 1, :]
            value = value * pivot_ref[level : level + 1, :]
            if level > 0:
                value = value - carry_ref[level : level + 1, :] * above
            forward_ref[level] = value
            above = value
    below = None
    for index in range(levels // group - 1, -1, -1):
        for level in range((index + 1) * group - 1, index * group - 1, -1):
            value = forward_ref[level]
            if below is not None:
                value = value - ratio_ref[level : level + 1, :] * below
            below = value
            forward_ref[level] = value
            spread_level(value, level, live_ref, spread_ref, group)
        own = matmul_group(index, spread_ref, targets_ref, rows)
        for level in range(index * group, (index + 1) * group):
            at = (level - index * group) * vectors
            moved_ref[level] = own[at : at + vectors] + forward_ref[level] * self_ref[level : level + 1, :]
    gram = None
    span = levels * columns // 4
    for index in range(4):
        part = stacked_products(stack_ref, stack_ref, span * index, span * (index + 1))
        gram = part if gram is None else gram + part
    gram_ref[...] = join_products(gram)


def stack_terms(value, level, stack_ref):
    vectors, columns = value.shape
    top, low = split(value)
    cols = slice(level * columns, (level + 1) * columns)
    stack_ref[0:vectors, cols] = top
    stack_ref[vectors:, cols] = low


def stacked_products(a_ref, b_ref, first, last):
    return lax.dot_general(a_ref[:, first:last], b_ref[:, first:last], NT, preferred_element_type=F32)


def join_products(products):
    half = products.shape[0] // 2
    return products[:half, :half] + (products[:half, half:] + products[half:, :half])


def second_kernel(halo, outer_ref, inner_ref, mirror_ref, stack_ref, moved_ref, live_ref,
                  self_ref, carry_ref, pivot_ref, ratio_ref, table_ref, gram_ref, image_ref, sums_ref,
                  plane_ref, target_ref, rim_field_ref, spread_ref, came_ref, forward_ref, images_ref):
    levels, vectors, columns = moved_ref.shape
    links = live_ref.shape[0]
    half = vectors // 2
    rows = levels // 4 * half
    even = lax.axis_index(AXES) % 2 == 0
    outer = outer_ref[...]
    inner = inner_ref[...]
    from_left = jnp.where(even, outer, inner)
    from_right = jnp.where(even, inner, outer)

    def parts_of(shape):
        return lane_group(shape, halo) % 4

    shape = (levels, columns)
    part = parts_of(shape)
    slot = lax.broadcasted_iota(jnp.int32, shape, 1) % halo
    lead = table_ref[8:16, :]
    trail = table_ref[16:24, :]
    own_column = jnp.concatenate([jnp.where(part[0:8] % 2 == 0, lead, trail)] * (levels // 8), axis=0)
    planes = [carry_ref[...], pivot_ref[...], ratio_ref[...]] + [live_ref[link] for link in range(links)]
    for index, plane in enumerate(planes):
        theirs = jnp.where(part == 2, pick(from_left[2 * rows :], slot + halo * index), pick(from_right[2 * rows :], slot + halo * index))
        plane_ref[index] = jnp.where(part < 2, pick(plane, own_column), theirs)
    plane_ref[len(planes)] = pick(self_ref[...], own_column)

    shape = (8, columns)
    part, slot, own_column = part[0:8], slot[0:8], own_column[0:8]
    named = pick(table_ref[0:8, :], own_column)
    from_links = slot + halo * len(planes)
    theirs = jnp.where(part == 2, pick(from_left[2 * rows : 2 * rows + 8], from_links), pick(from_right[2 * rows : 2 * rows + 8], from_links)).astype(jnp.int32)
    facing = jnp.where(part == 2, pick(lead, jnp.maximum(theirs, 0)), pick(trail, jnp.maximum(theirs, 0)))
    target = jnp.where(part < 2, jnp.where(named < columns, named, -1), jnp.where(theirs >= 0, facing, -1))
    link_row = lax.broadcasted_iota(jnp.int32, shape, 0)
    target = jnp.where(link_row == links, own_column, target)
    lane = lax.broadcasted_iota(jnp.int32, shape, 1)
    links_of = jnp.where(link_row < links, table_ref[0:8, :], lane)
    far = (links_of >= columns) & (links_of < columns + halo) & (lane >= halo)
    far = far | ((links_of >= columns + halo) & (lane < columns - halo))
    far = far | ((links_of < halo) & (lane >= 2 * halo))
    far = far | ((links_of >= columns - halo) & (links_of < columns) & (lane < columns - 2 * halo))
    far = jnp.sum(jnp.where(far, 1.0, 0.0), axis=1, keepdims=True)
    far = jnp.sum(far, axis=0, keepdims=True)
    first_half = lax.broadcasted_iota(jnp.int32, (columns, columns), 0) < 4 * halo
    for link, matrix in enumerate(one_hot(target, columns)[: links + 1]):
        at = slice(link * columns, (link + 1) * columns)
        target_ref[at, 0:columns] = jnp.where(first_half, matrix, jnp.zeros_like(matrix))
        target_ref[at, columns:] = jnp.where(first_half, jnp.zeros_like(matrix), matrix)

    half_part = parts_of((half, columns))

    def came_in(message, level, to):
        block = message[level // 4 * half : (level // 4 + 1) * half]
        turn = (to - level % 4) * halo % LANES
        return pltpu.roll(block, turn, 1) if turn else block

    above = None
    for level in range(levels):
        value = jnp.where(half_part == 0, came_in(from_left, level, 0), mirror_ref[level])
        value = jnp.where(half_part == 1, came_in(from_right, level, 1), value)
        value = value * plane_ref[1, level : level + 1, :]
        if level > 0:
            value = value - plane_ref[0, level : level + 1, :] * above
        rim_field_ref[level] = value
        above = value
    late_left = from_left[rows : 2 * rows]
    late_right = from_right[rows : 2 * rows]
    wide = levels // 4
    span = wide * half
    below = None
    for index in range(levels // wide - 1, -1, -1):
        for level in range((index + 1) * wide - 1, index * wide - 1, -1):
            value = rim_field_ref[level]
            if below is not None:
                value = value - plane_ref[2, level : level + 1, :] * below
            below = value
            at = 2 * span * index + level % wide * half
            for link in range(links + 1):
                term = value * plane_ref[3 + link, level : level + 1, :]
                if link == links:
                    term = jnp.where(half_part == 2, came_in(late_left, level, 2), term)
                    term = jnp.where(half_part == 3, came_in(late_right, level, 3), term)
                top, low = split(term)
                cols = slice(link * columns, (link + 1) * columns)
                spread_ref[at : at + half, cols] = top
                spread_ref[at + span : at + span + half, cols] = low
        both = jnp.dot(spread_ref[2 * span * index : 2 * span * (index + 1), :], target_ref[...], preferred_element_type=F32)
        came_ref[span * index : span * (index + 1), :] = both[:span] + both[span:]

    above = None
    for level in range(levels):
        rows = slice(level * half, (level + 1) * half)
        came = jnp.concatenate([came_ref[rows, :columns], came_ref[rows, columns:]], axis=0)
        value = (moved_ref[level] + came) * pivot_ref[level : level + 1, :]
        if level > 0:
            value = value - carry_ref[level : level + 1, :] * above
        forward_ref[level] = value
        above = value

    products = None
    square = jnp.zeros((vectors, columns), F32)
    below = None
    for index in range(levels // wide - 1, -1, -1):
        for level in range((index + 1) * wide - 1, index * wide - 1, -1):
            value = forward_ref[level]
            if below is not None:
                value = value - ratio_ref[level : level + 1, :] * below
            below = value
            image_ref[level] = value
            square = square + value * value
            stack_terms(value, level, images_ref)
        part = stacked_products(images_ref, stack_ref, wide * index * columns, wide * (index + 1) * columns)
        products = part if products is None else products + part
    cross = join_products(products)
    sums_ref[0:vectors, 0:vectors] = cross
    sums_ref[0:vectors, vectors : 2 * vectors] = gram_ref[...]
    norm = jnp.sum(square, axis=1, keepdims=True)
    shape = (vectors, 2 * vectors)
    eye = lax.broadcasted_iota(jnp.int32, shape, 0) == lax.broadcasted_iota(jnp.int32, shape, 1)
    norm = jnp.sum(jnp.where(eye, norm, 0.0), axis=0, keepdims=True)
    shape = (8, 2 * vectors)
    sums_ref[vectors : vectors + 8, :] = jnp.where(lax.broadcasted_iota(jnp.int32, shape, 0) == 0, norm, far)


def weigh_kernel(cells, sums_ref, more_ref, spans_ref, scale_ref, coupling_ref, direct_ref):
    vectors = coupling_ref.shape[0]
    sums = sums_ref[...] + more_ref[...]
    cross = sums[0:vectors, 0:vectors] / cells
    gram = sums[0:vectors, vectors : 2 * vectors] / cells
    coupling_ref[...] = cross.T
    shape = (vectors, vectors)
    eye = lax.broadcasted_iota(jnp.int32, shape, 0) == lax.broadcasted_iota(jnp.int32, shape, 1)
    square = sums[vectors : vectors + 1, 0:vectors] / cells
    square = jnp.sum(jnp.where(eye, square, 0.0), axis=1, keepdims=True)
    mixed = dot3(cross, gram, (((1,), (0,)), ((), ())))
    spanned = jnp.sum(cross * mixed, axis=1, keepdims=True)
    shared = 2.0 * jnp.sum(cross * cross, axis=1, keepdims=True)
    norm = square - shared + spanned
    small = norm + 1e-6 < 1e-2 * (square + shared + jnp.abs(spanned))
    scale_ref[...] = jnp.broadcast_to(1.0 / jnp.sqrt(jnp.maximum(norm, 0.0) + 1e-6), scale_ref.shape)
    far = jnp.sum(sums[vectors + 1 : vectors + 2, 0:1])
    direct_ref[0] = jnp.where(far + jnp.sum(jnp.where(small, 1.0, 0.0)) > 0.0, 1, 0)
    top, low = split(cross)
    spans_ref[...] = jnp.concatenate([jnp.concatenate([top, top], axis=1), jnp.concatenate([low, low], axis=1)], axis=0)


def last_kernel(spans_ref, scale_ref, image_ref, stack_ref, sums_ref, next_ref, coupling_ref, chunk_ref, sems):
    levels, vectors, columns = image_ref.shape
    chunks = chunk_ref.shape[0]
    step = levels // chunks
    copies = [pltpu.make_async_copy(chunk_ref.at[i], next_ref.at[:, step * i : step * (i + 1), :], sems.at[i]) for i in range(chunks)]
    copies.append(pltpu.make_async_copy(sums_ref, coupling_ref, sems.at[chunks]))
    copies[chunks].start()
    def spanned_by(index):
        cols = slice(step * index * columns, step * (index + 1) * columns)
        both = jnp.dot(spans_ref[...], stack_ref[:, cols], preferred_element_type=F32)
        return both[:vectors] + both[vectors:]

    ready = spanned_by(0)
    for index in range(chunks):
        spanned = ready
        if index + 1 < chunks:
            ready = spanned_by(index + 1)
        for level in range(step):
            at = level * columns
            chunk_ref[index, :, level, :] = (image_ref[step * index + level] - spanned[:, at : at + columns]) * scale_ref[...]
        copies[index].start()
    for copy in copies:
        copy.wait()


VMEM = pl.BlockSpec(memory_space=pltpu.VMEM)
SMEM = pl.BlockSpec(memory_space=pltpu.SMEM)
ANY = pl.BlockSpec(memory_space=pl.ANY)


def call(kernel, outs, out_specs, scratch, specs, *operands):
    return pl.pallas_call(
        kernel,
        out_shape=outs,
        in_specs=specs,
        out_specs=out_specs,
        scratch_shapes=scratch,
        compiler_params=pltpu.CompilerParams(vmem_limit_bytes=40 << 20),
    )(*operands)


def exchange(outer, inner):
    blocks = lax.axis_size(AXES)
    outer = lax.ppermute(outer, AXES, [(i, (i - 1) % blocks if i % 2 == 0 else (i + 1) % blocks) for i in range(blocks)])
    inner = lax.ppermute(inner, AXES, [(i, i ^ 1) for i in range(blocks)])
    return outer, inner


def almost_total(value):
    blocks = lax.axis_size(AXES)
    if blocks & (blocks - 1):
        return lax.psum(value, AXES), jnp.zeros_like(value)
    more = lax.ppermute(value, AXES, [(i, i ^ 1) for i in range(blocks)])
    distance = 2
    while distance < blocks:
        value = value + more
        more = lax.ppermute(value, AXES, [(i, i ^ distance) for i in range(blocks)])
        distance *= 2
    return value, more


def shards(basis, weights, kappa, thickness, depth, neighbours, rim_lists, counts):
    vectors, levels, columns = basis.shape
    links = weights.shape[0]
    halo = rim_lists.shape[1]
    group = 4
    rows = levels // 4 * vectors // 2
    chunks = 4

    def out(*shape, dtype=F32):
        return jax.ShapeDtypeStruct(shape, dtype)

    message = out(2 * rows + levels, LANES)
    whole = out(levels, vectors, columns)
    halved = out(levels, vectors // 2, columns)
    plane = out(levels, columns)
    forward = pltpu.VMEM((levels, vectors, columns), F32)
    half_forward = pltpu.VMEM((levels, vectors // 2, columns), F32)
    chunk = pltpu.VMEM((chunks, vectors, levels // chunks, columns), F32)
    sems = pltpu.SemaphoreType.DMA((chunks,))
    cells = levels * vectors
    table = out(24, columns, dtype=jnp.int32)
    outer, inner, mirror, field, live, self_weight, carry, pivot, ratio, table = call(
        functools.partial(edge_kernel, halo),
        (message, message, halved, whole, out(links, levels, columns), plane, plane, plane, plane, table), [VMEM] * 10,
        [pltpu.VMEM((links * columns, columns), BF16), pltpu.VMEM((links // 2 * columns, columns), BF16),
         pltpu.VMEM((cells, links * columns), BF16), pltpu.VMEM((cells, links // 2 * columns), BF16),
         half_forward, pltpu.VMEM((links + 4 + links // 2, levels, columns), F32), chunk,
         pltpu.VMEM((links, levels, columns), F32), pltpu.VMEM((levels, columns), F32), pltpu.VMEM((levels, columns), F32),
         pltpu.VMEM((1, columns), jnp.int32), pltpu.VMEM((links, columns), jnp.int32), sems, pltpu.SemaphoreType.DMA((5,))],
        [SMEM] * 2 + [ANY] * 6,
        counts, rim_lists, basis, weights, kappa, thickness, depth.reshape(1, columns), neighbours)
    outer, inner = exchange(outer, inner)
    moved, stack, gram = call(
        functools.partial(block_kernel, group),
        (whole, out(2 * vectors, levels * columns, dtype=BF16), out(vectors, vectors)), [VMEM] * 3,
        [pltpu.VMEM((links * columns, columns), BF16), pltpu.VMEM((2 * cells, links * columns), BF16), forward],
        [VMEM] * 7, table, field, live, self_weight, carry, pivot, ratio)
    image, sums = call(
        functools.partial(second_kernel, halo), (whole, out(vectors + 8, 2 * vectors)), [VMEM] * 2,
        [pltpu.VMEM((links + 4, levels, columns), F32), pltpu.VMEM(((links + 1) * columns, 2 * columns), BF16), half_forward,
         pltpu.VMEM((cells, (links + 1) * columns), BF16), pltpu.VMEM((cells // 2, 2 * columns), F32),
         forward, pltpu.VMEM((2 * vectors, levels * columns), BF16)],
        [VMEM] * 12,
        outer, inner, mirror, stack, moved, live, self_weight, carry, pivot, ratio, table, gram)
    sums, more = almost_total(sums)
    cells = float(levels * columns * lax.axis_size(AXES))
    spans, scale, coupling, direct = call(
        functools.partial(weigh_kernel, cells),
        (out(2 * vectors, 2 * vectors, dtype=BF16), out(vectors, columns), out(vectors, vectors), out(1, dtype=jnp.int32)),
        [VMEM] * 3 + [SMEM], [], [VMEM] * 2, sums, more)

    def from_sums():
        return call(last_kernel, (out(vectors, levels, columns), out(vectors, vectors)), [ANY] * 2,
                    [chunk, pltpu.SemaphoreType.DMA((chunks + 1,))], [VMEM] * 5, spans, scale, image, stack, coupling)

    def from_scratch():
        return direct_form(basis, weights, kappa, thickness, depth, neighbours, rim_lists, counts)

    return tuple(lax.cond(direct[0] > 0, from_scratch, lambda: tuple(from_sums())))


ITERS = 2


def from_behind(block, axis, distance):
    devices = range(lax.axis_size(axis))
    route = [((i - distance) % len(devices), i) for i in devices]
    return lax.ppermute(block, axis, route)


def column_factors(kappa, thickness, keep):
    levels = kappa.shape[0]
    below = jnp.concatenate([keep[1:], jnp.zeros_like(keep[:1])], axis=0)
    interface = kappa * keep * below
    lower, inv_pivot, ratio = ([], [], [])
    for level in range(levels):
        upper_term = interface[level]
        diag_term = 1.0 + upper_term / thickness[level]
        if level > 0:
            diag_term = diag_term + interface[level - 1] / thickness[level]
            low = -interface[level - 1] / thickness[level - 1]
        else:
            low = jnp.zeros_like(upper_term)
        if level < levels - 1:
            upp = -upper_term / thickness[level + 1]
        else:
            upp = jnp.zeros_like(upper_term)
        pivot = diag_term - low * ratio[level - 1] if level > 0 else diag_term
        inverse = 1.0 / pivot
        lower.append(low)
        inv_pivot.append(inverse)
        ratio.append(upp * inverse)
    return (lower, inv_pivot, ratio)


def column_solve(rhs, lower, inv_pivot, ratio):
    levels = rhs.shape[1]
    forward = []
    for level in range(levels):
        if level == 0:
            forward.append(rhs[:, 0] * inv_pivot[0])
        else:
            forward.append((rhs[:, level] - lower[level] * forward[level - 1]) * inv_pivot[level])
    result = [None] * levels
    result[levels - 1] = forward[levels - 1]
    for level in range(levels - 2, -1, -1):
        result[level] = forward[level] - ratio[level] * result[level + 1]
    return jnp.stack(result, axis=1)


def transport_back(field, weights, keep, self_weight, neighbours, rim_lists):
    columns = field.shape[2]
    halo_width = rim_lists.shape[1]
    masked = keep * field
    extended = jnp.zeros((field.shape[0], field.shape[1], columns + 2 * halo_width), jnp.float32)
    for link in range(weights.shape[0]):
        extended = extended.at[:, :, neighbours[link]].add(weights[link] * masked)
    from_right = from_behind(extended[:, :, columns : columns + halo_width], ("region", "sub"), -1)
    from_left = from_behind(extended[:, :, columns + halo_width :], ("region", "sub"), 1)
    result = self_weight * masked + extended[:, :, :columns]
    result = result.at[:, :, rim_lists[0]].add(from_right).at[:, :, rim_lists[1]].add(from_left)
    return keep * result


def direct_form(basis, weights, kappa, thickness, depth, neighbours, rim_lists, counts):
    vectors, levels, columns = basis.shape
    halo_width = rim_lists.shape[1]
    own_index = jnp.arange(columns, dtype=jnp.int32)
    live = (own_index < counts[0]) | (own_index >= columns - 2 * halo_width)
    wet = jnp.arange(levels, dtype=jnp.int32)[:, None] < depth[None, :]
    keep = (live[None, :] & wet).astype(jnp.float32)
    self_weight = 1.0 - jnp.sum(weights, axis=0)
    lower, inv_pivot, ratio = column_factors(kappa, thickness, keep)
    field = basis
    for step in range(ITERS):
        moved = transport_back(field, weights, keep, self_weight, neighbours, rim_lists)
        field = column_solve(keep * moved, lower, inv_pivot, ratio)
    cells = float(levels * columns * lax.axis_size(("region", "sub")))
    high = lax.Precision.HIGHEST
    local_cross = jnp.einsum("ilc,jlc->ij", basis, field, precision=high)
    coupling = lax.psum(local_cross, ("region", "sub")) / cells
    residual = field - jnp.einsum("ilc,ij->jlc", basis, coupling, precision=high)
    local_norms = jnp.einsum("jlc,jlc->j", residual, residual, precision=high)
    norms = lax.psum(local_norms, ("region", "sub")) / cells
    next_basis = residual / jnp.sqrt(norms + 1e-06)[:, None, None]
    return (next_basis, coupling)


def solution(mesh):
    placed = (
        P("groups", None, AXES),
        P(None, None, AXES),
        P(None, AXES),
        P(None, AXES),
        P(AXES),
        P(None, AXES),
        P(None, AXES),
        P(AXES),
    )
    return jax.shard_map(
        shards,
        mesh=mesh,
        in_specs=placed,
        out_specs=(P("groups", None, AXES), P("groups", None)),
        check_vma=False,
    )
```

```python
import functools

import jax
import jax.numpy as jnp
from jax import lax
from jax.experimental import pallas as pl
from jax.experimental.pallas import tpu as pltpu
from jax.sharding import PartitionSpec as P

AXES = ("region", "sub")
LANES = 128
PIECES = ((8, 0), (4, 8))
REACH = 12
SPAN = 16
F32 = jnp.float32
BF16 = jnp.bfloat16
NT = (((1,), (1,)), ((), ()))


def split(x):
    top = x.astype(BF16)
    return top, (x - top.astype(F32)).astype(BF16)


def dot3(a, b, dims):
    a_top, a_low = split(a)
    b_top, b_low = split(b)
    dot = functools.partial(lax.dot_general, dimension_numbers=dims, preferred_element_type=F32)
    return dot(a_top, b_top) + (dot(a_top, b_low) + dot(a_low, b_top))


def one_hot(hits, size):
    by_lane = hits.astype(F32).T
    lanes = by_lane.shape[0]
    column = lax.broadcasted_iota(jnp.int32, (lanes, size), 1).astype(F32)
    return [jnp.where(jnp.broadcast_to(by_lane[:, i : i + 1], (lanes, size)) == column, 1.0, 0.0).astype(BF16) for i in range(hits.shape[0])]


def matmul_group(index, spread_ref, targets_ref, rows):
    both = jnp.dot(spread_ref[2 * rows * index : 2 * rows * (index + 1), :], targets_ref[...], preferred_element_type=F32)
    return both[:rows] + both[rows:]


def factor_columns(kappa_ref, thickness_ref, keep, carry_ref, pivot_ref, ratio_ref):
    levels = keep.shape[0]
    interface = [kappa_ref[i : i + 1, :] * keep[i : i + 1] * keep[i + 1 : i + 2] for i in range(levels - 1)]
    ratio = None
    for level in range(levels):
        thick = thickness_ref[level : level + 1, :]
        pivot = jnp.ones_like(thick)
        if level < levels - 1:
            pivot = pivot + interface[level] / thick
        if level > 0:
            pivot = pivot + interface[level - 1] / thick
            low = -interface[level - 1] / thickness_ref[level - 1 : level, :]
            pivot = pivot - low * ratio
        inverse = 1.0 / pivot
        carry_ref[level : level + 1, :] = low * inverse if level > 0 else jnp.zeros_like(thick)
        pivot_ref[level : level + 1, :] = keep[level : level + 1] * inverse
        if level < levels - 1:
            ratio = -interface[level] / thickness_ref[level + 1 : level + 2, :] * inverse
            ratio_ref[level : level + 1, :] = ratio
        else:
            ratio_ref[level : level + 1, :] = jnp.zeros_like(thick)


def lane_group(shape, width):
    return lax.broadcasted_iota(jnp.int32, shape, 1) // width


def pick(plane, lanes):
    return jnp.take_along_axis(plane, lanes, axis=1, mode="promise_in_bounds")


def rim_lanes(rim_ref, row, halo, shape):
    slot = lax.broadcasted_iota(jnp.int32, shape, 1) % halo
    columns = jnp.zeros(shape, jnp.int32)
    for index in range(halo):
        columns = jnp.where(slot == index, rim_ref[row, index], columns)
    return columns


def rim_coefficients(planes, neighbours, columns, first, halo):
    group = lane_group(columns.shape, halo)
    packed = jnp.zeros(columns.shape, F32)
    for index, plane in enumerate(planes):
        packed = jnp.where(group == index, pick(plane, columns), packed)
    slot = pick(neighbours, columns) - first
    slot = jnp.where((slot >= 0) & (slot < halo), slot, -1)
    return jnp.where(group == len(planes), slot.astype(F32), packed)


def padded_links(neighbours_ref, rows):
    links, columns = neighbours_ref.shape
    padded = jnp.concatenate([neighbours_ref[...], jnp.zeros((8 - links, columns), jnp.int32)], axis=0)
    if rows > 8:
        padded = jnp.concatenate([padded, jnp.zeros((rows - 8, columns), jnp.int32)], axis=0)
    return padded


PLACES = (
    ((32, 40, 0, 8, 48, 56, 16, 24), (48, 56, 16, 24, 32, 40, 0, 8)),
    ((40, 44, 32, 36, 8, 12, 0, 4, 56, 60, 48, 52, 24, 28, 16, 20), (56, 60, 48, 52, 24, 28, 16, 20, 40, 44, 32, 36, 8, 12, 0, 4)),
)


def pack_slots(levels):
    lane = lax.broadcasted_iota(jnp.int32, levels[0].shape, 1)

    def pair(blocks, mask, turn):
        return [jnp.where(mask, a, pltpu.roll(b, turn % LANES, 1)) for a, b in zip(blocks[::2], blocks[1::2])]

    upper = lane % 64 >= 32
    first_of_two = lane // 16 % 2 == 0
    eights = pair(pair(levels, lane // 8 % 2 == 0, 8), upper, -32)
    fours = pair(pair(pair(levels, lane // 4 % 2 == 0, 4), lane // 8 % 2 == 1, -8), upper, -32)
    blocks = eights + fours
    return pair(blocks, first_of_two, 16), pair(blocks, ~first_of_two, -16)


def unpack_slots(message, level, side, slot_group, halo, half):
    base = level // SPAN * 3 * half
    pieces = []
    for (width, start), places in zip(PIECES, PLACES):
        fit = LANES // 2 // width
        at = base + level % SPAN // fit * half
        turn = (slot_group * halo + start - places[side][level % fit]) % LANES
        block = message[at : at + half]
        pieces.append(pltpu.roll(block, turn, 1) if turn else block)
        base += SPAN // fit * half
    return pieces


def edge_kernel(halo, counts_ref, rim_ref, basis_ref, weights_in, kappa_in, thickness_in, depth_in, neighbours_in,
                outer_ref, inner_ref, mirror_ref, field_ref, live_ref, self_ref, carry_ref, pivot_ref, ratio_ref, table_ref,
                near_ref, leave_ref, spread_ref, spread_two_ref, forward_ref, plane_ref, chunk_ref, weights_ref, kappa_ref,
                thickness_ref, depth_ref, neighbours_ref, sems, small_sems):
    small = [(weights_in, weights_ref), (kappa_in, kappa_ref), (thickness_in, thickness_ref), (depth_in, depth_ref), (neighbours_in, neighbours_ref)]
    small = [pltpu.make_async_copy(a, b, small_sems.at[i]) for i, (a, b) in enumerate(small)]
    for copy in small:
        copy.start()
    vectors, levels, columns = basis_ref.shape
    links = weights_ref.shape[0]
    half = vectors // 2
    chunks = chunk_ref.shape[0]
    step = levels // chunks
    copies = [pltpu.make_async_copy(basis_ref.at[:, step * i : step * (i + 1), :], chunk_ref.at[i], sems.at[i]) for i in range(chunks)]
    for copy in copies:
        copy.start()
    for copy in small:
        copy.wait()
    shape = (levels, columns)
    lane = lax.broadcasted_iota(jnp.int32, shape, 1)
    live = (lane < counts_ref[0]) | (lane >= columns - 2 * halo)
    keep = jnp.where(live & (lax.broadcasted_iota(jnp.int32, shape, 0) < depth_ref[...]), 1.0, 0.0)
    total = weights_ref[0]
    for link in range(1, links):
        total = total + weights_ref[link]
    self_ref[...] = keep * (1.0 - total)
    for link in range(links):
        live_ref[link] = keep * weights_ref[link]
    factor_columns(kappa_ref, thickness_ref, keep, carry_ref, pivot_ref, ratio_ref)

    def near(value, other):
        lanes = lax.broadcasted_iota(jnp.int32, value.shape, 1)
        return jnp.where((lanes >= columns // 4) & (lanes < 3 * columns // 4), pltpu.roll(other, columns // 2, 1), value)

    named = padded_links(neighbours_ref, 8)
    lane8 = lane[0:8]
    near_links = near(named.astype(F32), named.astype(F32)).astype(jnp.int32)
    second = (lane8 >= columns // 4) & (lane8 < 3 * columns // 4)
    first_rim = near_links < halo
    last_rim = (near_links >= columns - halo) & (near_links < columns + 2 * halo)
    hit = jnp.where(first_rim, near_links, jnp.where(last_rim, near_links - columns + 2 * halo, -1))
    hit = jnp.where((hit >= 0) & second, hit + columns // 2, hit)
    for link, matrix in enumerate(one_hot(hit, columns)[:links]):
        near_ref[link * columns : (link + 1) * columns, :] = matrix
    part8 = lane_group((8, columns), halo) % 4
    slot8 = lane8 % halo
    rim_column = jnp.where(part8 % 2 == 0, slot8, columns - halo + slot8)
    leaving = pick(named, rim_column)
    leaving = jnp.where(leaving >= columns, leaving - columns + 2 * halo + lane8 // (4 * halo) * (4 * halo), -1)
    leaving = jnp.where((part8 < 2) == (lax.broadcasted_iota(jnp.int32, (8, columns), 0) < links // 2), leaving, -1)
    matrices = one_hot(leaving, columns)
    for link in range(links // 2):
        leave_ref[link * columns : (link + 1) * columns, :] = matrices[link] + matrices[link + links // 2]

    for link in range(links):
        plane_ref[link] = near(live_ref[link], live_ref[link])
    plane_ref[links] = near(self_ref[...], self_ref[...])
    part = lane_group(shape, halo) % 4
    slot = lane % halo
    rim_column = jnp.where(part % 2 == 0, slot, columns - halo + slot)
    for index, ref in enumerate((carry_ref, pivot_ref, ratio_ref)):
        plane_ref[links + 1 + index] = jnp.where(part < 2, pick(ref[...], rim_column), 0.0)
    for link in range(links // 2):
        other = pick(live_ref[link + links // 2], rim_column)
        plane_ref[links + 4 + link] = jnp.where(part < 2, pick(live_ref[link], rim_column), other)

    def spread(value, level, wide, planes, target_ref):
        at = level // wide * 2 * wide * half + level % wide * half
        for index, plane in enumerate(planes):
            top, low = split(value * plane_ref[plane, level : level + 1, :])
            cols = slice(index * columns, (index + 1) * columns)
            target_ref[at : at + half, cols] = top
            target_ref[at + wide * half : at + (wide + 1) * half, cols] = low

    wide = levels // 4
    rows = wide * half
    part_half = lane_group((half, columns), halo) % 4
    even = lax.axis_index(AXES) % 2 == 0
    table_ref[0:8, :] = named
    table_ref[8:16, :] = rim_lanes(rim_ref, 1, halo, (8, columns))
    table_ref[16:24, :] = rim_lanes(rim_ref, 0, halo, (8, columns))

    total_rows = levels // SPAN * 3 * half

    def send(first, levels_of):
        left, right = pack_slots(levels_of)
        for index in range(len(left)):
            at = first + index * half
            outer_ref[at : at + half, :] = jnp.where(even, left[index], right[index])
            inner_ref[at : at + half, :] = jnp.where(even, right[index], left[index])

    def enter(index):
        own = []
        for level in range(index * wide, (index + 1) * wide):
            value = chunk_ref[level // step, :, level % step, :]
            field_ref[level] = value
            value = near(value[:half], value[half:])
            spread(value, level, wide, range(links), spread_ref)
            value = value * plane_ref[links, level : level + 1, :]
            own.append(jnp.where(part_half == 0, value, pltpu.roll(value, 2 * halo, 1)))
        return matmul_group(index, spread_ref, near_ref, rows), own

    for copy in copies:
        copy.wait()
    above = None
    ready = enter(0)
    for index in range(levels // wide):
        moved, own = ready
        if index + 1 < levels // wide:
            ready = enter(index + 1)
        slots = [moved[i * half : (i + 1) * half] for i in range(wide)]
        for level in range(index * wide, (index + 1) * wide):
            value = slots[level - index * wide]
            mirror_ref[level] = value
            value = (value + own[level - index * wide]) * plane_ref[links + 2, level : level + 1, :]
            if level > 0:
                value = value - plane_ref[links + 1, level : level + 1, :] * above
            forward_ref[level] = value
            above = value
        if (index + 1) * wide % SPAN == 0:
            last = (index + 1) * wide
            send((last // SPAN - 1) * 3 * half, [mirror_ref[level] for level in range(last - SPAN, last)])

    below = None
    for index in range(levels // wide - 1, -1, -1):
        span = range(index * wide, (index + 1) * wide)
        for level in reversed(span):
            value = forward_ref[level]
            if below is not None:
                value = value - plane_ref[links + 3, level : level + 1, :] * below
            below = value
            value = jnp.where(part_half < 2, value, pltpu.roll(value, 2 * halo, 1))
            spread(value, level, wide, range(links + 4, links + 4 + links // 2), spread_two_ref)
        moved = matmul_group(index, spread_two_ref, leave_ref, rows)
        for level in span:
            forward_ref[level] = moved[(level - index * wide) * half : (level - index * wide + 1) * half]
        if index * wide % SPAN == 0:
            first = index * wide
            send(total_rows + first // SPAN * 3 * half, [forward_ref[level] for level in range(first, first + SPAN)])
    planes = [carry_ref[...], pivot_ref[...], ratio_ref[...]] + [live_ref[link] for link in range(links)]
    neighbours = padded_links(neighbours_ref, levels)
    left = rim_coefficients(planes, neighbours, rim_lanes(rim_ref, 1, halo, shape), columns, halo)
    right = rim_coefficients(planes, neighbours, rim_lanes(rim_ref, 0, halo, shape), columns + halo, halo)
    outer_ref[2 * total_rows :, :] = jnp.where(even, left, right)
    inner_ref[2 * total_rows :, :] = jnp.where(even, right, left)


def block_kernel(table_ref, field_ref, live_ref, self_ref, carry_ref, pivot_ref, ratio_ref, moved_ref, stack_ref, gram_ref,
                 matrix_ref, forward_ref):
    levels, vectors, columns = field_ref.shape
    links = live_ref.shape[0]
    row = lax.broadcasted_iota(jnp.int32, (columns, columns), 0)
    own = row == lax.broadcasted_iota(jnp.int32, (columns, columns), 1)

    def move(terms, level):
        both = lax.dot_general(terms, matrix_ref[level], NT, preferred_element_type=F32)
        both = both[:, :columns] + both[:, columns:]
        return both[:vectors] + both[vectors:]

    above = None
    for level in range(levels):
        matrix = jnp.where(own, self_ref[level : level + 1, :], 0.0)
        for link in range(links):
            matrix = matrix + jnp.where(table_ref[link : link + 1, :] == row, live_ref[link, level : level + 1, :], 0.0)
        matrix_ref[level, 0:columns, :], matrix_ref[level, columns:, :] = split(matrix)
        stack_terms(field_ref[level], level, stack_ref)
        value = move(stack_ref[:, level * columns : (level + 1) * columns], level) * pivot_ref[level : level + 1, :]
        if level > 0:
            value = value - carry_ref[level : level + 1, :] * above
        forward_ref[level] = value
        above = value
    below = None
    for level in range(levels - 1, -1, -1):
        value = forward_ref[level]
        if below is not None:
            value = value - ratio_ref[level : level + 1, :] * below
        below = value
        moved_ref[level] = move(jnp.concatenate(split(value), axis=0), level)
    gram = None
    span = levels * columns // 4
    for index in range(4):
        part = stacked_products(stack_ref, stack_ref, span * index, span * (index + 1))
        gram = part if gram is None else gram + part
    gram_ref[...] = join_products(gram)


def stack_terms(value, level, stack_ref):
    vectors, columns = value.shape
    top, low = split(value)
    cols = slice(level * columns, (level + 1) * columns)
    stack_ref[0:vectors, cols] = top
    stack_ref[vectors:, cols] = low


def stacked_products(a_ref, b_ref, first, last):
    return lax.dot_general(a_ref[:, first:last], b_ref[:, first:last], NT, preferred_element_type=F32)


def join_products(products):
    half = products.shape[0] // 2
    return products[:half, :half] + (products[:half, half:] + products[half:, :half])


def second_kernel(halo, outer_ref, inner_ref, mirror_ref, stack_ref, moved_ref, live_ref,
                  self_ref, carry_ref, pivot_ref, ratio_ref, table_ref, gram_ref, image_ref, sums_ref,
                  plane_ref, target_ref, rim_field_ref, spread_ref, came_ref, forward_ref, images_ref):
    levels, vectors, columns = moved_ref.shape
    links = live_ref.shape[0]
    half = vectors // 2
    rows = levels // SPAN * 3 * half
    even = lax.axis_index(AXES) % 2 == 0
    outer = outer_ref[...]
    inner = inner_ref[...]
    from_left = jnp.where(even, outer, inner)
    from_right = jnp.where(even, inner, outer)

    def parts_of(shape):
        return lane_group(shape, halo) % 4

    shape = (levels, columns)
    part = parts_of(shape)
    slot = lax.broadcasted_iota(jnp.int32, shape, 1) % halo
    lead = table_ref[8:16, :]
    trail = table_ref[16:24, :]
    own_column = jnp.concatenate([jnp.where(part[0:8] % 2 == 0, lead, trail)] * (levels // 8), axis=0)
    planes = [carry_ref[...], pivot_ref[...], ratio_ref[...]] + [live_ref[link] for link in range(links)]
    for index, plane in enumerate(planes):
        theirs = jnp.where(part == 2, pick(from_left[2 * rows :], slot + halo * index), pick(from_right[2 * rows :], slot + halo * index))
        plane_ref[index] = jnp.where(part < 2, pick(plane, own_column), theirs)
    plane_ref[len(planes)] = pick(self_ref[...], own_column)
    plane_ref[1] = jnp.where(slot < REACH, plane_ref[1], 0.0)

    shape = (8, columns)
    part, slot, own_column = part[0:8], slot[0:8], own_column[0:8]
    named = pick(table_ref[0:8, :], own_column)
    from_links = slot + halo * len(planes)
    theirs = jnp.where(part == 2, pick(from_left[2 * rows : 2 * rows + 8], from_links), pick(from_right[2 * rows : 2 * rows + 8], from_links)).astype(jnp.int32)
    facing = jnp.where(part == 2, pick(lead, jnp.maximum(theirs, 0)), pick(trail, jnp.maximum(theirs, 0)))
    target = jnp.where(part < 2, jnp.where(named < columns, named, -1), jnp.where(theirs >= 0, facing, -1))
    link_row = lax.broadcasted_iota(jnp.int32, shape, 0)
    target = jnp.where(link_row == links, jnp.where((part < 2) | (slot < REACH), own_column, -1), target)
    lane = lax.broadcasted_iota(jnp.int32, shape, 1)
    links_of = jnp.where(link_row < links, table_ref[0:8, :], lane)
    far = (links_of >= columns) & (links_of < columns + halo) & (lane >= halo)
    far = far | ((links_of >= columns + halo) & (lane < columns - halo))
    far = far | ((links_of >= columns) & ((links_of - columns) % halo >= REACH))
    far = far | ((links_of < halo) & (lane >= 2 * halo))
    far = far | ((links_of >= columns - halo) & (links_of < columns) & (lane < columns - 2 * halo))
    far = jnp.sum(jnp.where(far, 1.0, 0.0), axis=1, keepdims=True)
    far = jnp.sum(far, axis=0, keepdims=True)
    first_half = lax.broadcasted_iota(jnp.int32, (columns, columns), 0) < 4 * halo
    for link, matrix in enumerate(one_hot(target, columns)[: links + 1]):
        at = slice(link * columns, (link + 1) * columns)
        target_ref[at, 0:columns] = jnp.where(first_half, matrix, jnp.zeros_like(matrix))
        target_ref[at, columns:] = jnp.where(first_half, jnp.zeros_like(matrix), matrix)

    half_part = parts_of((half, columns))

    head = lax.broadcasted_iota(jnp.int32, (half, columns), 1) % halo < PIECES[1][1]

    def put(value, message, level, side, to):
        first, second = unpack_slots(message, level, side, to, halo, half)
        return jnp.where(half_part == to, jnp.where(head, first, second), value)

    above = None
    for level in range(levels):
        value = put(put(mirror_ref[level], from_left, level, 1, 0), from_right, level, 0, 1)
        value = value * plane_ref[1, level : level + 1, :]
        if level > 0:
            value = value - plane_ref[0, level : level + 1, :] * above
        rim_field_ref[level] = value
        above = value
    late_left = from_left[rows : 2 * rows]
    late_right = from_right[rows : 2 * rows]
    wide = levels // 4
    span = wide * half
    below = None
    for index in range(levels // wide - 1, -1, -1):
        for level in range((index + 1) * wide - 1, index * wide - 1, -1):
            value = rim_field_ref[level]
            if below is not None:
                value = value - plane_ref[2, level : level + 1, :] * below
            below = value
            at = 2 * span * index + level % wide * half
            for link in range(links + 1):
                term = value * plane_ref[3 + link, level : level + 1, :]
                if link == links:
                    term = put(put(term, late_left, level, 1, 2), late_right, level, 0, 3)
                top, low = split(term)
                cols = slice(link * columns, (link + 1) * columns)
                spread_ref[at : at + half, cols] = top
                spread_ref[at + span : at + span + half, cols] = low
        both = jnp.dot(spread_ref[2 * span * index : 2 * span * (index + 1), :], target_ref[...], preferred_element_type=F32)
        came_ref[span * index : span * (index + 1), :] = both[:span] + both[span:]

    above = None
    for level in range(levels):
        rows = slice(level * half, (level + 1) * half)
        came = jnp.concatenate([came_ref[rows, :columns], came_ref[rows, columns:]], axis=0)
        value = (moved_ref[level] + came) * pivot_ref[level : level + 1, :]
        if level > 0:
            value = value - carry_ref[level : level + 1, :] * above
        forward_ref[level] = value
        above = value

    products = None
    square = jnp.zeros((vectors, columns), F32)
    below = None
    for index in range(levels // wide - 1, -1, -1):
        for level in range((index + 1) * wide - 1, index * wide - 1, -1):
            value = forward_ref[level]
            if below is not None:
                value = value - ratio_ref[level : level + 1, :] * below
            below = value
            image_ref[level] = value
            square = square + value * value
            stack_terms(value, level, images_ref)
        part = stacked_products(images_ref, stack_ref, wide * index * columns, wide * (index + 1) * columns)
        products = part if products is None else products + part
    cross = join_products(products)
    sums_ref[0:vectors, 0:vectors] = cross
    sums_ref[0:vectors, vectors : 2 * vectors] = gram_ref[...]
    norm = jnp.sum(square, axis=1, keepdims=True)
    shape = (vectors, 2 * vectors)
    eye = lax.broadcasted_iota(jnp.int32, shape, 0) == lax.broadcasted_iota(jnp.int32, shape, 1)
    norm = jnp.sum(jnp.where(eye, norm, 0.0), axis=0, keepdims=True)
    shape = (8, 2 * vectors)
    sums_ref[vectors : vectors + 8, :] = jnp.where(lax.broadcasted_iota(jnp.int32, shape, 0) == 0, norm, far)


def weigh_kernel(cells, sums_ref, more_ref, spans_ref, scale_ref, coupling_ref, direct_ref):
    vectors = coupling_ref.shape[0]
    sums = sums_ref[...] + more_ref[...]
    cross = sums[0:vectors, 0:vectors] / cells
    gram = sums[0:vectors, vectors : 2 * vectors] / cells
    coupling_ref[...] = cross.T
    shape = (vectors, vectors)
    eye = lax.broadcasted_iota(jnp.int32, shape, 0) == lax.broadcasted_iota(jnp.int32, shape, 1)
    square = sums[vectors : vectors + 1, 0:vectors] / cells
    square = jnp.sum(jnp.where(eye, square, 0.0), axis=1, keepdims=True)
    mixed = dot3(cross, gram, (((1,), (0,)), ((), ())))
    spanned = jnp.sum(cross * mixed, axis=1, keepdims=True)
    shared = 2.0 * jnp.sum(cross * cross, axis=1, keepdims=True)
    norm = square - shared + spanned
    small = norm + 1e-6 < 1e-2 * (square + shared + jnp.abs(spanned))
    scale_ref[...] = jnp.broadcast_to(1.0 / jnp.sqrt(jnp.maximum(norm, 0.0) + 1e-6), scale_ref.shape)
    far = jnp.sum(sums[vectors + 1 : vectors + 2, 0:1])
    direct_ref[0] = jnp.where(far + jnp.sum(jnp.where(small, 1.0, 0.0)) > 0.0, 1, 0)
    top, low = split(cross)
    spans_ref[...] = jnp.concatenate([jnp.concatenate([top, top], axis=1), jnp.concatenate([low, low], axis=1)], axis=0)


def last_kernel(spans_ref, scale_ref, image_ref, stack_ref, sums_ref, next_ref, coupling_ref, chunk_ref, sems):
    levels, vectors, columns = image_ref.shape
    chunks = chunk_ref.shape[0]
    step = levels // chunks
    copies = [pltpu.make_async_copy(chunk_ref.at[i], next_ref.at[:, step * i : step * (i + 1), :], sems.at[i]) for i in range(chunks)]
    copies.append(pltpu.make_async_copy(sums_ref, coupling_ref, sems.at[chunks]))
    copies[chunks].start()
    def spanned_by(index):
        cols = slice(step * index * columns, step * (index + 1) * columns)
        both = jnp.dot(spans_ref[...], stack_ref[:, cols], preferred_element_type=F32)
        return both[:vectors] + both[vectors:]

    ready = spanned_by(0)
    for index in range(chunks):
        spanned = ready
        if index + 1 < chunks:
            ready = spanned_by(index + 1)
        for level in range(step):
            at = level * columns
            chunk_ref[index, :, level, :] = (image_ref[step * index + level] - spanned[:, at : at + columns]) * scale_ref[...]
        copies[index].start()
    for copy in copies:
        copy.wait()


VMEM = pl.BlockSpec(memory_space=pltpu.VMEM)
SMEM = pl.BlockSpec(memory_space=pltpu.SMEM)
ANY = pl.BlockSpec(memory_space=pl.ANY)


def call(kernel, outs, out_specs, scratch, specs, *operands):
    return pl.pallas_call(
        kernel,
        out_shape=outs,
        in_specs=specs,
        out_specs=out_specs,
        scratch_shapes=scratch,
        compiler_params=pltpu.CompilerParams(vmem_limit_bytes=40 << 20),
    )(*operands)


def exchange(outer, inner):
    blocks = lax.axis_size(AXES)
    outer = lax.ppermute(outer, AXES, [(i, (i - 1) % blocks if i % 2 == 0 else (i + 1) % blocks) for i in range(blocks)])
    inner = lax.ppermute(inner, AXES, [(i, i ^ 1) for i in range(blocks)])
    return outer, inner


def almost_total(value):
    blocks = lax.axis_size(AXES)
    if blocks & (blocks - 1):
        return lax.psum(value, AXES), jnp.zeros_like(value)
    more = lax.ppermute(value, AXES, [(i, i ^ 1) for i in range(blocks)])
    distance = 2
    while distance < blocks:
        value = value + more
        more = lax.ppermute(value, AXES, [(i, i ^ distance) for i in range(blocks)])
        distance *= 2
    return value, more


def shards(basis, weights, kappa, thickness, depth, neighbours, rim_lists, counts):
    vectors, levels, columns = basis.shape
    links = weights.shape[0]
    halo = rim_lists.shape[1]
    rows = levels // SPAN * 3 * vectors // 2
    chunks = 4

    def out(*shape, dtype=F32):
        return jax.ShapeDtypeStruct(shape, dtype)

    message = out(2 * rows + levels, LANES)
    whole = out(levels, vectors, columns)
    halved = out(levels, vectors // 2, columns)
    plane = out(levels, columns)
    forward = pltpu.VMEM((levels, vectors, columns), F32)
    half_forward = pltpu.VMEM((levels, vectors // 2, columns), F32)
    chunk = pltpu.VMEM((chunks, vectors, levels // chunks, columns), F32)
    sems = pltpu.SemaphoreType.DMA((chunks,))
    cells = levels * vectors
    table = out(24, columns, dtype=jnp.int32)
    outer, inner, mirror, field, live, self_weight, carry, pivot, ratio, table = call(
        functools.partial(edge_kernel, halo),
        (message, message, halved, whole, out(links, levels, columns), plane, plane, plane, plane, table), [VMEM] * 10,
        [pltpu.VMEM((links * columns, columns), BF16), pltpu.VMEM((links // 2 * columns, columns), BF16),
         pltpu.VMEM((cells, links * columns), BF16), pltpu.VMEM((cells, links // 2 * columns), BF16),
         half_forward, pltpu.VMEM((links + 4 + links // 2, levels, columns), F32), chunk,
         pltpu.VMEM((links, levels, columns), F32), pltpu.VMEM((levels, columns), F32), pltpu.VMEM((levels, columns), F32),
         pltpu.VMEM((1, columns), jnp.int32), pltpu.VMEM((links, columns), jnp.int32), sems, pltpu.SemaphoreType.DMA((5,))],
        [SMEM] * 2 + [ANY] * 6,
        counts, rim_lists, basis, weights, kappa, thickness, depth.reshape(1, columns), neighbours)
    outer, inner = exchange(outer, inner)
    moved, stack, gram = call(
        block_kernel,
        (whole, out(2 * vectors, levels * columns, dtype=BF16), out(vectors, vectors)), [VMEM] * 3,
        [pltpu.VMEM((levels, 2 * columns, columns), BF16), forward],
        [VMEM] * 7, table, field, live, self_weight, carry, pivot, ratio)
    image, sums = call(
        functools.partial(second_kernel, halo), (whole, out(vectors + 8, 2 * vectors)), [VMEM] * 2,
        [pltpu.VMEM((links + 4, levels, columns), F32), pltpu.VMEM(((links + 1) * columns, 2 * columns), BF16), half_forward,
         pltpu.VMEM((cells, (links + 1) * columns), BF16), pltpu.VMEM((cells // 2, 2 * columns), F32),
         forward, pltpu.VMEM((2 * vectors, levels * columns), BF16)],
        [VMEM] * 12,
        outer, inner, mirror, stack, moved, live, self_weight, carry, pivot, ratio, table, gram)
    sums, more = almost_total(sums)
    cells = float(levels * columns * lax.axis_size(AXES))
    spans, scale, coupling, direct = call(
        functools.partial(weigh_kernel, cells),
        (out(2 * vectors, 2 * vectors, dtype=BF16), out(vectors, columns), out(vectors, vectors), out(1, dtype=jnp.int32)),
        [VMEM] * 3 + [SMEM], [], [VMEM] * 2, sums, more)

    def from_sums():
        return call(last_kernel, (out(vectors, levels, columns), out(vectors, vectors)), [ANY] * 2,
                    [chunk, pltpu.SemaphoreType.DMA((chunks + 1,))], [VMEM] * 5, spans, scale, image, stack, coupling)

    def from_scratch():
        return direct_form(basis, weights, kappa, thickness, depth, neighbours, rim_lists, counts)

    return tuple(lax.cond(direct[0] > 0, from_scratch, lambda: tuple(from_sums())))


ITERS = 2


def from_behind(block, axis, distance):
    devices = range(lax.axis_size(axis))
    route = [((i - distance) % len(devices), i) for i in devices]
    return lax.ppermute(block, axis, route)


def column_factors(kappa, thickness, keep):
    levels = kappa.shape[0]
    below = jnp.concatenate([keep[1:], jnp.zeros_like(keep[:1])], axis=0)
    interface = kappa * keep * below
    lower, inv_pivot, ratio = ([], [], [])
    for level in range(levels):
        upper_term = interface[level]
        diag_term = 1.0 + upper_term / thickness[level]
        if level > 0:
            diag_term = diag_term + interface[level - 1] / thickness[level]
            low = -interface[level - 1] / thickness[level - 1]
        else:
            low = jnp.zeros_like(upper_term)
        if level < levels - 1:
            upp = -upper_term / thickness[level + 1]
        else:
            upp = jnp.zeros_like(upper_term)
        pivot = diag_term - low * ratio[level - 1] if level > 0 else diag_term
        inverse = 1.0 / pivot
        lower.append(low)
        inv_pivot.append(inverse)
        ratio.append(upp * inverse)
    return (lower, inv_pivot, ratio)


def column_solve(rhs, lower, inv_pivot, ratio):
    levels = rhs.shape[1]
    forward = []
    for level in range(levels):
        if level == 0:
            forward.append(rhs[:, 0] * inv_pivot[0])
        else:
            forward.append((rhs[:, level] - lower[level] * forward[level - 1]) * inv_pivot[level])
    result = [None] * levels
    result[levels - 1] = forward[levels - 1]
    for level in range(levels - 2, -1, -1):
        result[level] = forward[level] - ratio[level] * result[level + 1]
    return jnp.stack(result, axis=1)


def transport_back(field, weights, keep, self_weight, neighbours, rim_lists):
    columns = field.shape[2]
    halo_width = rim_lists.shape[1]
    masked = keep * field
    extended = jnp.zeros((field.shape[0], field.shape[1], columns + 2 * halo_width), jnp.float32)
    for link in range(weights.shape[0]):
        extended = extended.at[:, :, neighbours[link]].add(weights[link] * masked)
    from_right = from_behind(extended[:, :, columns : columns + halo_width], ("region", "sub"), -1)
    from_left = from_behind(extended[:, :, columns + halo_width :], ("region", "sub"), 1)
    result = self_weight * masked + extended[:, :, :columns]
    result = result.at[:, :, rim_lists[0]].add(from_right).at[:, :, rim_lists[1]].add(from_left)
    return keep * result


def direct_form(basis, weights, kappa, thickness, depth, neighbours, rim_lists, counts):
    vectors, levels, columns = basis.shape
    halo_width = rim_lists.shape[1]
    own_index = jnp.arange(columns, dtype=jnp.int32)
    live = (own_index < counts[0]) | (own_index >= columns - 2 * halo_width)
    wet = jnp.arange(levels, dtype=jnp.int32)[:, None] < depth[None, :]
    keep = (live[None, :] & wet).astype(jnp.float32)
    self_weight = 1.0 - jnp.sum(weights, axis=0)
    lower, inv_pivot, ratio = column_factors(kappa, thickness, keep)
    field = basis
    for step in range(ITERS):
        moved = transport_back(field, weights, keep, self_weight, neighbours, rim_lists)
        field = column_solve(keep * moved, lower, inv_pivot, ratio)
    cells = float(levels * columns * lax.axis_size(("region", "sub")))
    high = lax.Precision.HIGHEST
    local_cross = jnp.einsum("ilc,jlc->ij", basis, field, precision=high)
    coupling = lax.psum(local_cross, ("region", "sub")) / cells
    residual = field - jnp.einsum("ilc,ij->jlc", basis, coupling, precision=high)
    local_norms = jnp.einsum("jlc,jlc->j", residual, residual, precision=high)
    norms = lax.psum(local_norms, ("region", "sub")) / cells
    next_basis = residual / jnp.sqrt(norms + 1e-06)[:, None, None]
    return (next_basis, coupling)


def solution(mesh):
    placed = (
        P("groups", None, AXES),
        P(None, None, AXES),
        P(None, AXES),
        P(None, AXES),
        P(AXES),
        P(None, AXES),
        P(None, AXES),
        P(AXES),
    )
    return jax.shard_map(
        shards,
        mesh=mesh,
        in_specs=placed,
        out_specs=(P("groups", None, AXES), P("groups", None)),
        check_vma=False,
    )
```

```python
import functools

import jax
import jax.numpy as jnp
from jax import lax
from jax.experimental import pallas as pl
from jax.experimental.pallas import tpu as pltpu
from jax.sharding import PartitionSpec as P

AXES = ("region", "sub")
LANES = 128
PIECES = ((8, 0), (4, 8))
REACH = 12
SPAN = 16
F32 = jnp.float32
BF16 = jnp.bfloat16
NT = (((1,), (1,)), ((), ()))


def split(x):
    top = x.astype(BF16)
    return top, (x - top.astype(F32)).astype(BF16)


def dot3(a, b, dims):
    a_top, a_low = split(a)
    b_top, b_low = split(b)
    dot = functools.partial(lax.dot_general, dimension_numbers=dims, preferred_element_type=F32)
    return dot(a_top, b_top) + (dot(a_top, b_low) + dot(a_low, b_top))


def one_hot(hits, size):
    by_lane = hits.astype(F32).T
    lanes = by_lane.shape[0]
    column = lax.broadcasted_iota(jnp.int32, (lanes, size), 1).astype(F32)
    return [jnp.where(jnp.broadcast_to(by_lane[:, i : i + 1], (lanes, size)) == column, 1.0, 0.0).astype(BF16) for i in range(hits.shape[0])]


def matmul_group(index, spread_ref, targets_ref, rows):
    both = jnp.dot(spread_ref[2 * rows * index : 2 * rows * (index + 1), :], targets_ref[...], preferred_element_type=F32)
    return both[:rows] + both[rows:]


def factor_columns(kappa_ref, thickness_ref, keep, carry_ref, pivot_ref, ratio_ref):
    levels = keep.shape[0]
    interface = [kappa_ref[i : i + 1, :] * keep[i : i + 1] * keep[i + 1 : i + 2] for i in range(levels - 1)]
    ratio = None
    for level in range(levels):
        thick = thickness_ref[level : level + 1, :]
        pivot = jnp.ones_like(thick)
        if level < levels - 1:
            pivot = pivot + interface[level] / thick
        if level > 0:
            pivot = pivot + interface[level - 1] / thick
            low = -interface[level - 1] / thickness_ref[level - 1 : level, :]
            pivot = pivot - low * ratio
        inverse = 1.0 / pivot
        carry_ref[level : level + 1, :] = low * inverse if level > 0 else jnp.zeros_like(thick)
        pivot_ref[level : level + 1, :] = keep[level : level + 1] * inverse
        if level < levels - 1:
            ratio = -interface[level] / thickness_ref[level + 1 : level + 2, :] * inverse
            ratio_ref[level : level + 1, :] = ratio
        else:
            ratio_ref[level : level + 1, :] = jnp.zeros_like(thick)


def lane_group(shape, width):
    return lax.broadcasted_iota(jnp.int32, shape, 1) // width


def pick(plane, lanes):
    return jnp.take_along_axis(plane, lanes, axis=1, mode="promise_in_bounds")


def rim_lanes(rim_ref, row, halo, shape):
    slot = lax.broadcasted_iota(jnp.int32, shape, 1) % halo
    columns = jnp.zeros(shape, jnp.int32)
    for index in range(halo):
        columns = jnp.where(slot == index, rim_ref[row, index], columns)
    return columns


def rim_coefficients(planes, neighbours, columns, first, halo):
    group = lane_group(columns.shape, halo)
    packed = jnp.zeros(columns.shape, F32)
    for index, plane in enumerate(planes):
        packed = jnp.where(group == index, pick(plane, columns), packed)
    slot = pick(neighbours, columns) - first
    slot = jnp.where((slot >= 0) & (slot < halo), slot, -1)
    return jnp.where(group == len(planes), slot.astype(F32), packed)


def padded_links(neighbours_ref, rows):
    links, columns = neighbours_ref.shape
    padded = jnp.concatenate([neighbours_ref[...], jnp.zeros((8 - links, columns), jnp.int32)], axis=0)
    if rows > 8:
        padded = jnp.concatenate([padded, jnp.zeros((rows - 8, columns), jnp.int32)], axis=0)
    return padded


PLACES = (
    ((32, 40, 0, 8, 48, 56, 16, 24), (48, 56, 16, 24, 32, 40, 0, 8)),
    ((40, 44, 32, 36, 8, 12, 0, 4, 56, 60, 48, 52, 24, 28, 16, 20), (56, 60, 48, 52, 24, 28, 16, 20, 40, 44, 32, 36, 8, 12, 0, 4)),
)


def pack_slots(levels):
    lane = lax.broadcasted_iota(jnp.int32, levels[0].shape, 1)

    def pair(blocks, mask, turn):
        return [jnp.where(mask, a, pltpu.roll(b, turn % LANES, 1)) for a, b in zip(blocks[::2], blocks[1::2])]

    upper = lane % 64 >= 32
    first_of_two = lane // 16 % 2 == 0
    eights = pair(pair(levels, lane // 8 % 2 == 0, 8), upper, -32)
    fours = pair(pair(pair(levels, lane // 4 % 2 == 0, 4), lane // 8 % 2 == 1, -8), upper, -32)
    blocks = eights + fours
    return pair(blocks, first_of_two, 16), pair(blocks, ~first_of_two, -16)


def unpack_slots(message, level, side, slot_group, halo, half):
    base = level // SPAN * 3 * half
    pieces = []
    for (width, start), places in zip(PIECES, PLACES):
        fit = LANES // 2 // width
        at = base + level % SPAN // fit * half
        turn = (slot_group * halo + start - places[side][level % fit]) % LANES
        block = message[at : at + half]
        pieces.append(pltpu.roll(block, turn, 1) if turn else block)
        base += SPAN // fit * half
    return pieces


def edge_kernel(halo, counts_ref, rim_ref, basis_ref, weights_in, kappa_in, thickness_in, depth_in, neighbours_in,
                outer_ref, inner_ref, mirror_ref, field_ref, live_ref, self_ref, carry_ref, pivot_ref, ratio_ref, table_ref,
                near_ref, leave_ref, spread_ref, spread_two_ref, forward_ref, plane_ref, chunk_ref, weights_ref, kappa_ref,
                thickness_ref, depth_ref, neighbours_ref, sems, small_sems):
    small = [(weights_in, weights_ref), (kappa_in, kappa_ref), (thickness_in, thickness_ref), (depth_in, depth_ref), (neighbours_in, neighbours_ref)]
    small = [pltpu.make_async_copy(a, b, small_sems.at[i]) for i, (a, b) in enumerate(small)]
    for copy in small:
        copy.start()
    vectors, levels, columns = basis_ref.shape
    links = weights_ref.shape[0]
    half = vectors // 2
    chunks = chunk_ref.shape[0]
    step = levels // chunks
    copies = [pltpu.make_async_copy(basis_ref.at[:, step * i : step * (i + 1), :], chunk_ref.at[i], sems.at[i]) for i in range(chunks)]
    for copy in copies:
        copy.start()
    for copy in small:
        copy.wait()
    shape = (levels, columns)
    lane = lax.broadcasted_iota(jnp.int32, shape, 1)
    live = (lane < counts_ref[0]) | (lane >= columns - 2 * halo)
    keep = jnp.where(live & (lax.broadcasted_iota(jnp.int32, shape, 0) < depth_ref[...]), 1.0, 0.0)
    total = weights_ref[0]
    for link in range(1, links):
        total = total + weights_ref[link]
    self_ref[...] = keep * (1.0 - total)
    for link in range(links):
        live_ref[link] = keep * weights_ref[link]
    factor_columns(kappa_ref, thickness_ref, keep, carry_ref, pivot_ref, ratio_ref)

    def near(value, other):
        lanes = lax.broadcasted_iota(jnp.int32, value.shape, 1)
        return jnp.where((lanes >= columns // 4) & (lanes < 3 * columns // 4), pltpu.roll(other, columns // 2, 1), value)

    named = padded_links(neighbours_ref, 8)
    lane8 = lane[0:8]
    near_links = near(named.astype(F32), named.astype(F32)).astype(jnp.int32)
    second = (lane8 >= columns // 4) & (lane8 < 3 * columns // 4)
    first_rim = near_links < halo
    last_rim = (near_links >= columns - halo) & (near_links < columns + 2 * halo)
    hit = jnp.where(first_rim, near_links, jnp.where(last_rim, near_links - columns + 2 * halo, -1))
    hit = jnp.where((hit >= 0) & second, hit + columns // 2, hit)
    for link, matrix in enumerate(one_hot(hit, columns)[:links]):
        near_ref[link * columns : (link + 1) * columns, :] = matrix
    part8 = lane_group((8, columns), halo) % 4
    slot8 = lane8 % halo
    rim_column = jnp.where(part8 % 2 == 0, slot8, columns - halo + slot8)
    leaving = pick(named, rim_column)
    leaving = jnp.where(leaving >= columns, leaving - columns + 2 * halo + lane8 // (4 * halo) * (4 * halo), -1)
    leaving = jnp.where((part8 < 2) == (lax.broadcasted_iota(jnp.int32, (8, columns), 0) < links // 2), leaving, -1)
    matrices = one_hot(leaving, columns)
    for link in range(links // 2):
        leave_ref[link * columns : (link + 1) * columns, :] = matrices[link] + matrices[link + links // 2]

    for link in range(links):
        plane_ref[link] = near(live_ref[link], live_ref[link])
    plane_ref[links] = near(self_ref[...], self_ref[...])
    part = lane_group(shape, halo) % 4
    slot = lane % halo
    rim_column = jnp.where(part % 2 == 0, slot, columns - halo + slot)
    for index, ref in enumerate((carry_ref, pivot_ref, ratio_ref)):
        plane_ref[links + 1 + index] = jnp.where(part < 2, pick(ref[...], rim_column), 0.0)
    for link in range(links // 2):
        other = pick(live_ref[link + links // 2], rim_column)
        plane_ref[links + 4 + link] = jnp.where(part < 2, pick(live_ref[link], rim_column), other)

    def spread(value, level, wide, planes, target_ref):
        at = level // wide * 2 * wide * half + level % wide * half
        for index, plane in enumerate(planes):
            top, low = split(value * plane_ref[plane, level : level + 1, :])
            cols = slice(index * columns, (index + 1) * columns)
            target_ref[at : at + half, cols] = top
            target_ref[at + wide * half : at + (wide + 1) * half, cols] = low

    wide = levels // 4
    rows = wide * half
    part_half = lane_group((half, columns), halo) % 4
    even = lax.axis_index(AXES) % 2 == 0
    table_ref[0:8, :] = named
    table_ref[8:16, :] = rim_lanes(rim_ref, 1, halo, (8, columns))
    table_ref[16:24, :] = rim_lanes(rim_ref, 0, halo, (8, columns))

    total_rows = levels // SPAN * 3 * half

    def send(first, levels_of):
        left, right = pack_slots(levels_of)
        for index in range(len(left)):
            at = first + index * half
            outer_ref[at : at + half, :] = jnp.where(even, left[index], right[index])
            inner_ref[at : at + half, :] = jnp.where(even, right[index], left[index])

    def enter(index):
        own = []
        for level in range(index * wide, (index + 1) * wide):
            value = chunk_ref[level // step, :, level % step, :]
            field_ref[level] = value
            value = near(value[:half], value[half:])
            spread(value, level, wide, range(links), spread_ref)
            value = value * plane_ref[links, level : level + 1, :]
            own.append(jnp.where(part_half == 0, value, pltpu.roll(value, 2 * halo, 1)))
        return matmul_group(index, spread_ref, near_ref, rows), own

    for copy in copies:
        copy.wait()
    above = None
    ready = enter(0)
    for index in range(levels // wide):
        moved, own = ready
        if index + 1 < levels // wide:
            ready = enter(index + 1)
        slots = [moved[i * half : (i + 1) * half] for i in range(wide)]
        for level in range(index * wide, (index + 1) * wide):
            value = slots[level - index * wide]
            mirror_ref[level] = value
            value = (value + own[level - index * wide]) * plane_ref[links + 2, level : level + 1, :]
            if level > 0:
                value = value - plane_ref[links + 1, level : level + 1, :] * above
            forward_ref[level] = value
            above = value
        if (index + 1) * wide % SPAN == 0:
            last = (index + 1) * wide
            send((last // SPAN - 1) * 3 * half, [mirror_ref[level] for level in range(last - SPAN, last)])

    below = None
    for index in range(levels // wide - 1, -1, -1):
        span = range(index * wide, (index + 1) * wide)
        for level in reversed(span):
            value = forward_ref[level]
            if below is not None:
                value = value - plane_ref[links + 3, level : level + 1, :] * below
            below = value
            value = jnp.where(part_half < 2, value, pltpu.roll(value, 2 * halo, 1))
            spread(value, level, wide, range(links + 4, links + 4 + links // 2), spread_two_ref)
        moved = matmul_group(index, spread_two_ref, leave_ref, rows)
        for level in span:
            forward_ref[level] = moved[(level - index * wide) * half : (level - index * wide + 1) * half]
        if index * wide % SPAN == 0:
            first = index * wide
            send(total_rows + first // SPAN * 3 * half, [forward_ref[level] for level in range(first, first + SPAN)])
    planes = [carry_ref[...], pivot_ref[...], ratio_ref[...]] + [live_ref[link] for link in range(links)]
    neighbours = padded_links(neighbours_ref, levels)
    left = rim_coefficients(planes, neighbours, rim_lanes(rim_ref, 1, halo, shape), columns, halo)
    right = rim_coefficients(planes, neighbours, rim_lanes(rim_ref, 0, halo, shape), columns + halo, halo)
    outer_ref[2 * total_rows :, :] = jnp.where(even, left, right)
    inner_ref[2 * total_rows :, :] = jnp.where(even, right, left)


def block_kernel(table_ref, field_ref, live_ref, self_ref, carry_ref, pivot_ref, ratio_ref, moved_ref, stack_ref, gram_ref,
                 matrix_ref, forward_ref):
    levels, vectors, columns = field_ref.shape
    links = live_ref.shape[0]
    row = lax.broadcasted_iota(jnp.int32, (columns, columns), 0)
    own = row == lax.broadcasted_iota(jnp.int32, (columns, columns), 1)

    def move(terms, level):
        both = lax.dot_general(terms, matrix_ref[level], NT, preferred_element_type=F32)
        both = both[:, :columns] + both[:, columns:]
        return both[:vectors] + both[vectors:]

    above = None
    for level in range(levels):
        matrix = jnp.where(own, self_ref[level : level + 1, :], 0.0)
        for link in range(links):
            matrix = matrix + jnp.where(table_ref[link : link + 1, :] == row, live_ref[link, level : level + 1, :], 0.0)
        matrix_ref[level, 0:columns, :], matrix_ref[level, columns:, :] = split(matrix)
        stack_terms(field_ref[level], level, stack_ref)
        value = move(stack_ref[:, level * columns : (level + 1) * columns], level) * pivot_ref[level : level + 1, :]
        if level > 0:
            value = value - carry_ref[level : level + 1, :] * above
        forward_ref[level] = value
        above = value
    below = None
    for level in range(levels - 1, -1, -1):
        value = forward_ref[level]
        if below is not None:
            value = value - ratio_ref[level : level + 1, :] * below
        below = value
        moved_ref[level] = move(jnp.concatenate(split(value), axis=0), level)
    gram = None
    span = levels * columns // 4
    for index in range(4):
        part = stacked_products(stack_ref, stack_ref, span * index, span * (index + 1))
        gram = part if gram is None else gram + part
    gram_ref[...] = join_products(gram)


def stack_terms(value, level, stack_ref):
    vectors, columns = value.shape
    top, low = split(value)
    cols = slice(level * columns, (level + 1) * columns)
    stack_ref[0:vectors, cols] = top
    stack_ref[vectors:, cols] = low


def stacked_products(a_ref, b_ref, first, last):
    return lax.dot_general(a_ref[:, first:last], b_ref[:, first:last], NT, preferred_element_type=F32)


def join_products(products):
    half = products.shape[0] // 2
    return products[:half, :half] + (products[:half, half:] + products[half:, :half])


def second_kernel(halo, outer_ref, inner_ref, mirror_ref, stack_ref, moved_ref, live_ref,
                  self_ref, carry_ref, pivot_ref, ratio_ref, table_ref, gram_ref, image_ref, sums_ref,
                  plane_ref, target_ref, rim_field_ref, spread_ref, came_ref, forward_ref, images_ref):
    levels, vectors, columns = moved_ref.shape
    links = live_ref.shape[0]
    half = vectors // 2
    rows = levels // SPAN * 3 * half
    even = lax.axis_index(AXES) % 2 == 0
    outer = outer_ref[...]
    inner = inner_ref[...]
    from_left = jnp.where(even, outer, inner)
    from_right = jnp.where(even, inner, outer)

    def parts_of(shape):
        return lane_group(shape, halo) % 4

    shape = (levels, columns)
    part = parts_of(shape)
    slot = lax.broadcasted_iota(jnp.int32, shape, 1) % halo
    lead = table_ref[8:16, :]
    trail = table_ref[16:24, :]
    own_column = jnp.concatenate([jnp.where(part[0:8] % 2 == 0, lead, trail)] * (levels // 8), axis=0)
    planes = [carry_ref[...], pivot_ref[...], ratio_ref[...]] + [live_ref[link] for link in range(links)]
    for index, plane in enumerate(planes):
        theirs = jnp.where(part == 2, pick(from_left[2 * rows :], slot + halo * index), pick(from_right[2 * rows :], slot + halo * index))
        plane_ref[index] = jnp.where(part < 2, pick(plane, own_column), theirs)
    plane_ref[len(planes)] = pick(self_ref[...], own_column)
    plane_ref[1] = jnp.where(slot < REACH, plane_ref[1], 0.0)

    shape = (8, columns)
    part, slot, own_column = part[0:8], slot[0:8], own_column[0:8]
    named = pick(table_ref[0:8, :], own_column)
    from_links = slot + halo * len(planes)
    theirs = jnp.where(part == 2, pick(from_left[2 * rows : 2 * rows + 8], from_links), pick(from_right[2 * rows : 2 * rows + 8], from_links)).astype(jnp.int32)
    facing = jnp.where(part == 2, pick(lead, jnp.maximum(theirs, 0)), pick(trail, jnp.maximum(theirs, 0)))
    target = jnp.where(part < 2, jnp.where(named < columns, named, -1), jnp.where(theirs >= 0, facing, -1))
    link_row = lax.broadcasted_iota(jnp.int32, shape, 0)
    target = jnp.where(link_row == links, jnp.where((part < 2) | (slot < REACH), own_column, -1), target)
    lane = lax.broadcasted_iota(jnp.int32, shape, 1)
    links_of = jnp.where(link_row < links, table_ref[0:8, :], lane)
    far = (links_of >= columns) & (links_of < columns + halo) & (lane >= halo)
    far = far | ((links_of >= columns + halo) & (lane < columns - halo))
    far = far | ((links_of >= columns) & ((links_of - columns) % halo >= REACH))
    far = far | ((links_of < halo) & (lane >= 2 * halo))
    far = far | ((links_of >= columns - halo) & (links_of < columns) & (lane < columns - 2 * halo))
    far = jnp.sum(jnp.where(far, 1.0, 0.0), axis=1, keepdims=True)
    far = jnp.sum(far, axis=0, keepdims=True)
    first_half = lax.broadcasted_iota(jnp.int32, (columns, columns), 0) < 4 * halo
    for link, matrix in enumerate(one_hot(target, columns)[: links + 1]):
        at = slice(link * columns, (link + 1) * columns)
        target_ref[at, 0:columns] = jnp.where(first_half, matrix, jnp.zeros_like(matrix))
        target_ref[at, columns:] = jnp.where(first_half, jnp.zeros_like(matrix), matrix)

    half_part = parts_of((half, columns))

    head = lax.broadcasted_iota(jnp.int32, (half, columns), 1) % halo < PIECES[1][1]

    def put(value, message, level, side, to):
        first, second = unpack_slots(message, level, side, to, halo, half)
        return jnp.where(half_part == to, jnp.where(head, first, second), value)

    above = None
    for level in range(levels):
        value = put(put(mirror_ref[level], from_left, level, 1, 0), from_right, level, 0, 1)
        value = value * plane_ref[1, level : level + 1, :]
        if level > 0:
            value = value - plane_ref[0, level : level + 1, :] * above
        rim_field_ref[level] = value
        above = value
    late_left = from_left[rows : 2 * rows]
    late_right = from_right[rows : 2 * rows]
    wide = levels // 4
    span = wide * half
    below = None
    for index in range(levels // wide - 1, -1, -1):
        for level in range((index + 1) * wide - 1, index * wide - 1, -1):
            value = rim_field_ref[level]
            if below is not None:
                value = value - plane_ref[2, level : level + 1, :] * below
            below = value
            at = 2 * span * index + level % wide * half
            for link in range(links + 1):
                term = value * plane_ref[3 + link, level : level + 1, :]
                if link == links:
                    term = put(put(term, late_left, level, 1, 2), late_right, level, 0, 3)
                top, low = split(term)
                cols = slice(link * columns, (link + 1) * columns)
                spread_ref[at : at + half, cols] = top
                spread_ref[at + span : at + span + half, cols] = low
        both = jnp.dot(spread_ref[2 * span * index : 2 * span * (index + 1), :], target_ref[...], preferred_element_type=F32)
        came_ref[span * index : span * (index + 1), :] = both[:span] + both[span:]

    above = None
    for level in range(levels):
        rows = slice(level * half, (level + 1) * half)
        came = jnp.concatenate([came_ref[rows, :columns], came_ref[rows, columns:]], axis=0)
        value = (moved_ref[level] + came) * pivot_ref[level : level + 1, :]
        if level > 0:
            value = value - carry_ref[level : level + 1, :] * above
        forward_ref[level] = value
        above = value

    products = None
    square = jnp.zeros((vectors, columns), F32)
    below = None
    for index in range(levels // wide - 1, -1, -1):
        for level in range((index + 1) * wide - 1, index * wide - 1, -1):
            value = forward_ref[level]
            if below is not None:
                value = value - ratio_ref[level : level + 1, :] * below
            below = value
            image_ref[level] = value
            square = square + value * value
            stack_terms(value, level, images_ref)
        part = stacked_products(images_ref, stack_ref, wide * index * columns, wide * (index + 1) * columns)
        products = part if products is None else products + part
    cross = join_products(products)
    sums_ref[0:vectors, 0:vectors] = cross
    sums_ref[0:vectors, vectors : 2 * vectors] = gram_ref[...]
    norm = jnp.sum(square, axis=1, keepdims=True)
    shape = (vectors, 2 * vectors)
    eye = lax.broadcasted_iota(jnp.int32, shape, 0) == lax.broadcasted_iota(jnp.int32, shape, 1)
    norm = jnp.sum(jnp.where(eye, norm, 0.0), axis=0, keepdims=True)
    shape = (8, 2 * vectors)
    sums_ref[vectors : vectors + 8, :] = jnp.where(lax.broadcasted_iota(jnp.int32, shape, 0) == 0, norm, far)


def weigh_kernel(cells, sums_ref, more_ref, spans_ref, scale_ref, coupling_ref, direct_ref):
    vectors = coupling_ref.shape[0]
    sums = sums_ref[...] + more_ref[...]
    cross = sums[0:vectors, 0:vectors] / cells
    gram = sums[0:vectors, vectors : 2 * vectors] / cells
    coupling_ref[...] = cross.T
    shape = (vectors, vectors)
    eye = lax.broadcasted_iota(jnp.int32, shape, 0) == lax.broadcasted_iota(jnp.int32, shape, 1)
    square = sums[vectors : vectors + 1, 0:vectors] / cells
    square = jnp.sum(jnp.where(eye, square, 0.0), axis=1, keepdims=True)
    mixed = dot3(cross, gram, (((1,), (0,)), ((), ())))
    spanned = jnp.sum(cross * mixed, axis=1, keepdims=True)
    shared = 2.0 * jnp.sum(cross * cross, axis=1, keepdims=True)
    norm = square - shared + spanned
    small = norm + 1e-6 < 1e-2 * (square + shared + jnp.abs(spanned))
    scale_ref[...] = jnp.broadcast_to(1.0 / jnp.sqrt(jnp.maximum(norm, 0.0) + 1e-6), scale_ref.shape)
    far = jnp.sum(sums[vectors + 1 : vectors + 2, 0:1])
    direct_ref[0] = jnp.where(far + jnp.sum(jnp.where(small, 1.0, 0.0)) > 0.0, 1, 0)
    top, low = split(cross)
    spans_ref[...] = jnp.concatenate([jnp.concatenate([top, top], axis=1), jnp.concatenate([low, low], axis=1)], axis=0)


def last_kernel(spans_ref, scale_ref, image_ref, stack_ref, sums_ref, next_ref, coupling_ref, chunk_ref, sems):
    levels, vectors, columns = image_ref.shape
    chunks = chunk_ref.shape[0]
    step = levels // chunks
    copies = [pltpu.make_async_copy(chunk_ref.at[i], next_ref.at[:, step * i : step * (i + 1), :], sems.at[i]) for i in range(chunks)]
    copies.append(pltpu.make_async_copy(sums_ref, coupling_ref, sems.at[chunks]))
    copies[chunks].start()
    def spanned_by(index):
        cols = slice(step * index * columns, step * (index + 1) * columns)
        both = jnp.dot(spans_ref[...], stack_ref[:, cols], preferred_element_type=F32)
        return both[:vectors] + both[vectors:]

    ready = spanned_by(0)
    for index in range(chunks):
        spanned = ready
        if index + 1 < chunks:
            ready = spanned_by(index + 1)
        for level in range(step):
            at = level * columns
            chunk_ref[index, :, level, :] = (image_ref[step * index + level] - spanned[:, at : at + columns]) * scale_ref[...]
        copies[index].start()
    for copy in copies:
        copy.wait()


VMEM = pl.BlockSpec(memory_space=pltpu.VMEM)
SMEM = pl.BlockSpec(memory_space=pltpu.SMEM)
ANY = pl.BlockSpec(memory_space=pl.ANY)


def call(kernel, outs, out_specs, scratch, specs, *operands):
    return pl.pallas_call(
        kernel,
        out_shape=outs,
        in_specs=specs,
        out_specs=out_specs,
        scratch_shapes=scratch,
        compiler_params=pltpu.CompilerParams(vmem_limit_bytes=40 << 20),
    )(*operands)


def exchange(outer, inner):
    blocks = lax.axis_size(AXES)
    outer = lax.ppermute(outer, AXES, [(i, (i - 1) % blocks if i % 2 == 0 else (i + 1) % blocks) for i in range(blocks)])
    inner = lax.ppermute(inner, AXES, [(i, i ^ 1) for i in range(blocks)])
    return outer, inner


def almost_total(value):
    blocks = lax.axis_size(AXES)
    if blocks & (blocks - 1):
        return lax.psum(value, AXES), jnp.zeros_like(value)
    distance = 2
    while distance < blocks:
        value = value + lax.ppermute(value, AXES, [(i, i ^ distance) for i in range(blocks)])
        distance *= 2
    more = lax.ppermute(value, AXES, [(i, i ^ 1) for i in range(blocks)])
    return value, more


def shards(basis, weights, kappa, thickness, depth, neighbours, rim_lists, counts):
    vectors, levels, columns = basis.shape
    links = weights.shape[0]
    halo = rim_lists.shape[1]
    rows = levels // SPAN * 3 * vectors // 2
    chunks = 4

    def out(*shape, dtype=F32):
        return jax.ShapeDtypeStruct(shape, dtype)

    message = out(2 * rows + levels, LANES)
    whole = out(levels, vectors, columns)
    halved = out(levels, vectors // 2, columns)
    plane = out(levels, columns)
    forward = pltpu.VMEM((levels, vectors, columns), F32)
    half_forward = pltpu.VMEM((levels, vectors // 2, columns), F32)
    chunk = pltpu.VMEM((chunks, vectors, levels // chunks, columns), F32)
    sems = pltpu.SemaphoreType.DMA((chunks,))
    cells = levels * vectors
    table = out(24, columns, dtype=jnp.int32)
    outer, inner, mirror, field, live, self_weight, carry, pivot, ratio, table = call(
        functools.partial(edge_kernel, halo),
        (message, message, halved, whole, out(links, levels, columns), plane, plane, plane, plane, table), [VMEM] * 10,
        [pltpu.VMEM((links * columns, columns), BF16), pltpu.VMEM((links // 2 * columns, columns), BF16),
         pltpu.VMEM((cells, links * columns), BF16), pltpu.VMEM((cells, links // 2 * columns), BF16),
         half_forward, pltpu.VMEM((links + 4 + links // 2, levels, columns), F32), chunk,
         pltpu.VMEM((links, levels, columns), F32), pltpu.VMEM((levels, columns), F32), pltpu.VMEM((levels, columns), F32),
         pltpu.VMEM((1, columns), jnp.int32), pltpu.VMEM((links, columns), jnp.int32), sems, pltpu.SemaphoreType.DMA((5,))],
        [SMEM] * 2 + [ANY] * 6,
        counts, rim_lists, basis, weights, kappa, thickness, depth.reshape(1, columns), neighbours)
    outer, inner = exchange(outer, inner)
    moved, stack, gram = call(
        block_kernel,
        (whole, out(2 * vectors, levels * columns, dtype=BF16), out(vectors, vectors)), [VMEM] * 3,
        [pltpu.VMEM((levels, 2 * columns, columns), BF16), forward],
        [VMEM] * 7, table, field, live, self_weight, carry, pivot, ratio)
    image, sums = call(
        functools.partial(second_kernel, halo), (whole, out(vectors + 8, 2 * vectors)), [VMEM] * 2,
        [pltpu.VMEM((links + 4, levels, columns), F32), pltpu.VMEM(((links + 1) * columns, 2 * columns), BF16), half_forward,
         pltpu.VMEM((cells, (links + 1) * columns), BF16), pltpu.VMEM((cells // 2, 2 * columns), F32),
         forward, pltpu.VMEM((2 * vectors, levels * columns), BF16)],
        [VMEM] * 12,
        outer, inner, mirror, stack, moved, live, self_weight, carry, pivot, ratio, table, gram)
    sums, more = almost_total(sums)
    cells = float(levels * columns * lax.axis_size(AXES))
    spans, scale, coupling, direct = call(
        functools.partial(weigh_kernel, cells),
        (out(2 * vectors, 2 * vectors, dtype=BF16), out(vectors, columns), out(vectors, vectors), out(1, dtype=jnp.int32)),
        [VMEM] * 3 + [SMEM], [], [VMEM] * 2, sums, more)

    def from_sums():
        return call(last_kernel, (out(vectors, levels, columns), out(vectors, vectors)), [ANY] * 2,
                    [chunk, pltpu.SemaphoreType.DMA((chunks + 1,))], [VMEM] * 5, spans, scale, image, stack, coupling)

    def from_scratch():
        return direct_form(basis, weights, kappa, thickness, depth, neighbours, rim_lists, counts)

    return tuple(lax.cond(direct[0] > 0, from_scratch, lambda: tuple(from_sums())))


ITERS = 2


def from_behind(block, axis, distance):
    devices = range(lax.axis_size(axis))
    route = [((i - distance) % len(devices), i) for i in devices]
    return lax.ppermute(block, axis, route)


def column_factors(kappa, thickness, keep):
    levels = kappa.shape[0]
    below = jnp.concatenate([keep[1:], jnp.zeros_like(keep[:1])], axis=0)
    interface = kappa * keep * below
    lower, inv_pivot, ratio = ([], [], [])
    for level in range(levels):
        upper_term = interface[level]
        diag_term = 1.0 + upper_term / thickness[level]
        if level > 0:
            diag_term = diag_term + interface[level - 1] / thickness[level]
            low = -interface[level - 1] / thickness[level - 1]
        else:
            low = jnp.zeros_like(upper_term)
        if level < levels - 1:
            upp = -upper_term / thickness[level + 1]
        else:
            upp = jnp.zeros_like(upper_term)
        pivot = diag_term - low * ratio[level - 1] if level > 0 else diag_term
        inverse = 1.0 / pivot
        lower.append(low)
        inv_pivot.append(inverse)
        ratio.append(upp * inverse)
    return (lower, inv_pivot, ratio)


def column_solve(rhs, lower, inv_pivot, ratio):
    levels = rhs.shape[1]
    forward = []
    for level in range(levels):
        if level == 0:
            forward.append(rhs[:, 0] * inv_pivot[0])
        else:
            forward.append((rhs[:, level] - lower[level] * forward[level - 1]) * inv_pivot[level])
    result = [None] * levels
    result[levels - 1] = forward[levels - 1]
    for level in range(levels - 2, -1, -1):
        result[level] = forward[level] - ratio[level] * result[level + 1]
    return jnp.stack(result, axis=1)


def transport_back(field, weights, keep, self_weight, neighbours, rim_lists):
    columns = field.shape[2]
    halo_width = rim_lists.shape[1]
    masked = keep * field
    extended = jnp.zeros((field.shape[0], field.shape[1], columns + 2 * halo_width), jnp.float32)
    for link in range(weights.shape[0]):
        extended = extended.at[:, :, neighbours[link]].add(weights[link] * masked)
    from_right = from_behind(extended[:, :, columns : columns + halo_width], ("region", "sub"), -1)
    from_left = from_behind(extended[:, :, columns + halo_width :], ("region", "sub"), 1)
    result = self_weight * masked + extended[:, :, :columns]
    result = result.at[:, :, rim_lists[0]].add(from_right).at[:, :, rim_lists[1]].add(from_left)
    return keep * result


def direct_form(basis, weights, kappa, thickness, depth, neighbours, rim_lists, counts):
    vectors, levels, columns = basis.shape
    halo_width = rim_lists.shape[1]
    own_index = jnp.arange(columns, dtype=jnp.int32)
    live = (own_index < counts[0]) | (own_index >= columns - 2 * halo_width)
    wet = jnp.arange(levels, dtype=jnp.int32)[:, None] < depth[None, :]
    keep = (live[None, :] & wet).astype(jnp.float32)
    self_weight = 1.0 - jnp.sum(weights, axis=0)
    lower, inv_pivot, ratio = column_factors(kappa, thickness, keep)
    field = basis
    for step in range(ITERS):
        moved = transport_back(field, weights, keep, self_weight, neighbours, rim_lists)
        field = column_solve(keep * moved, lower, inv_pivot, ratio)
    cells = float(levels * columns * lax.axis_size(("region", "sub")))
    high = lax.Precision.HIGHEST
    local_cross = jnp.einsum("ilc,jlc->ij", basis, field, precision=high)
    coupling = lax.psum(local_cross, ("region", "sub")) / cells
    residual = field - jnp.einsum("ilc,ij->jlc", basis, coupling, precision=high)
    local_norms = jnp.einsum("jlc,jlc->j", residual, residual, precision=high)
    norms = lax.psum(local_norms, ("region", "sub")) / cells
    next_basis = residual / jnp.sqrt(norms + 1e-06)[:, None, None]
    return (next_basis, coupling)


def solution(mesh):
    placed = (
        P("groups", None, AXES),
        P(None, None, AXES),
        P(None, AXES),
        P(None, AXES),
        P(AXES),
        P(None, AXES),
        P(None, AXES),
        P(AXES),
    )
    return jax.shard_map(
        shards,
        mesh=mesh,
        in_specs=placed,
        out_specs=(P("groups", None, AXES), P("groups", None)),
        check_vma=False,
    )
```

```python
import functools

import jax
import jax.numpy as jnp
from jax import lax
from jax.experimental import pallas as pl
from jax.experimental.pallas import tpu as pltpu
from jax.sharding import PartitionSpec as P

AXES = ("region", "sub")
LANES = 128
PIECES = ((8, 0), (4, 8))
REACH = 12
SPAN = 16
F32 = jnp.float32
BF16 = jnp.bfloat16
NT = (((1,), (1,)), ((), ()))


def split(x):
    top = x.astype(BF16)
    return top, (x - top.astype(F32)).astype(BF16)


def dot3(a, b, dims):
    a_top, a_low = split(a)
    b_top, b_low = split(b)
    dot = functools.partial(lax.dot_general, dimension_numbers=dims, preferred_element_type=F32)
    return dot(a_top, b_top) + (dot(a_top, b_low) + dot(a_low, b_top))


def one_hot(hits, size):
    by_lane = hits.astype(F32).T
    lanes = by_lane.shape[0]
    column = lax.broadcasted_iota(jnp.int32, (lanes, size), 1).astype(F32)
    return [jnp.where(jnp.broadcast_to(by_lane[:, i : i + 1], (lanes, size)) == column, 1.0, 0.0).astype(BF16) for i in range(hits.shape[0])]


def matmul_group(index, spread_ref, targets_ref, rows):
    both = jnp.dot(spread_ref[2 * rows * index : 2 * rows * (index + 1), :], targets_ref[...], preferred_element_type=F32)
    return both[:rows] + both[rows:]


def factor_columns(kappa_ref, thickness_ref, keep, carry_ref, pivot_ref, ratio_ref):
    levels = keep.shape[0]
    interface = [kappa_ref[i : i + 1, :] * keep[i : i + 1] * keep[i + 1 : i + 2] for i in range(levels - 1)]
    ratio = None
    for level in range(levels):
        thick = thickness_ref[level : level + 1, :]
        pivot = jnp.ones_like(thick)
        if level < levels - 1:
            pivot = pivot + interface[level] / thick
        if level > 0:
            pivot = pivot + interface[level - 1] / thick
            low = -interface[level - 1] / thickness_ref[level - 1 : level, :]
            pivot = pivot - low * ratio
        inverse = 1.0 / pivot
        carry_ref[level : level + 1, :] = low * inverse if level > 0 else jnp.zeros_like(thick)
        pivot_ref[level : level + 1, :] = keep[level : level + 1] * inverse
        if level < levels - 1:
            ratio = -interface[level] / thickness_ref[level + 1 : level + 2, :] * inverse
            ratio_ref[level : level + 1, :] = ratio
        else:
            ratio_ref[level : level + 1, :] = jnp.zeros_like(thick)


def lane_group(shape, width):
    return lax.broadcasted_iota(jnp.int32, shape, 1) // width


def pick(plane, lanes):
    return jnp.take_along_axis(plane, lanes, axis=1, mode="promise_in_bounds")


def rim_lanes(rim_ref, row, halo, shape):
    slot = lax.broadcasted_iota(jnp.int32, shape, 1) % halo
    columns = jnp.zeros(shape, jnp.int32)
    for index in range(halo):
        columns = jnp.where(slot == index, rim_ref[row, index], columns)
    return columns


def rim_coefficients(planes, neighbours, columns, first, halo):
    group = lane_group(columns.shape, halo)
    packed = jnp.zeros(columns.shape, F32)
    for index, plane in enumerate(planes):
        packed = jnp.where(group == index, pick(plane, columns), packed)
    slot = pick(neighbours, columns) - first
    slot = jnp.where((slot >= 0) & (slot < halo), slot, -1)
    return jnp.where(group == len(planes), slot.astype(F32), packed)


def padded_links(neighbours_ref, rows):
    links, columns = neighbours_ref.shape
    padded = jnp.concatenate([neighbours_ref[...], jnp.zeros((8 - links, columns), jnp.int32)], axis=0)
    if rows > 8:
        padded = jnp.concatenate([padded, jnp.zeros((rows - 8, columns), jnp.int32)], axis=0)
    return padded


def pack_slots(levels):
    lane = lax.broadcasted_iota(jnp.int32, levels[0].shape, 1)

    def pair(blocks, mask, turn):
        return [jnp.where(mask, a, pltpu.roll(b, turn % LANES, 1)) for a, b in zip(blocks[::2], blocks[1::2])]

    upper = lane % 64 >= 32
    first_of_two = lane // 16 % 2 == 0
    eights = pair(pair(levels, lane // 8 % 2 == 0, 8), upper, -32)
    fours = pair(pair(pair(levels, lane // 4 % 2 == 0, 4), lane // 8 % 2 == 1, -8), upper, -32)
    blocks = eights + fours
    return pair(blocks, first_of_two, 16), pair(blocks, ~first_of_two, -16)


def unpack_slots(left, right, upper):
    lane = lax.broadcasted_iota(jnp.int32, left[0].shape, 1)
    first_of_two = lane // 16 % 2 == 0

    def turned(block, turn):
        return pltpu.roll(block, turn % LANES, 1) if turn else block

    def apart(blocks, first, second):
        return [turned(block, turn) for block in blocks for turn in (first, second)]

    blocks = []
    for a, b in zip(left, right):
        blocks.append(jnp.where(first_of_two, a, b))
        blocks.append(jnp.where(first_of_two, turned(a, -16), turned(b, 16)))
    blocks = apart(blocks, 0, 32) if upper else apart(blocks, -32, 0)
    eights = apart(blocks[: SPAN // 2], 0, -8)
    fours = apart(apart(blocks[SPAN // 2 :], 0, 8), 0, -4)
    return [jnp.where(lane % 16 < PIECES[1][1], a, b) for a, b in zip(eights, fours)]


def edge_kernel(halo, counts_ref, rim_ref, basis_ref, weights_in, kappa_in, thickness_in, depth_in, neighbours_in,
                outer_ref, inner_ref, mirror_ref, field_ref, live_ref, self_ref, carry_ref, pivot_ref, ratio_ref, table_ref,
                near_ref, leave_ref, spread_ref, spread_two_ref, forward_ref, plane_ref, chunk_ref, weights_ref, kappa_ref,
                thickness_ref, depth_ref, neighbours_ref, sems, small_sems):
    small = [(weights_in, weights_ref), (kappa_in, kappa_ref), (thickness_in, thickness_ref), (depth_in, depth_ref), (neighbours_in, neighbours_ref)]
    small = [pltpu.make_async_copy(a, b, small_sems.at[i]) for i, (a, b) in enumerate(small)]
    for copy in small:
        copy.start()
    vectors, levels, columns = basis_ref.shape
    links = weights_ref.shape[0]
    half = vectors // 2
    chunks = chunk_ref.shape[0]
    step = levels // chunks
    copies = [pltpu.make_async_copy(basis_ref.at[:, step * i : step * (i + 1), :], chunk_ref.at[i], sems.at[i]) for i in range(chunks)]
    for copy in copies:
        copy.start()
    for copy in small:
        copy.wait()
    shape = (levels, columns)
    lane = lax.broadcasted_iota(jnp.int32, shape, 1)
    live = (lane < counts_ref[0]) | (lane >= columns - 2 * halo)
    keep = jnp.where(live & (lax.broadcasted_iota(jnp.int32, shape, 0) < depth_ref[...]), 1.0, 0.0)
    total = weights_ref[0]
    for link in range(1, links):
        total = total + weights_ref[link]
    self_ref[...] = keep * (1.0 - total)
    for link in range(links):
        live_ref[link] = keep * weights_ref[link]
    factor_columns(kappa_ref, thickness_ref, keep, carry_ref, pivot_ref, ratio_ref)

    def near(value, other):
        lanes = lax.broadcasted_iota(jnp.int32, value.shape, 1)
        return jnp.where((lanes >= columns // 4) & (lanes < 3 * columns // 4), pltpu.roll(other, columns // 2, 1), value)

    named = padded_links(neighbours_ref, 8)
    lane8 = lane[0:8]
    near_links = near(named.astype(F32), named.astype(F32)).astype(jnp.int32)
    second = (lane8 >= columns // 4) & (lane8 < 3 * columns // 4)
    first_rim = near_links < halo
    last_rim = (near_links >= columns - halo) & (near_links < columns + 2 * halo)
    hit = jnp.where(first_rim, near_links, jnp.where(last_rim, near_links - columns + 2 * halo, -1))
    hit = jnp.where((hit >= 0) & second, hit + columns // 2, hit)
    for link, matrix in enumerate(one_hot(hit, columns)[:links]):
        near_ref[link * columns : (link + 1) * columns, :] = matrix
    part8 = lane_group((8, columns), halo) % 4
    slot8 = lane8 % halo
    rim_column = jnp.where(part8 % 2 == 0, slot8, columns - halo + slot8)
    leaving = pick(named, rim_column)
    leaving = jnp.where(leaving >= columns, leaving - columns + 2 * halo + lane8 // (4 * halo) * (4 * halo), -1)
    leaving = jnp.where((part8 < 2) == (lax.broadcasted_iota(jnp.int32, (8, columns), 0) < links // 2), leaving, -1)
    matrices = one_hot(leaving, columns)
    for link in range(links // 2):
        leave_ref[link * columns : (link + 1) * columns, :] = matrices[link] + matrices[link + links // 2]

    for link in range(links):
        plane_ref[link] = near(live_ref[link], live_ref[link])
    plane_ref[links] = near(self_ref[...], self_ref[...])
    part = lane_group(shape, halo) % 4
    slot = lane % halo
    rim_column = jnp.where(part % 2 == 0, slot, columns - halo + slot)
    for index, ref in enumerate((carry_ref, pivot_ref, ratio_ref)):
        plane_ref[links + 1 + index] = jnp.where(part < 2, pick(ref[...], rim_column), 0.0)
    for link in range(links // 2):
        other = pick(live_ref[link + links // 2], rim_column)
        plane_ref[links + 4 + link] = jnp.where(part < 2, pick(live_ref[link], rim_column), other)

    def spread(value, level, wide, planes, target_ref):
        at = level // wide * 2 * wide * half + level % wide * half
        for index, plane in enumerate(planes):
            top, low = split(value * plane_ref[plane, level : level + 1, :])
            cols = slice(index * columns, (index + 1) * columns)
            target_ref[at : at + half, cols] = top
            target_ref[at + wide * half : at + (wide + 1) * half, cols] = low

    wide = levels // 4
    rows = wide * half
    part_half = lane_group((half, columns), halo) % 4
    even = lax.axis_index(AXES) % 2 == 0
    table_ref[0:8, :] = named
    table_ref[8:16, :] = rim_lanes(rim_ref, 1, halo, (8, columns))
    table_ref[16:24, :] = rim_lanes(rim_ref, 0, halo, (8, columns))

    total_rows = levels // SPAN * 3 * half

    def send(first, levels_of):
        left, right = pack_slots(levels_of)
        for index in range(len(left)):
            at = first + index * half
            outer_ref[at : at + half, :] = jnp.where(even, left[index], right[index])
            inner_ref[at : at + half, :] = jnp.where(even, right[index], left[index])

    def enter(index):
        own = []
        for level in range(index * wide, (index + 1) * wide):
            value = chunk_ref[level // step, :, level % step, :]
            field_ref[level] = value
            value = near(value[:half], value[half:])
            spread(value, level, wide, range(links), spread_ref)
            value = value * plane_ref[links, level : level + 1, :]
            own.append(jnp.where(part_half == 0, value, pltpu.roll(value, 2 * halo, 1)))
        return matmul_group(index, spread_ref, near_ref, rows), own

    for copy in copies:
        copy.wait()
    above = None
    ready = enter(0)
    for index in range(levels // wide):
        moved, own = ready
        if index + 1 < levels // wide:
            ready = enter(index + 1)
        slots = [moved[i * half : (i + 1) * half] for i in range(wide)]
        for level in range(index * wide, (index + 1) * wide):
            value = slots[level - index * wide]
            mirror_ref[level] = value
            value = (value + own[level - index * wide]) * plane_ref[links + 2, level : level + 1, :]
            if level > 0:
                value = value - plane_ref[links + 1, level : level + 1, :] * above
            forward_ref[level] = value
            above = value
        if (index + 1) * wide % SPAN == 0:
            last = (index + 1) * wide
            send((last // SPAN - 1) * 3 * half, [mirror_ref[level] for level in range(last - SPAN, last)])

    below = None
    for index in range(levels // wide - 1, -1, -1):
        span = range(index * wide, (index + 1) * wide)
        for level in reversed(span):
            value = forward_ref[level]
            if below is not None:
                value = value - plane_ref[links + 3, level : level + 1, :] * below
            below = value
            value = jnp.where(part_half < 2, value, pltpu.roll(value, 2 * halo, 1))
            spread(value, level, wide, range(links + 4, links + 4 + links // 2), spread_two_ref)
        moved = matmul_group(index, spread_two_ref, leave_ref, rows)
        for level in span:
            forward_ref[level] = moved[(level - index * wide) * half : (level - index * wide + 1) * half]
        if index * wide % SPAN == 0:
            first = index * wide
            send(total_rows + first // SPAN * 3 * half, [forward_ref[level] for level in range(first, first + SPAN)])
    planes = [carry_ref[...], pivot_ref[...], ratio_ref[...]] + [live_ref[link] for link in range(links)]
    neighbours = padded_links(neighbours_ref, levels)
    left = rim_coefficients(planes, neighbours, rim_lanes(rim_ref, 1, halo, shape), columns, halo)
    right = rim_coefficients(planes, neighbours, rim_lanes(rim_ref, 0, halo, shape), columns + halo, halo)
    outer_ref[2 * total_rows :, :] = jnp.where(even, left, right)
    inner_ref[2 * total_rows :, :] = jnp.where(even, right, left)


def block_kernel(table_ref, field_ref, live_ref, self_ref, carry_ref, pivot_ref, ratio_ref, moved_ref, stack_ref, gram_ref,
                 matrix_ref, forward_ref):
    levels, vectors, columns = field_ref.shape
    links = live_ref.shape[0]
    row = lax.broadcasted_iota(jnp.int32, (columns, columns), 0)
    own = row == lax.broadcasted_iota(jnp.int32, (columns, columns), 1)

    def move(terms, level):
        both = lax.dot_general(terms, matrix_ref[level], NT, preferred_element_type=F32)
        both = both[:, :columns] + both[:, columns:]
        return both[:vectors] + both[vectors:]

    above = None
    for level in range(levels):
        matrix = jnp.where(own, self_ref[level : level + 1, :], 0.0)
        for link in range(links):
            matrix = matrix + jnp.where(table_ref[link : link + 1, :] == row, live_ref[link, level : level + 1, :], 0.0)
        matrix_ref[level, 0:columns, :], matrix_ref[level, columns:, :] = split(matrix)
        stack_terms(field_ref[level], level, stack_ref)
        value = move(stack_ref[:, level * columns : (level + 1) * columns], level) * pivot_ref[level : level + 1, :]
        if level > 0:
            value = value - carry_ref[level : level + 1, :] * above
        forward_ref[level] = value
        above = value
    below = None
    for level in range(levels - 1, -1, -1):
        value = forward_ref[level]
        if below is not None:
            value = value - ratio_ref[level : level + 1, :] * below
        below = value
        moved_ref[level] = move(jnp.concatenate(split(value), axis=0), level)
    gram = None
    span = levels * columns // 4
    for index in range(4):
        part = stacked_products(stack_ref, stack_ref, span * index, span * (index + 1))
        gram = part if gram is None else gram + part
    gram_ref[...] = join_products(gram)


def stack_terms(value, level, stack_ref):
    vectors, columns = value.shape
    top, low = split(value)
    cols = slice(level * columns, (level + 1) * columns)
    stack_ref[0:vectors, cols] = top
    stack_ref[vectors:, cols] = low


def stacked_products(a_ref, b_ref, first, last):
    return lax.dot_general(a_ref[:, first:last], b_ref[:, first:last], NT, preferred_element_type=F32)


def join_products(products):
    half = products.shape[0] // 2
    return products[:half, :half] + (products[:half, half:] + products[half:, :half])


def second_kernel(halo, outer_ref, inner_ref, mirror_ref, stack_ref, moved_ref, live_ref,
                  self_ref, carry_ref, pivot_ref, ratio_ref, table_ref, gram_ref, image_ref, sums_ref,
                  plane_ref, target_ref, rim_field_ref, spread_ref, came_ref, forward_ref, images_ref):
    levels, vectors, columns = moved_ref.shape
    links = live_ref.shape[0]
    half = vectors // 2
    rows = levels // SPAN * 3 * half
    even = lax.axis_index(AXES) % 2 == 0
    outer = outer_ref[...]
    inner = inner_ref[...]
    from_left = jnp.where(even, outer, inner)
    from_right = jnp.where(even, inner, outer)

    def parts_of(shape):
        return lane_group(shape, halo) % 4

    shape = (levels, columns)
    part = parts_of(shape)
    slot = lax.broadcasted_iota(jnp.int32, shape, 1) % halo
    lead = table_ref[8:16, :]
    trail = table_ref[16:24, :]
    own_column = jnp.concatenate([jnp.where(part[0:8] % 2 == 0, trail, lead)] * (levels // 8), axis=0)
    planes = [carry_ref[...], pivot_ref[...], ratio_ref[...]] + [live_ref[link] for link in range(links)]
    for index, plane in enumerate(planes):
        theirs = jnp.where(part == 2, pick(from_left[2 * rows :], slot + halo * index), pick(from_right[2 * rows :], slot + halo * index))
        plane_ref[index] = jnp.where(part < 2, pick(plane, own_column), theirs)
    plane_ref[len(planes)] = pick(self_ref[...], own_column)
    plane_ref[1] = jnp.where(slot < REACH, plane_ref[1], 0.0)

    shape = (8, columns)
    part, slot, own_column = part[0:8], slot[0:8], own_column[0:8]
    named = pick(table_ref[0:8, :], own_column)
    from_links = slot + halo * len(planes)
    theirs = jnp.where(part == 2, pick(from_left[2 * rows : 2 * rows + 8], from_links), pick(from_right[2 * rows : 2 * rows + 8], from_links)).astype(jnp.int32)
    facing = jnp.where(part == 2, pick(lead, jnp.maximum(theirs, 0)), pick(trail, jnp.maximum(theirs, 0)))
    target = jnp.where(part < 2, jnp.where(named < columns, named, -1), jnp.where(theirs >= 0, facing, -1))
    link_row = lax.broadcasted_iota(jnp.int32, shape, 0)
    target = jnp.where(link_row == links, jnp.where((part < 2) | (slot < REACH), own_column, -1), target)
    lane = lax.broadcasted_iota(jnp.int32, shape, 1)
    links_of = jnp.where(link_row < links, table_ref[0:8, :], lane)
    far = (links_of >= columns) & (links_of < columns + halo) & (lane >= halo)
    far = far | ((links_of >= columns + halo) & (lane < columns - halo))
    far = far | ((links_of >= columns) & ((links_of - columns) % halo >= REACH))
    far = far | ((links_of < halo) & (lane >= 2 * halo))
    far = far | ((links_of >= columns - halo) & (links_of < columns) & (lane < columns - 2 * halo))
    far = jnp.sum(jnp.where(far, 1.0, 0.0), axis=1, keepdims=True)
    far = jnp.sum(far, axis=0, keepdims=True)
    first_half = lax.broadcasted_iota(jnp.int32, (columns, columns), 0) < 4 * halo
    for link, matrix in enumerate(one_hot(target, columns)[: links + 1]):
        at = slice(link * columns, (link + 1) * columns)
        target_ref[at, 0:columns] = jnp.where(first_half, matrix, jnp.zeros_like(matrix))
        target_ref[at, columns:] = jnp.where(first_half, jnp.zeros_like(matrix), matrix)

    half_part = parts_of((half, columns))

    def came_in(first, upper):
        came = []
        for start in range(first, first + rows, 3 * half):
            cut = [slice(start + i * half, start + (i + 1) * half) for i in range(3)]
            came += unpack_slots([from_right[c] for c in cut], [from_left[c] for c in cut], upper)
        return came

    early = came_in(0, False)
    late = came_in(rows, True)
    above = None
    for level in range(levels):
        value = jnp.where(half_part < 2, early[level], mirror_ref[level])
        value = value * plane_ref[1, level : level + 1, :]
        if level > 0:
            value = value - plane_ref[0, level : level + 1, :] * above
        rim_field_ref[level] = value
        above = value
    wide = levels // 4
    span = wide * half
    below = None
    for index in range(levels // wide - 1, -1, -1):
        for level in range((index + 1) * wide - 1, index * wide - 1, -1):
            value = rim_field_ref[level]
            if below is not None:
                value = value - plane_ref[2, level : level + 1, :] * below
            below = value
            at = 2 * span * index + level % wide * half
            for link in range(links + 1):
                term = value * plane_ref[3 + link, level : level + 1, :]
                if link == links:
                    term = jnp.where(half_part < 2, term, late[level])
                top, low = split(term)
                cols = slice(link * columns, (link + 1) * columns)
                spread_ref[at : at + half, cols] = top
                spread_ref[at + span : at + span + half, cols] = low
        both = jnp.dot(spread_ref[2 * span * index : 2 * span * (index + 1), :], target_ref[...], preferred_element_type=F32)
        came_ref[span * index : span * (index + 1), :] = both[:span] + both[span:]

    above = None
    for level in range(levels):
        rows = slice(level * half, (level + 1) * half)
        came = jnp.concatenate([came_ref[rows, :columns], came_ref[rows, columns:]], axis=0)
        value = (moved_ref[level] + came) * pivot_ref[level : level + 1, :]
        if level > 0:
            value = value - carry_ref[level : level + 1, :] * above
        forward_ref[level] = value
        above = value

    products = None
    square = jnp.zeros((vectors, columns), F32)
    below = None
    for index in range(levels // wide - 1, -1, -1):
        for level in range((index + 1) * wide - 1, index * wide - 1, -1):
            value = forward_ref[level]
            if below is not None:
                value = value - ratio_ref[level : level + 1, :] * below
            below = value
            image_ref[level] = value
            square = square + value * value
            stack_terms(value, level, images_ref)
        part = stacked_products(images_ref, stack_ref, wide * index * columns, wide * (index + 1) * columns)
        products = part if products is None else products + part
    cross = join_products(products)
    sums_ref[0:vectors, 0:vectors] = cross
    sums_ref[0:vectors, vectors : 2 * vectors] = gram_ref[...]
    norm = jnp.sum(square, axis=1, keepdims=True)
    shape = (vectors, 2 * vectors)
    eye = lax.broadcasted_iota(jnp.int32, shape, 0) == lax.broadcasted_iota(jnp.int32, shape, 1)
    norm = jnp.sum(jnp.where(eye, norm, 0.0), axis=0, keepdims=True)
    shape = (8, 2 * vectors)
    sums_ref[vectors : vectors + 8, :] = jnp.where(lax.broadcasted_iota(jnp.int32, shape, 0) == 0, norm, far)


def weigh_kernel(cells, sums_ref, more_ref, spans_ref, scale_ref, coupling_ref, direct_ref):
    vectors = coupling_ref.shape[0]
    sums = sums_ref[...] + more_ref[...]
    cross = sums[0:vectors, 0:vectors] / cells
    gram = sums[0:vectors, vectors : 2 * vectors] / cells
    coupling_ref[...] = cross.T
    shape = (vectors, vectors)
    eye = lax.broadcasted_iota(jnp.int32, shape, 0) == lax.broadcasted_iota(jnp.int32, shape, 1)
    square = sums[vectors : vectors + 1, 0:vectors] / cells
    square = jnp.sum(jnp.where(eye, square, 0.0), axis=1, keepdims=True)
    mixed = dot3(cross, gram, (((1,), (0,)), ((), ())))
    spanned = jnp.sum(cross * mixed, axis=1, keepdims=True)
    shared = 2.0 * jnp.sum(cross * cross, axis=1, keepdims=True)
    norm = square - shared + spanned
    small = norm + 1e-6 < 1e-2 * (square + shared + jnp.abs(spanned))
    scale_ref[...] = jnp.broadcast_to(1.0 / jnp.sqrt(jnp.maximum(norm, 0.0) + 1e-6), scale_ref.shape)
    far = jnp.sum(sums[vectors + 1 : vectors + 2, 0:1])
    direct_ref[0] = jnp.where(far + jnp.sum(jnp.where(small, 1.0, 0.0)) > 0.0, 1, 0)
    top, low = split(cross)
    spans_ref[...] = jnp.concatenate([jnp.concatenate([top, top], axis=1), jnp.concatenate([low, low], axis=1)], axis=0)


def last_kernel(spans_ref, scale_ref, image_ref, stack_ref, sums_ref, next_ref, coupling_ref, chunk_ref, sems):
    levels, vectors, columns = image_ref.shape
    chunks = chunk_ref.shape[0]
    step = levels // chunks
    copies = [pltpu.make_async_copy(chunk_ref.at[i], next_ref.at[:, step * i : step * (i + 1), :], sems.at[i]) for i in range(chunks)]
    copies.append(pltpu.make_async_copy(sums_ref, coupling_ref, sems.at[chunks]))
    copies[chunks].start()
    def spanned_by(index):
        cols = slice(step * index * columns, step * (index + 1) * columns)
        both = jnp.dot(spans_ref[...], stack_ref[:, cols], preferred_element_type=F32)
        return both[:vectors] + both[vectors:]

    ready = spanned_by(0)
    for index in range(chunks):
        spanned = ready
        if index + 1 < chunks:
            ready = spanned_by(index + 1)
        for level in range(step):
            at = level * columns
            chunk_ref[index, :, level, :] = (image_ref[step * index + level] - spanned[:, at : at + columns]) * scale_ref[...]
        copies[index].start()
    for copy in copies:
        copy.wait()


VMEM = pl.BlockSpec(memory_space=pltpu.VMEM)
SMEM = pl.BlockSpec(memory_space=pltpu.SMEM)
ANY = pl.BlockSpec(memory_space=pl.ANY)


def call(kernel, outs, out_specs, scratch, specs, *operands):
    return pl.pallas_call(
        kernel,
        out_shape=outs,
        in_specs=specs,
        out_specs=out_specs,
        scratch_shapes=scratch,
        compiler_params=pltpu.CompilerParams(vmem_limit_bytes=40 << 20),
    )(*operands)


def exchange(outer, inner):
    blocks = lax.axis_size(AXES)
    outer = lax.ppermute(outer, AXES, [(i, (i - 1) % blocks if i % 2 == 0 else (i + 1) % blocks) for i in range(blocks)])
    inner = lax.ppermute(inner, AXES, [(i, i ^ 1) for i in range(blocks)])
    return outer, inner


def almost_total(value):
    blocks = lax.axis_size(AXES)
    if blocks & (blocks - 1):
        return lax.psum(value, AXES), jnp.zeros_like(value)
    distance = 2
    while distance < blocks:
        value = value + lax.ppermute(value, AXES, [(i, i ^ distance) for i in range(blocks)])
        distance *= 2
    more = lax.ppermute(value, AXES, [(i, i ^ 1) for i in range(blocks)])
    return value, more


def shards(basis, weights, kappa, thickness, depth, neighbours, rim_lists, counts):
    vectors, levels, columns = basis.shape
    links = weights.shape[0]
    halo = rim_lists.shape[1]
    rows = levels // SPAN * 3 * vectors // 2
    chunks = 4

    def out(*shape, dtype=F32):
        return jax.ShapeDtypeStruct(shape, dtype)

    message = out(2 * rows + levels, LANES)
    whole = out(levels, vectors, columns)
    halved = out(levels, vectors // 2, columns)
    plane = out(levels, columns)
    forward = pltpu.VMEM((levels, vectors, columns), F32)
    half_forward = pltpu.VMEM((levels, vectors // 2, columns), F32)
    chunk = pltpu.VMEM((chunks, vectors, levels // chunks, columns), F32)
    sems = pltpu.SemaphoreType.DMA((chunks,))
    cells = levels * vectors
    table = out(24, columns, dtype=jnp.int32)
    outer, inner, mirror, field, live, self_weight, carry, pivot, ratio, table = call(
        functools.partial(edge_kernel, halo),
        (message, message, halved, whole, out(links, levels, columns), plane, plane, plane, plane, table), [VMEM] * 10,
        [pltpu.VMEM((links * columns, columns), BF16), pltpu.VMEM((links // 2 * columns, columns), BF16),
         pltpu.VMEM((cells, links * columns), BF16), pltpu.VMEM((cells, links // 2 * columns), BF16),
         half_forward, pltpu.VMEM((links + 4 + links // 2, levels, columns), F32), chunk,
         pltpu.VMEM((links, levels, columns), F32), pltpu.VMEM((levels, columns), F32), pltpu.VMEM((levels, columns), F32),
         pltpu.VMEM((1, columns), jnp.int32), pltpu.VMEM((links, columns), jnp.int32), sems, pltpu.SemaphoreType.DMA((5,))],
        [SMEM] * 2 + [ANY] * 6,
        counts, rim_lists, basis, weights, kappa, thickness, depth.reshape(1, columns), neighbours)
    outer, inner = exchange(outer, inner)
    moved, stack, gram = call(
        block_kernel,
        (whole, out(2 * vectors, levels * columns, dtype=BF16), out(vectors, vectors)), [VMEM] * 3,
        [pltpu.VMEM((levels, 2 * columns, columns), BF16), forward],
        [VMEM] * 7, table, field, live, self_weight, carry, pivot, ratio)
    image, sums = call(
        functools.partial(second_kernel, halo), (whole, out(vectors + 8, 2 * vectors)), [VMEM] * 2,
        [pltpu.VMEM((links + 4, levels, columns), F32), pltpu.VMEM(((links + 1) * columns, 2 * columns), BF16), half_forward,
         pltpu.VMEM((cells, (links + 1) * columns), BF16), pltpu.VMEM((cells // 2, 2 * columns), F32),
         forward, pltpu.VMEM((2 * vectors, levels * columns), BF16)],
        [VMEM] * 12,
        outer, inner, mirror, stack, moved, live, self_weight, carry, pivot, ratio, table, gram)
    sums, more = almost_total(sums)
    cells = float(levels * columns * lax.axis_size(AXES))
    spans, scale, coupling, direct = call(
        functools.partial(weigh_kernel, cells),
        (out(2 * vectors, 2 * vectors, dtype=BF16), out(vectors, columns), out(vectors, vectors), out(1, dtype=jnp.int32)),
        [VMEM] * 3 + [SMEM], [], [VMEM] * 2, sums, more)

    def from_sums():
        return call(last_kernel, (out(vectors, levels, columns), out(vectors, vectors)), [ANY] * 2,
                    [chunk, pltpu.SemaphoreType.DMA((chunks + 1,))], [VMEM] * 5, spans, scale, image, stack, coupling)

    def from_scratch():
        return direct_form(basis, weights, kappa, thickness, depth, neighbours, rim_lists, counts)

    return tuple(lax.cond(direct[0] > 0, from_scratch, lambda: tuple(from_sums())))


ITERS = 2


def from_behind(block, axis, distance):
    devices = range(lax.axis_size(axis))
    route = [((i - distance) % len(devices), i) for i in devices]
    return lax.ppermute(block, axis, route)


def column_factors(kappa, thickness, keep):
    levels = kappa.shape[0]
    below = jnp.concatenate([keep[1:], jnp.zeros_like(keep[:1])], axis=0)
    interface = kappa * keep * below
    lower, inv_pivot, ratio = ([], [], [])
    for level in range(levels):
        upper_term = interface[level]
        diag_term = 1.0 + upper_term / thickness[level]
        if level > 0:
            diag_term = diag_term + interface[level - 1] / thickness[level]
            low = -interface[level - 1] / thickness[level - 1]
        else:
            low = jnp.zeros_like(upper_term)
        if level < levels - 1:
            upp = -upper_term / thickness[level + 1]
        else:
            upp = jnp.zeros_like(upper_term)
        pivot = diag_term - low * ratio[level - 1] if level > 0 else diag_term
        inverse = 1.0 / pivot
        lower.append(low)
        inv_pivot.append(inverse)
        ratio.append(upp * inverse)
    return (lower, inv_pivot, ratio)


def column_solve(rhs, lower, inv_pivot, ratio):
    levels = rhs.shape[1]
    forward = []
    for level in range(levels):
        if level == 0:
            forward.append(rhs[:, 0] * inv_pivot[0])
        else:
            forward.append((rhs[:, level] - lower[level] * forward[level - 1]) * inv_pivot[level])
    result = [None] * levels
    result[levels - 1] = forward[levels - 1]
    for level in range(levels - 2, -1, -1):
        result[level] = forward[level] - ratio[level] * result[level + 1]
    return jnp.stack(result, axis=1)


def transport_back(field, weights, keep, self_weight, neighbours, rim_lists):
    columns = field.shape[2]
    halo_width = rim_lists.shape[1]
    masked = keep * field
    extended = jnp.zeros((field.shape[0], field.shape[1], columns + 2 * halo_width), jnp.float32)
    for link in range(weights.shape[0]):
        extended = extended.at[:, :, neighbours[link]].add(weights[link] * masked)
    from_right = from_behind(extended[:, :, columns : columns + halo_width], ("region", "sub"), -1)
    from_left = from_behind(extended[:, :, columns + halo_width :], ("region", "sub"), 1)
    result = self_weight * masked + extended[:, :, :columns]
    result = result.at[:, :, rim_lists[0]].add(from_right).at[:, :, rim_lists[1]].add(from_left)
    return keep * result


def direct_form(basis, weights, kappa, thickness, depth, neighbours, rim_lists, counts):
    vectors, levels, columns = basis.shape
    halo_width = rim_lists.shape[1]
    own_index = jnp.arange(columns, dtype=jnp.int32)
    live = (own_index < counts[0]) | (own_index >= columns - 2 * halo_width)
    wet = jnp.arange(levels, dtype=jnp.int32)[:, None] < depth[None, :]
    keep = (live[None, :] & wet).astype(jnp.float32)
    self_weight = 1.0 - jnp.sum(weights, axis=0)
    lower, inv_pivot, ratio = column_factors(kappa, thickness, keep)
    field = basis
    for step in range(ITERS):
        moved = transport_back(field, weights, keep, self_weight, neighbours, rim_lists)
        field = column_solve(keep * moved, lower, inv_pivot, ratio)
    cells = float(levels * columns * lax.axis_size(("region", "sub")))
    high = lax.Precision.HIGHEST
    local_cross = jnp.einsum("ilc,jlc->ij", basis, field, precision=high)
    coupling = lax.psum(local_cross, ("region", "sub")) / cells
    residual = field - jnp.einsum("ilc,ij->jlc", basis, coupling, precision=high)
    local_norms = jnp.einsum("jlc,jlc->j", residual, residual, precision=high)
    norms = lax.psum(local_norms, ("region", "sub")) / cells
    next_basis = residual / jnp.sqrt(norms + 1e-06)[:, None, None]
    return (next_basis, coupling)


def solution(mesh):
    placed = (
        P("groups", None, AXES),
        P(None, None, AXES),
        P(None, AXES),
        P(None, AXES),
        P(AXES),
        P(None, AXES),
        P(None, AXES),
        P(AXES),
    )
    return jax.shard_map(
        shards,
        mesh=mesh,
        in_specs=placed,
        out_specs=(P("groups", None, AXES), P("groups", None)),
        check_vma=False,
    )
```

```python
import functools

import jax
import jax.numpy as jnp
from jax import lax
from jax.experimental import pallas as pl
from jax.experimental.pallas import tpu as pltpu
from jax.sharding import PartitionSpec as P

AXES = ("region", "sub")
LANES = 128
PIECES = ((8, 0), (4, 8))
REACH = 12
SPAN = 16
F32 = jnp.float32
BF16 = jnp.bfloat16
NT = (((1,), (1,)), ((), ()))


def split(x):
    top = x.astype(BF16)
    return top, (x - top.astype(F32)).astype(BF16)


def dot3(a, b, dims):
    a_top, a_low = split(a)
    b_top, b_low = split(b)
    dot = functools.partial(lax.dot_general, dimension_numbers=dims, preferred_element_type=F32)
    return dot(a_top, b_top) + (dot(a_top, b_low) + dot(a_low, b_top))


def one_hot(hits, size):
    by_lane = hits.astype(F32).T
    lanes = by_lane.shape[0]
    column = lax.broadcasted_iota(jnp.int32, (lanes, size), 1).astype(F32)
    return [jnp.where(jnp.broadcast_to(by_lane[:, i : i + 1], (lanes, size)) == column, 1.0, 0.0).astype(BF16) for i in range(hits.shape[0])]


def matmul_group(index, spread_ref, targets_ref, rows):
    both = jnp.dot(spread_ref[2 * rows * index : 2 * rows * (index + 1), :], targets_ref[...], preferred_element_type=F32)
    return both[:rows] + both[rows:]


def factor_columns(kappa_ref, thickness_ref, keep, carry_ref, pivot_ref, ratio_ref):
    levels = keep.shape[0]
    interface = [kappa_ref[i : i + 1, :] * keep[i : i + 1] * keep[i + 1 : i + 2] for i in range(levels - 1)]
    ratio = None
    for level in range(levels):
        thick = thickness_ref[level : level + 1, :]
        pivot = jnp.ones_like(thick)
        if level < levels - 1:
            pivot = pivot + interface[level] / thick
        if level > 0:
            pivot = pivot + interface[level - 1] / thick
            low = -interface[level - 1] / thickness_ref[level - 1 : level, :]
            pivot = pivot - low * ratio
        inverse = 1.0 / pivot
        carry_ref[level : level + 1, :] = low * inverse if level > 0 else jnp.zeros_like(thick)
        pivot_ref[level : level + 1, :] = keep[level : level + 1] * inverse
        if level < levels - 1:
            ratio = -interface[level] / thickness_ref[level + 1 : level + 2, :] * inverse
            ratio_ref[level : level + 1, :] = ratio
        else:
            ratio_ref[level : level + 1, :] = jnp.zeros_like(thick)


def lane_group(shape, width):
    return lax.broadcasted_iota(jnp.int32, shape, 1) // width


def pick(plane, lanes):
    return jnp.take_along_axis(plane, lanes, axis=1, mode="promise_in_bounds")


def rim_lanes(rim_ref, row, halo, shape):
    slot = lax.broadcasted_iota(jnp.int32, shape, 1) % halo
    columns = jnp.zeros(shape, jnp.int32)
    for index in range(halo):
        columns = jnp.where(slot == index, rim_ref[row, index], columns)
    return columns


def rim_coefficients(planes, neighbours, columns, first, halo):
    group = lane_group(columns.shape, halo)
    packed = jnp.zeros(columns.shape, F32)
    for index, plane in enumerate(planes):
        packed = jnp.where(group == index, pick(plane, columns), packed)
    slot = pick(neighbours, columns) - first
    slot = jnp.where((slot >= 0) & (slot < halo), slot, -1)
    return jnp.where(group == len(planes), slot.astype(F32), packed)


def padded_links(neighbours_ref, rows):
    links, columns = neighbours_ref.shape
    padded = jnp.concatenate([neighbours_ref[...], jnp.zeros((8 - links, columns), jnp.int32)], axis=0)
    if rows > 8:
        padded = jnp.concatenate([padded, jnp.zeros((rows - 8, columns), jnp.int32)], axis=0)
    return padded


def pack_slots(levels):
    lane = lax.broadcasted_iota(jnp.int32, levels[0].shape, 1)

    def pair(blocks, mask, turn):
        return [jnp.where(mask, a, pltpu.roll(b, turn % LANES, 1)) for a, b in zip(blocks[::2], blocks[1::2])]

    upper = lane % 64 >= 32
    first_of_two = lane // 16 % 2 == 0
    eights = pair(pair(levels, lane // 8 % 2 == 0, 8), upper, -32)
    fours = pair(pair(pair(levels, lane // 4 % 2 == 0, 4), lane // 8 % 2 == 1, -8), upper, -32)
    blocks = eights + fours
    return pair(blocks, first_of_two, 16), pair(blocks, ~first_of_two, -16)


def unpack_slots(left, right, upper):
    lane = lax.broadcasted_iota(jnp.int32, left[0].shape, 1)
    first_of_two = lane // 16 % 2 == 0

    def turned(block, turn):
        return pltpu.roll(block, turn % LANES, 1) if turn else block

    def apart(blocks, first, second):
        return [turned(block, turn) for block in blocks for turn in (first, second)]

    blocks = []
    for a, b in zip(left, right):
        blocks.append(jnp.where(first_of_two, a, b))
        blocks.append(jnp.where(first_of_two, turned(a, -16), turned(b, 16)))
    blocks = apart(blocks, 0, 32) if upper else apart(blocks, -32, 0)
    eights = apart(blocks[: SPAN // 2], 0, -8)
    fours = apart(apart(blocks[SPAN // 2 :], 0, 8), 0, -4)
    return [jnp.where(lane % 16 < PIECES[1][1], a, b) for a, b in zip(eights, fours)]


def edge_kernel(halo, counts_ref, rim_ref, basis_ref, weights_in, kappa_in, thickness_in, depth_in, neighbours_in,
                outer_ref, inner_ref, mirror_ref, field_ref, live_ref, self_ref, carry_ref, pivot_ref, ratio_ref, table_ref,
                near_ref, leave_ref, spread_ref, spread_two_ref, forward_ref, plane_ref, chunk_ref, weights_ref, kappa_ref,
                thickness_ref, depth_ref, neighbours_ref, sems, small_sems):
    small = [(weights_in, weights_ref), (kappa_in, kappa_ref), (thickness_in, thickness_ref), (depth_in, depth_ref), (neighbours_in, neighbours_ref)]
    small = [pltpu.make_async_copy(a, b, small_sems.at[i]) for i, (a, b) in enumerate(small)]
    for copy in small:
        copy.start()
    vectors, levels, columns = basis_ref.shape
    links = weights_ref.shape[0]
    half = vectors // 2
    chunks = chunk_ref.shape[0]
    step = levels // chunks
    copies = [pltpu.make_async_copy(basis_ref.at[:, step * i : step * (i + 1), :], chunk_ref.at[i], sems.at[i]) for i in range(chunks)]
    for copy in copies:
        copy.start()
    for copy in small:
        copy.wait()
    shape = (levels, columns)
    lane = lax.broadcasted_iota(jnp.int32, shape, 1)
    live = (lane < counts_ref[0]) | (lane >= columns - 2 * halo)
    keep = jnp.where(live & (lax.broadcasted_iota(jnp.int32, shape, 0) < depth_ref[...]), 1.0, 0.0)
    total = weights_ref[0]
    for link in range(1, links):
        total = total + weights_ref[link]
    self_ref[...] = keep * (1.0 - total)
    for link in range(links):
        live_ref[link] = keep * weights_ref[link]
    factor_columns(kappa_ref, thickness_ref, keep, carry_ref, pivot_ref, ratio_ref)

    def near(value, other):
        lanes = lax.broadcasted_iota(jnp.int32, value.shape, 1)
        return jnp.where((lanes >= columns // 4) & (lanes < 3 * columns // 4), pltpu.roll(other, columns // 2, 1), value)

    named = padded_links(neighbours_ref, 8)
    lane8 = lane[0:8]
    near_links = near(named.astype(F32), named.astype(F32)).astype(jnp.int32)
    second = (lane8 >= columns // 4) & (lane8 < 3 * columns // 4)
    first_rim = near_links < halo
    last_rim = (near_links >= columns - halo) & (near_links < columns + 2 * halo)
    hit = jnp.where(first_rim, near_links, jnp.where(last_rim, near_links - columns + 2 * halo, -1))
    hit = jnp.where((hit >= 0) & second, hit + columns // 2, hit)
    for link, matrix in enumerate(one_hot(hit, columns)[:links]):
        near_ref[link * columns : (link + 1) * columns, :] = matrix
    part8 = lane_group((8, columns), halo) % 4
    slot8 = lane8 % halo
    rim_column = jnp.where(part8 % 2 == 0, slot8, columns - halo + slot8)
    leaving = pick(named, rim_column)
    leaving = jnp.where(leaving >= columns, leaving - columns + 2 * halo + lane8 // (4 * halo) * (4 * halo), -1)
    leaving = jnp.where((part8 < 2) == (lax.broadcasted_iota(jnp.int32, (8, columns), 0) < links // 2), leaving, -1)
    matrices = one_hot(leaving, columns)
    for link in range(links // 2):
        leave_ref[link * columns : (link + 1) * columns, :] = matrices[link] + matrices[link + links // 2]

    for link in range(links):
        plane_ref[link] = near(live_ref[link], live_ref[link])
    plane_ref[links] = near(self_ref[...], self_ref[...])
    part = lane_group(shape, halo) % 4
    slot = lane % halo
    rim_column = jnp.where(part % 2 == 0, slot, columns - halo + slot)
    for index, ref in enumerate((carry_ref, pivot_ref, ratio_ref)):
        plane_ref[links + 1 + index] = jnp.where(part < 2, pick(ref[...], rim_column), 0.0)
    for link in range(links // 2):
        other = pick(live_ref[link + links // 2], rim_column)
        plane_ref[links + 4 + link] = jnp.where(part < 2, pick(live_ref[link], rim_column), other)

    def spread(value, level, wide, planes, target_ref):
        at = level // wide * 2 * wide * half + level % wide * half
        for index, plane in enumerate(planes):
            top, low = split(value * plane_ref[plane, level : level + 1, :])
            cols = slice(index * columns, (index + 1) * columns)
            target_ref[at : at + half, cols] = top
            target_ref[at + wide * half : at + (wide + 1) * half, cols] = low

    wide = levels // 4
    rows = wide * half
    part_half = lane_group((half, columns), halo) % 4
    even = lax.axis_index(AXES) % 2 == 0
    table_ref[0:8, :] = named
    table_ref[8:16, :] = rim_lanes(rim_ref, 1, halo, (8, columns))
    table_ref[16:24, :] = rim_lanes(rim_ref, 0, halo, (8, columns))

    total_rows = levels // SPAN * 3 * half

    def send(first, levels_of):
        left, right = pack_slots(levels_of)
        for index in range(len(left)):
            at = first + index * half
            outer_ref[at : at + half, :] = jnp.where(even, left[index], right[index])
            inner_ref[at : at + half, :] = jnp.where(even, right[index], left[index])

    def enter(index):
        own = []
        for level in range(index * wide, (index + 1) * wide):
            value = chunk_ref[level // step, :, level % step, :]
            field_ref[level] = value
            value = near(value[:half], value[half:])
            spread(value, level, wide, range(links), spread_ref)
            value = value * plane_ref[links, level : level + 1, :]
            own.append(jnp.where(part_half == 0, value, pltpu.roll(value, 2 * halo, 1)))
        return matmul_group(index, spread_ref, near_ref, rows), own

    for copy in copies:
        copy.wait()
    above = None
    ready = enter(0)
    for index in range(levels // wide):
        moved, own = ready
        if index + 1 < levels // wide:
            ready = enter(index + 1)
        slots = [moved[i * half : (i + 1) * half] for i in range(wide)]
        for level in range(index * wide, (index + 1) * wide):
            value = slots[level - index * wide]
            mirror_ref[level] = value
            value = (value + own[level - index * wide]) * plane_ref[links + 2, level : level + 1, :]
            if level > 0:
                value = value - plane_ref[links + 1, level : level + 1, :] * above
            forward_ref[level] = value
            above = value
        if (index + 1) * wide % SPAN == 0:
            last = (index + 1) * wide
            send((last // SPAN - 1) * 3 * half, [mirror_ref[level] for level in range(last - SPAN, last)])

    below = None
    for index in range(levels // wide - 1, -1, -1):
        span = range(index * wide, (index + 1) * wide)
        for level in reversed(span):
            value = forward_ref[level]
            if below is not None:
                value = value - plane_ref[links + 3, level : level + 1, :] * below
            below = value
            value = jnp.where(part_half < 2, value, pltpu.roll(value, 2 * halo, 1))
            spread(value, level, wide, range(links + 4, links + 4 + links // 2), spread_two_ref)
        moved = matmul_group(index, spread_two_ref, leave_ref, rows)
        for level in span:
            forward_ref[level] = moved[(level - index * wide) * half : (level - index * wide + 1) * half]
        if index * wide % SPAN == 0:
            first = index * wide
            send(total_rows + first // SPAN * 3 * half, [forward_ref[level] for level in range(first, first + SPAN)])
    planes = [carry_ref[...], pivot_ref[...], ratio_ref[...]] + [live_ref[link] for link in range(links)]
    neighbours = padded_links(neighbours_ref, levels)
    left = rim_coefficients(planes, neighbours, rim_lanes(rim_ref, 1, halo, shape), columns, halo)
    right = rim_coefficients(planes, neighbours, rim_lanes(rim_ref, 0, halo, shape), columns + halo, halo)
    outer_ref[2 * total_rows :, :] = jnp.where(even, left, right)
    inner_ref[2 * total_rows :, :] = jnp.where(even, right, left)


def block_kernel(table_ref, field_ref, live_ref, self_ref, carry_ref, pivot_ref, ratio_ref, moved_ref, stack_ref, gram_ref,
                 matrix_ref, forward_ref):
    levels, vectors, columns = field_ref.shape
    links = live_ref.shape[0]
    row = lax.broadcasted_iota(jnp.int32, (columns, columns), 0)
    own = row == lax.broadcasted_iota(jnp.int32, (columns, columns), 1)

    def move(terms, level):
        both = lax.dot_general(terms, matrix_ref[level], NT, preferred_element_type=F32)
        both = both[:, :columns] + both[:, columns:]
        return both[:vectors] + both[vectors:]

    above = None
    for level in range(levels):
        matrix = jnp.where(own, self_ref[level : level + 1, :], 0.0)
        for link in range(links):
            matrix = matrix + jnp.where(table_ref[link : link + 1, :] == row, live_ref[link, level : level + 1, :], 0.0)
        matrix_ref[level, 0:columns, :], matrix_ref[level, columns:, :] = split(matrix)
        stack_terms(field_ref[level], level, stack_ref)
        value = move(stack_ref[:, level * columns : (level + 1) * columns], level) * pivot_ref[level : level + 1, :]
        if level > 0:
            value = value - carry_ref[level : level + 1, :] * above
        forward_ref[level] = value
        above = value
    below = None
    for level in range(levels - 1, -1, -1):
        value = forward_ref[level]
        if below is not None:
            value = value - ratio_ref[level : level + 1, :] * below
        below = value
        moved_ref[level] = move(jnp.concatenate(split(value), axis=0), level)
    gram = None
    span = levels * columns // 4
    for index in range(4):
        part = stacked_products(stack_ref, stack_ref, span * index, span * (index + 1))
        gram = part if gram is None else gram + part
    gram_ref[...] = join_products(gram)


def stack_terms(value, level, stack_ref):
    vectors, columns = value.shape
    top, low = split(value)
    cols = slice(level * columns, (level + 1) * columns)
    stack_ref[0:vectors, cols] = top
    stack_ref[vectors:, cols] = low


def stacked_products(a_ref, b_ref, first, last):
    return lax.dot_general(a_ref[:, first:last], b_ref[:, first:last], NT, preferred_element_type=F32)


def join_products(products):
    half = products.shape[0] // 2
    return products[:half, :half] + (products[:half, half:] + products[half:, :half])


def second_kernel(halo, outer_ref, inner_ref, mirror_ref, stack_ref, moved_ref, live_ref,
                  self_ref, carry_ref, pivot_ref, ratio_ref, table_ref, gram_ref, image_ref, sums_ref,
                  plane_ref, target_ref, rim_field_ref, spread_ref, came_ref, forward_ref, images_ref):
    levels, vectors, columns = moved_ref.shape
    links = live_ref.shape[0]
    half = vectors // 2
    rows = levels // SPAN * 3 * half
    even = lax.axis_index(AXES) % 2 == 0
    outer = outer_ref[...]
    inner = inner_ref[...]
    from_left = jnp.where(even, outer, inner)
    from_right = jnp.where(even, inner, outer)

    def parts_of(shape):
        return lane_group(shape, halo) % 4

    shape = (levels, columns)
    part = parts_of(shape)
    slot = lax.broadcasted_iota(jnp.int32, shape, 1) % halo
    lead = table_ref[8:16, :]
    trail = table_ref[16:24, :]
    own_column = jnp.concatenate([jnp.where(part[0:8] % 2 == 0, trail, lead)] * (levels // 8), axis=0)
    planes = [carry_ref[...], pivot_ref[...], ratio_ref[...]] + [live_ref[link] for link in range(links)]
    for index, plane in enumerate(planes):
        theirs = jnp.where(part == 2, pick(from_left[2 * rows :], slot + halo * index), pick(from_right[2 * rows :], slot + halo * index))
        plane_ref[index] = jnp.where(part < 2, pick(plane, own_column), theirs)
    plane_ref[len(planes)] = pick(self_ref[...], own_column)
    plane_ref[1] = jnp.where(slot < REACH, plane_ref[1], 0.0)

    shape = (8, columns)
    part, slot, own_column = part[0:8], slot[0:8], own_column[0:8]
    named = pick(table_ref[0:8, :], own_column)
    from_links = slot + halo * len(planes)
    theirs = jnp.where(part == 2, pick(from_left[2 * rows : 2 * rows + 8], from_links), pick(from_right[2 * rows : 2 * rows + 8], from_links)).astype(jnp.int32)
    facing = jnp.where(part == 2, pick(lead, jnp.maximum(theirs, 0)), pick(trail, jnp.maximum(theirs, 0)))
    target = jnp.where(part < 2, jnp.where(named < columns, named, -1), jnp.where(theirs >= 0, facing, -1))
    link_row = lax.broadcasted_iota(jnp.int32, shape, 0)
    target = jnp.where(link_row == links, jnp.where((part < 2) | (slot < REACH), own_column, -1), target)
    lane = lax.broadcasted_iota(jnp.int32, shape, 1)
    links_of = jnp.where(link_row < links, table_ref[0:8, :], lane)
    far = (links_of >= columns) & (links_of < columns + halo) & (lane >= halo)
    far = far | ((links_of >= columns + halo) & (lane < columns - halo))
    far = far | ((links_of >= columns) & ((links_of - columns) % halo >= REACH))
    far = far | ((links_of < halo) & (lane >= 2 * halo))
    far = far | ((links_of >= columns - halo) & (links_of < columns) & (lane < columns - 2 * halo))
    far = jnp.sum(jnp.where(far, 1.0, 0.0), axis=1, keepdims=True)
    far = jnp.sum(far, axis=0, keepdims=True)
    first_half = lax.broadcasted_iota(jnp.int32, (columns, columns), 0) < 4 * halo
    for link, matrix in enumerate(one_hot(target, columns)[: links + 1]):
        at = slice(link * columns, (link + 1) * columns)
        target_ref[at, 0:columns] = jnp.where(first_half, matrix, jnp.zeros_like(matrix))
        target_ref[at, columns:] = jnp.where(first_half, jnp.zeros_like(matrix), matrix)

    half_part = parts_of((half, columns))

    def came_in(first, upper):
        came = []
        for start in range(first, first + rows, 3 * half):
            cut = [slice(start + i * half, start + (i + 1) * half) for i in range(3)]
            came += unpack_slots([from_right[c] for c in cut], [from_left[c] for c in cut], upper)
        return came

    early = came_in(0, False)
    late = came_in(rows, True)
    above = None
    for level in range(levels):
        value = jnp.where(half_part < 2, early[level], mirror_ref[level])
        value = value * plane_ref[1, level : level + 1, :]
        if level > 0:
            value = value - plane_ref[0, level : level + 1, :] * above
        rim_field_ref[level] = value
        above = value
    wide = levels // 4
    span = wide * half
    below = None
    for index in range(levels // wide - 1, -1, -1):
        for level in range((index + 1) * wide - 1, index * wide - 1, -1):
            value = rim_field_ref[level]
            if below is not None:
                value = value - plane_ref[2, level : level + 1, :] * below
            below = value
            at = 2 * span * index + level % wide * half
            for link in range(links + 1):
                term = value * plane_ref[3 + link, level : level + 1, :]
                if link == links:
                    term = jnp.where(half_part < 2, term, late[level])
                top, low = split(term)
                cols = slice(link * columns, (link + 1) * columns)
                spread_ref[at : at + half, cols] = top
                spread_ref[at + span : at + span + half, cols] = low
        both = jnp.dot(spread_ref[2 * span * index : 2 * span * (index + 1), :], target_ref[...], preferred_element_type=F32)
        came_ref[span * index : span * (index + 1), :] = both[:span] + both[span:]

    above = None
    for level in range(levels):
        rows = slice(level * half, (level + 1) * half)
        came = jnp.concatenate([came_ref[rows, :columns], came_ref[rows, columns:]], axis=0)
        value = (moved_ref[level] + came) * pivot_ref[level : level + 1, :]
        if level > 0:
            value = value - carry_ref[level : level + 1, :] * above
        forward_ref[level] = value
        above = value

    products = None
    square = jnp.zeros((vectors, columns), F32)
    below = None
    for index in range(levels // wide - 1, -1, -1):
        for level in range((index + 1) * wide - 1, index * wide - 1, -1):
            value = forward_ref[level]
            if below is not None:
                value = value - ratio_ref[level : level + 1, :] * below
            below = value
            image_ref[level] = value
            square = square + value * value
            stack_terms(value, level, images_ref)
        part = stacked_products(images_ref, stack_ref, wide * index * columns, wide * (index + 1) * columns)
        products = part if products is None else products + part
    cross = join_products(products)
    sums_ref[0:vectors, 0:vectors] = cross
    sums_ref[0:vectors, vectors : 2 * vectors] = gram_ref[...]
    norm = jnp.sum(square, axis=1, keepdims=True)
    shape = (vectors, 2 * vectors)
    eye = lax.broadcasted_iota(jnp.int32, shape, 0) == lax.broadcasted_iota(jnp.int32, shape, 1)
    norm = jnp.sum(jnp.where(eye, norm, 0.0), axis=0, keepdims=True)
    shape = (8, 2 * vectors)
    sums_ref[vectors : vectors + 8, :] = jnp.where(lax.broadcasted_iota(jnp.int32, shape, 0) == 0, norm, far)


def weigh_kernel(cells, sums_ref, more_ref, spans_ref, scale_ref, coupling_ref, direct_ref):
    vectors = coupling_ref.shape[0]
    sums = sums_ref[...] + more_ref[...]
    cross = sums[0:vectors, 0:vectors] / cells
    gram = sums[0:vectors, vectors : 2 * vectors] / cells
    coupling_ref[...] = cross.T
    shape = (vectors, vectors)
    eye = lax.broadcasted_iota(jnp.int32, shape, 0) == lax.broadcasted_iota(jnp.int32, shape, 1)
    square = sums[vectors : vectors + 1, 0:vectors] / cells
    square = jnp.sum(jnp.where(eye, square, 0.0), axis=1, keepdims=True)
    mixed = dot3(cross, gram, (((1,), (0,)), ((), ())))
    spanned = jnp.sum(cross * mixed, axis=1, keepdims=True)
    shared = 2.0 * jnp.sum(cross * cross, axis=1, keepdims=True)
    norm = square - shared + spanned
    small = norm + 1e-6 < 1e-2 * (square + shared + jnp.abs(spanned))
    scale_ref[...] = jnp.broadcast_to(1.0 / jnp.sqrt(jnp.maximum(norm, 0.0) + 1e-6), scale_ref.shape)
    far = jnp.sum(sums[vectors + 1 : vectors + 2, 0:1])
    direct_ref[0] = jnp.where(far + jnp.sum(jnp.where(small, 1.0, 0.0)) > 0.0, 1, 0)
    top, low = split(cross)
    spans_ref[...] = jnp.concatenate([jnp.concatenate([top, top], axis=1), jnp.concatenate([low, low], axis=1)], axis=0)


def last_kernel(spans_ref, scale_ref, image_ref, stack_ref, sums_ref, next_ref, coupling_ref, chunk_ref, sems):
    levels, vectors, columns = image_ref.shape
    chunks = chunk_ref.shape[0]
    step = levels // chunks
    copies = [pltpu.make_async_copy(chunk_ref.at[i], next_ref.at[:, step * i : step * (i + 1), :], sems.at[i]) for i in range(chunks)]
    copies.append(pltpu.make_async_copy(sums_ref, coupling_ref, sems.at[chunks]))
    copies[chunks].start()
    def spanned_by(index):
        cols = slice(step * index * columns, step * (index + 1) * columns)
        both = jnp.dot(spans_ref[...], stack_ref[:, cols], preferred_element_type=F32)
        return both[:vectors] + both[vectors:]

    ready = spanned_by(0)
    for index in range(chunks):
        spanned = ready
        if index + 1 < chunks:
            ready = spanned_by(index + 1)
        for level in range(step):
            at = level * columns
            chunk_ref[index, :, level, :] = (image_ref[step * index + level] - spanned[:, at : at + columns]) * scale_ref[...]
        copies[index].start()
    for copy in copies:
        copy.wait()


VMEM = pl.BlockSpec(memory_space=pltpu.VMEM)
SMEM = pl.BlockSpec(memory_space=pltpu.SMEM)
ANY = pl.BlockSpec(memory_space=pl.ANY)


def call(kernel, outs, out_specs, scratch, specs, *operands):
    return pl.pallas_call(
        kernel,
        out_shape=outs,
        in_specs=specs,
        out_specs=out_specs,
        scratch_shapes=scratch,
        compiler_params=pltpu.CompilerParams(vmem_limit_bytes=40 << 20),
    )(*operands)


def exchange(outer, inner):
    blocks = lax.axis_size(AXES)
    outer = lax.ppermute(outer, AXES, [(i, (i - 1) % blocks if i % 2 == 0 else (i + 1) % blocks) for i in range(blocks)])
    inner = lax.ppermute(inner, AXES, [(i, i ^ 1) for i in range(blocks)])
    return outer, inner


def almost_total(value):
    blocks = lax.axis_size(AXES)
    if blocks & (blocks - 1):
        return lax.psum(value, AXES), jnp.zeros_like(value)
    distance = 2
    while distance < blocks:
        value = value + lax.ppermute(value, AXES, [(i, i ^ distance) for i in range(blocks)])
        distance *= 2
    more = lax.ppermute(value, AXES, [(i, i ^ 1) for i in range(blocks)])
    return value, more


def shards(basis, weights, kappa, thickness, depth, neighbours, rim_lists, counts):
    vectors, levels, columns = basis.shape
    links = weights.shape[0]
    halo = rim_lists.shape[1]
    rows = levels // SPAN * 3 * vectors // 2
    chunks = 4

    def out(*shape, dtype=F32):
        return jax.ShapeDtypeStruct(shape, dtype)

    message = out(2 * rows + levels, LANES)
    whole = out(levels, vectors, columns)
    halved = out(levels, vectors // 2, columns)
    plane = out(levels, columns)
    forward = pltpu.VMEM((levels, vectors, columns), F32)
    half_forward = pltpu.VMEM((levels, vectors // 2, columns), F32)
    chunk = pltpu.VMEM((chunks, vectors, levels // chunks, columns), F32)
    sems = pltpu.SemaphoreType.DMA((chunks,))
    entry = pltpu.VMEM((1, vectors, levels, columns), F32)
    cells = levels * vectors
    table = out(24, columns, dtype=jnp.int32)
    outer, inner, mirror, field, live, self_weight, carry, pivot, ratio, table = call(
        functools.partial(edge_kernel, halo),
        (message, message, halved, whole, out(links, levels, columns), plane, plane, plane, plane, table), [VMEM] * 10,
        [pltpu.VMEM((links * columns, columns), BF16), pltpu.VMEM((links // 2 * columns, columns), BF16),
         pltpu.VMEM((cells, links * columns), BF16), pltpu.VMEM((cells, links // 2 * columns), BF16),
         half_forward, pltpu.VMEM((links + 4 + links // 2, levels, columns), F32), entry,
         pltpu.VMEM((links, levels, columns), F32), pltpu.VMEM((levels, columns), F32), pltpu.VMEM((levels, columns), F32),
         pltpu.VMEM((1, columns), jnp.int32), pltpu.VMEM((links, columns), jnp.int32), sems, pltpu.SemaphoreType.DMA((5,))],
        [SMEM] * 2 + [ANY] * 6,
        counts, rim_lists, basis, weights, kappa, thickness, depth.reshape(1, columns), neighbours)
    outer, inner = exchange(outer, inner)
    moved, stack, gram = call(
        block_kernel,
        (whole, out(2 * vectors, levels * columns, dtype=BF16), out(vectors, vectors)), [VMEM] * 3,
        [pltpu.VMEM((levels, 2 * columns, columns), BF16), forward],
        [VMEM] * 7, table, field, live, self_weight, carry, pivot, ratio)
    image, sums = call(
        functools.partial(second_kernel, halo), (whole, out(vectors + 8, 2 * vectors)), [VMEM] * 2,
        [pltpu.VMEM((links + 4, levels, columns), F32), pltpu.VMEM(((links + 1) * columns, 2 * columns), BF16), half_forward,
         pltpu.VMEM((cells, (links + 1) * columns), BF16), pltpu.VMEM((cells // 2, 2 * columns), F32),
         forward, pltpu.VMEM((2 * vectors, levels * columns), BF16)],
        [VMEM] * 12,
        outer, inner, mirror, stack, moved, live, self_weight, carry, pivot, ratio, table, gram)
    sums, more = almost_total(sums)
    cells = float(levels * columns * lax.axis_size(AXES))
    spans, scale, coupling, direct = call(
        functools.partial(weigh_kernel, cells),
        (out(2 * vectors, 2 * vectors, dtype=BF16), out(vectors, columns), out(vectors, vectors), out(1, dtype=jnp.int32)),
        [VMEM] * 3 + [SMEM], [], [VMEM] * 2, sums, more)

    def from_sums():
        return call(last_kernel, (out(vectors, levels, columns), out(vectors, vectors)), [ANY] * 2,
                    [chunk, pltpu.SemaphoreType.DMA((chunks + 1,))], [VMEM] * 5, spans, scale, image, stack, coupling)

    def from_scratch():
        return direct_form(basis, weights, kappa, thickness, depth, neighbours, rim_lists, counts)

    return tuple(lax.cond(direct[0] > 0, from_scratch, lambda: tuple(from_sums())))


ITERS = 2


def from_behind(block, axis, distance):
    devices = range(lax.axis_size(axis))
    route = [((i - distance) % len(devices), i) for i in devices]
    return lax.ppermute(block, axis, route)


def column_factors(kappa, thickness, keep):
    levels = kappa.shape[0]
    below = jnp.concatenate([keep[1:], jnp.zeros_like(keep[:1])], axis=0)
    interface = kappa * keep * below
    lower, inv_pivot, ratio = ([], [], [])
    for level in range(levels):
        upper_term = interface[level]
        diag_term = 1.0 + upper_term / thickness[level]
        if level > 0:
            diag_term = diag_term + interface[level - 1] / thickness[level]
            low = -interface[level - 1] / thickness[level - 1]
        else:
            low = jnp.zeros_like(upper_term)
        if level < levels - 1:
            upp = -upper_term / thickness[level + 1]
        else:
            upp = jnp.zeros_like(upper_term)
        pivot = diag_term - low * ratio[level - 1] if level > 0 else diag_term
        inverse = 1.0 / pivot
        lower.append(low)
        inv_pivot.append(inverse)
        ratio.append(upp * inverse)
    return (lower, inv_pivot, ratio)


def column_solve(rhs, lower, inv_pivot, ratio):
    levels = rhs.shape[1]
    forward = []
    for level in range(levels):
        if level == 0:
            forward.append(rhs[:, 0] * inv_pivot[0])
        else:
            forward.append((rhs[:, level] - lower[level] * forward[level - 1]) * inv_pivot[level])
    result = [None] * levels
    result[levels - 1] = forward[levels - 1]
    for level in range(levels - 2, -1, -1):
        result[level] = forward[level] - ratio[level] * result[level + 1]
    return jnp.stack(result, axis=1)


def transport_back(field, weights, keep, self_weight, neighbours, rim_lists):
    columns = field.shape[2]
    halo_width = rim_lists.shape[1]
    masked = keep * field
    extended = jnp.zeros((field.shape[0], field.shape[1], columns + 2 * halo_width), jnp.float32)
    for link in range(weights.shape[0]):
        extended = extended.at[:, :, neighbours[link]].add(weights[link] * masked)
    from_right = from_behind(extended[:, :, columns : columns + halo_width], ("region", "sub"), -1)
    from_left = from_behind(extended[:, :, columns + halo_width :], ("region", "sub"), 1)
    result = self_weight * masked + extended[:, :, :columns]
    result = result.at[:, :, rim_lists[0]].add(from_right).at[:, :, rim_lists[1]].add(from_left)
    return keep * result


def direct_form(basis, weights, kappa, thickness, depth, neighbours, rim_lists, counts):
    vectors, levels, columns = basis.shape
    halo_width = rim_lists.shape[1]
    own_index = jnp.arange(columns, dtype=jnp.int32)
    live = (own_index < counts[0]) | (own_index >= columns - 2 * halo_width)
    wet = jnp.arange(levels, dtype=jnp.int32)[:, None] < depth[None, :]
    keep = (live[None, :] & wet).astype(jnp.float32)
    self_weight = 1.0 - jnp.sum(weights, axis=0)
    lower, inv_pivot, ratio = column_factors(kappa, thickness, keep)
    field = basis
    for step in range(ITERS):
        moved = transport_back(field, weights, keep, self_weight, neighbours, rim_lists)
        field = column_solve(keep * moved, lower, inv_pivot, ratio)
    cells = float(levels * columns * lax.axis_size(("region", "sub")))
    high = lax.Precision.HIGHEST
    local_cross = jnp.einsum("ilc,jlc->ij", basis, field, precision=high)
    coupling = lax.psum(local_cross, ("region", "sub")) / cells
    residual = field - jnp.einsum("ilc,ij->jlc", basis, coupling, precision=high)
    local_norms = jnp.einsum("jlc,jlc->j", residual, residual, precision=high)
    norms = lax.psum(local_norms, ("region", "sub")) / cells
    next_basis = residual / jnp.sqrt(norms + 1e-06)[:, None, None]
    return (next_basis, coupling)


def solution(mesh):
    placed = (
        P("groups", None, AXES),
        P(None, None, AXES),
        P(None, AXES),
        P(None, AXES),
        P(AXES),
        P(None, AXES),
        P(None, AXES),
        P(AXES),
    )
    return jax.shard_map(
        shards,
        mesh=mesh,
        in_specs=placed,
        out_specs=(P("groups", None, AXES), P("groups", None)),
        check_vma=False,
    )
```
